32 devices in a mesh: grp: 2 (over x), hist: 16 (over z, y, core).
Axes of the slice: x: 2, y: 2, z: 4, core: 2. Of those that a mesh axis runs over, the one named last changes fastest.
Arguments:
- item_ids: int32 [512], P(('grp', 'hist')), parts along dimension 0, may hold values from 0 to 16383
- item_table: bfloat16 [16384, 1024], P('hist'), may hold values from -6 to 6
- key_cache: bfloat16 [32768, 1024], P(('grp', 'hist')), parts along dimension 0, may hold values from -6 to 6
- value_cache: bfloat16 [32768, 1024], P(('grp', 'hist')), parts along dimension 0, may hold values from -6 to 6
- time_buckets: int32 [32768], P(('grp', 'hist')), parts along dimension 0, may hold values from 0 to 127
- window_start: int32 [2], P('grp'), parts along dimension 0, may hold values from 0 to 16384
- norm_gain: float32 [1024], replicated, may hold values from 0.25 to 1.75
- proj_in: bfloat16 [1024, 2048], replicated, may hold values from -0.1875 to 0.1875
- time_bias: float32 [16, 128], replicated, may hold values from -3 to 3
- pos_bias: float32 [16, 18], replicated, may hold values from -1 to 1
- out_gain: float32 [1024], replicated, may hold values from 0.25 to 1.75
- proj_out: bfloat16 [1024, 1024], replicated, may hold values from -0.1875 to 0.1875
Outputs:
- scored: bfloat16 [512, 1024], P(('grp', 'hist')), parts along dimension 0
The draws below stay inside these ranges and needn't reach their ends.
There are 2 independent parts, one for each index of `grp`. The reference program is written for one: setup_inputs(seed, part) draws one part's arguments, and reference() takes and returns one part's arrays. A program takes and returns all parts, laid end to end along the dimension named above; an argument that names none is the same for every part. Nothing has to cross between parts.
All inputs are finite; a program needn't handle non-finite values.
Results may differ from the reference program's by a relative error of at most 0.0075.
Values may be sent and summed in bfloat16 or wider, within the bound.
No kernel may reach another device: no remote copies, remote signals or barrier semaphores. Data moves between devices by JAX's collectives and lax.ppermute only.
A program may use at most 128 MiB of HBM per device.

```python
import jax
import jax.numpy as jnp
from jax import lax

D = 1024
HEADS = 16
HEAD_DIM = 64
NTB = 128
NPOS = 18
EV_DEV = 1024
CANDS = 256
WINDOW = 16384
HISTORY = 32768
ITEMS = 16384
N_HIST = 16


def place_ends(array, rng, smallest, high):
    place = [jax.random.randint(jax.random.fold_in(rng, axis), (), 0, length) for axis, length in enumerate(array.shape)]
    widest = array.shape.index(max(array.shape))
    neighbour = place[:widest] + [(place[widest] + 1) % array.shape[widest]] + place[widest + 1:]
    return array.at[tuple(place)].set(smallest).at[tuple(neighbour)].set(high)


def block_levels(key, dims, split, smallest, top_value):
    gain = 1.0
    for position, parts in split:
        heights = jax.random.uniform(jax.random.fold_in(jax.random.fold_in(key, 6), position), (parts,), jnp.float32, smallest / len(split), top_value / len(split))
        gain = gain * jnp.repeat(jnp.exp(heights), dims[position] // parts).reshape((-1,) + (1,) * (len(dims) - 1 - position))
    return gain


def noise(own_key, shape, scale, most, cuts=(), held_as=jnp.bfloat16):
    factor_of = block_levels(own_key, shape, cuts, -0.22, 0.18) if cuts else 1.0
    drawn = jax.random.normal(own_key, shape, jnp.float32) * scale * factor_of
    return jnp.minimum(jnp.maximum(drawn, -most), most).astype(held_as)


def setup_inputs(seed: int = 0, part: int = 0) -> dict:
    key_list = jax.random.split(jax.random.key(seed), 13)
    part_keys = jax.random.split(jax.random.fold_in(key_list[12], part), 13)
    return {
        "item_ids": place_ends(jax.random.randint(part_keys[0], (CANDS,), 0, ITEMS), jax.random.fold_in(part_keys[0], 1), 0, ITEMS - 1).astype(jnp.int32),
        "item_table": noise(key_list[1], (ITEMS, D), 1.0, 6.0, ((0, 16),)),
        "key_cache": noise(part_keys[2], (WINDOW, D), 1.0, 6.0, ((0, 16),)),
        "value_cache": noise(part_keys[3], (WINDOW, D), 1.0, 6.0, ((0, 16),)),
        "time_buckets": place_ends(jax.random.randint(part_keys[4], (WINDOW,), 0, NTB), jax.random.fold_in(part_keys[4], 1), 0, NTB - 1).astype(jnp.int32),
        "window_start": jax.random.randint(part_keys[5], (1,), 0, WINDOW + 1).astype(jnp.int32),
        "norm_gain": jnp.clip(1.0 + 0.15 * jax.random.normal(key_list[6], (D,), jnp.float32), 0.25, 1.75),
        "proj_in": noise(key_list[7], (D, 2 * D), D ** -0.5, 0.1875),
        "time_bias": noise(key_list[8], (HEADS, NTB), 0.5, 3.0, (), jnp.float32),
        "pos_bias": jnp.clip(jax.random.uniform(key_list[9], (HEADS, NPOS), jnp.float32, -1.0, 1.0), -1.0, 1.0),
        "out_gain": jnp.clip(1.0 + 0.15 * jax.random.normal(key_list[10], (D,), jnp.float32), 0.25, 1.75),
        "proj_out": noise(key_list[11], (D, D), D ** -0.5, 0.1875),
    }


def reference(item_ids, item_table, key_cache, value_cache, time_buckets, window_start, norm_gain, proj_in, time_bias, pos_bias, out_gain, proj_out):
    embedded = item_table[item_ids]
    xfloat = embedded.astype(jnp.float32)
    meansq = lax.optimization_barrier(jnp.mean(xfloat * xfloat, axis=-1, keepdims=True))
    normed = (xfloat * lax.rsqrt(meansq + 1e-06) * norm_gain).astype(jnp.bfloat16)
    projected = jnp.dot(normed, proj_in, preferred_element_type=jnp.float32)
    queries = jax.nn.silu(projected[:, :D]).astype(jnp.bfloat16)
    gates = jax.nn.silu(projected[:, D:]).astype(jnp.bfloat16)
    positions = jnp.arange(WINDOW, dtype=jnp.int32)
    distance = HISTORY - window_start[0] - positions
    thresholds = jnp.left_shift(jnp.ones((NPOS - 1,), jnp.int32), jnp.arange(1, NPOS, dtype=jnp.int32))
    buckets = lax.optimization_barrier(jnp.sum((distance[:, None] >= thresholds[None, :]).astype(jnp.int32), axis=1)).astype(jnp.int32)
    event_bias = time_bias[:, time_buckets] + pos_bias[:, buckets]
    scale = HEAD_DIM ** (-0.5)
    query_heads = queries.reshape(CANDS, HEADS, HEAD_DIM).astype(jnp.float32)
    key_blocks = key_cache.reshape(N_HIST, EV_DEV, HEADS, HEAD_DIM)
    value_blocks = value_cache.reshape(N_HIST, EV_DEV, HEADS, HEAD_DIM)
    bias_blocks = event_bias.reshape(HEADS, N_HIST, EV_DEV).transpose(1, 0, 2)

    def one_block(total, operands):
        keys, values, biases = operands
        scores = jnp.einsum('chd,jhd->chj', query_heads, keys.astype(jnp.float32)) * scale + biases[None]
        weights = jax.nn.silu(scores).astype(jnp.bfloat16)
        return (total + jnp.einsum('chj,jhd->chd', weights.astype(jnp.float32), values.astype(jnp.float32)), None)
    start = jnp.zeros((CANDS, HEADS, HEAD_DIM), jnp.float32)
    attended, _ = lax.scan(one_block, start, (key_blocks, value_blocks, bias_blocks))
    attended = attended.reshape(CANDS, D)
    centred = attended - lax.optimization_barrier(jnp.mean(attended, axis=-1, keepdims=True))
    variance = lax.optimization_barrier(jnp.mean(centred * centred, axis=-1, keepdims=True))
    gated = (centred * lax.rsqrt(variance + 1e-05) * out_gain * gates.astype(jnp.float32)).astype(jnp.bfloat16)
    return (embedded.astype(jnp.float32) + jnp.dot(gated, proj_out, preferred_element_type=jnp.float32)).astype(jnp.bfloat16)
```

```python
import functools

import jax
import jax.numpy as jnp
from jax import lax
from jax.experimental import pallas as pl
from jax.experimental.pallas import tpu as pltpu
from jax.sharding import PartitionSpec as P

BF16 = jnp.bfloat16
F32 = jnp.float32
LANES = 128
ROWS_AT_ONCE = 256
EVENTS_AT_ONCE = 512
NT = (((1,), (1,)), ((), ()))
VMEM = pl.BlockSpec(memory_space=pltpu.VMEM)
SMEM = pl.BlockSpec(memory_space=pltpu.SMEM)


def params(mib):
    return pltpu.CompilerParams(vmem_limit_bytes=mib << 20)


def stage_masks(size, joined_tail):
    bits = [1 << k for k in range(size.bit_length() - 1)][::-1]
    near = bits[-2:]
    far = bits[:-2]
    stages = [sorted(far[k : k + 2]) for k in range(0, len(far), 2)]
    return stages + ([near] if joined_tail else [[b] for b in near])


def combos(bits):
    out = [0]
    for b in bits:
        out = out + [m | b for m in out]
    return out


def swap(x, mask, axis, size):
    return lax.ppermute(x, axis, [(i, i ^ mask) for i in range(size)])


def gather_relative(x, dim, axis, size, joined_tail):
    for bits in stage_masks(size, joined_tail):
        x = jnp.concatenate([x] + [swap(x, m, axis, size) for m in combos(bits)[1:]], axis=dim)
    return x


def position_bits(size):
    return [b for stage in stage_masks(size, False) for b in stage]


def rounds_of(ranks, slots):
    return jnp.max(ranks) // slots + 1


def candidates_info(ids_ref, me, size, table_rows):
    count = ids_ref.shape[1]
    each = count // size
    ids = ids_ref[...]
    owner = ids // table_rows
    place = lax.broadcasted_iota(jnp.int32, (1, count), 1)
    block = place // each
    mask = jnp.zeros_like(place)
    for k, b in enumerate(position_bits(size)):
        mask = mask + ((block >> k) & 1) * b
    key = owner * count + (mask ^ me) * each + place % each
    return owner, key, ids - owner * table_rows


def to_column(row):
    count = row.shape[1]
    r = lax.broadcasted_iota(jnp.int32, (count, count), 0)
    c = lax.broadcasted_iota(jnp.int32, (count, count), 1)
    return jnp.sum(jnp.where(r == c, row, 0), axis=1, keepdims=True)


def lookup_kernel(place_ref, ids_ref, table_ref, out_ref, *, size):
    me, turn = place_ref[0], place_ref[1]
    slots = out_ref.shape[0]
    rows = table_ref.shape[0]
    count = ids_ref.shape[1]
    owner, key, offset = candidates_info(ids_ref, me, size, rows)
    key_col = to_column(key)
    before = (key_col < key) & (key_col >= owner * count)
    rank = jnp.sum(before.astype(jnp.int32), axis=0, keepdims=True)
    slot = lax.broadcasted_iota(jnp.int32, (slots, count), 0) + turn * slots
    hit = (owner == me) & (rank == slot)
    want = jnp.sum(jnp.where(hit, offset + 1, 0), axis=1, keepdims=True) - 1
    pick = (want == lax.broadcasted_iota(jnp.int32, (slots, rows), 1)).astype(F32).astype(BF16)
    out_ref[...] = jnp.dot(pick, table_ref[...], preferred_element_type=F32).astype(BF16)


def lookup(place, ids, table, slots, size):
    return pl.pallas_call(
        functools.partial(lookup_kernel, size=size),
        out_shape=jax.ShapeDtypeStruct((slots, table.shape[1]), BF16),
        in_specs=[SMEM, VMEM, VMEM],
        out_specs=VMEM,
        compiler_params=params(24),
        name="lookup",
    )(place, ids, table)


def plan_kernel(place_ref, ids_ref, pick_ref, rounds_ref, *, size, slots, table_rows):
    me, turn = place_ref[0], place_ref[1]
    count = ids_ref.shape[1]
    owner, key, _ = candidates_info(ids_ref, me, size, table_rows)
    key_col = to_column(key)
    owner_col = key_col // count
    before = (key < key_col) & (key >= owner_col * count)
    rank = jnp.sum(before.astype(jnp.int32), axis=1, keepdims=True)
    rounds_ref[0] = rounds_of(rank, slots)
    away = owner_col ^ me
    block = jnp.zeros_like(away)
    for k, b in enumerate(position_bits(size)):
        block = block + jnp.where((away & b) != 0, 1 << k, 0)
    mine = rank - turn * slots
    slot = jnp.where((mine >= 0) & (mine < slots), block * slots + mine, -1)
    pick = slot == lax.broadcasted_iota(jnp.int32, pick_ref.shape, 1)
    pick_ref[...] = pick.astype(F32).astype(BF16)


def plan(place, ids, slots, table_rows, size):
    count = ids.shape[1]
    return pl.pallas_call(
        functools.partial(plan_kernel, size=size, slots=slots, table_rows=table_rows),
        out_shape=(
            jax.ShapeDtypeStruct((count, size * slots), BF16),
            jax.ShapeDtypeStruct((1,), jnp.int32),
        ),
        in_specs=[SMEM, VMEM],
        out_specs=(VMEM, SMEM),
        compiler_params=params(40),
        cost_estimate=pl.CostEstimate(flops=1 << 22, transcendentals=0, bytes_accessed=1 << 20),
        name="plan",
    )(place, ids)


def select_kernel(pick_ref, rows_ref, out_ref):
    out_ref[...] = jnp.dot(pick_ref[...], rows_ref[...], preferred_element_type=F32).astype(BF16)


def select(pick, rows):
    return pl.pallas_call(
        select_kernel,
        out_shape=jax.ShapeDtypeStruct((pick.shape[0], rows.shape[1]), BF16),
        in_specs=[VMEM, VMEM],
        out_specs=VMEM,
        compiler_params=params(32),
        name="select",
    )(pick, rows)


def three_parts(x):
    high = x.astype(BF16)
    rest = x - high.astype(F32)
    middle = rest.astype(BF16)
    return [high, middle, (rest - middle.astype(F32)).astype(BF16)]


def bias_kernel(place_ref, start_ref, times_ref, time_bias_ref, pos_bias_ref, out_ref, *, npos, history):
    events = times_ref.shape[1]
    first = history - start_ref[0] - place_ref[0] * events
    distance = first - lax.broadcasted_iota(jnp.int32, (1, events), 1)
    bucket = jnp.zeros((1, events), jnp.int32)
    for k in range(1, npos):
        bucket = bucket + (distance >= (1 << k)).astype(jnp.int32)
    columns = []
    for table_ref, index in ((time_bias_ref, times_ref[...]), (pos_bias_ref, bucket)):
        table = jnp.concatenate(three_parts(table_ref[...] * 0.5), axis=0)
        kinds = table.shape[1]
        hot = lax.broadcasted_iota(jnp.int32, (kinds, events), 0) == index
        columns.append(
            jnp.dot(table, hot.astype(F32).astype(BF16), preferred_element_type=F32)
        )
    used = sum(c.shape[0] for c in columns)
    columns.append(jnp.zeros((LANES - used, events), F32))
    out_ref[...] = jnp.concatenate(columns, axis=0).T.astype(BF16)


def bias_columns(place, start, times, time_bias, pos_bias, npos, history):
    return pl.pallas_call(
        functools.partial(bias_kernel, npos=npos, history=history),
        out_shape=jax.ShapeDtypeStruct((times.shape[1], LANES), BF16),
        in_specs=[SMEM, SMEM, VMEM, VMEM, VMEM],
        out_specs=VMEM,
        compiler_params=params(16),
        cost_estimate=pl.CostEstimate(flops=1 << 25, transcendentals=0, bytes_accessed=1 << 20),
        name="bias",
    )(place, start, times, time_bias, pos_bias)


def silu(x):
    return x / (1.0 + jnp.exp(-x))


def normalise(embedded, gain):
    x = embedded.astype(F32)
    meansq = jnp.mean(x * x, axis=-1, keepdims=True)
    return (x * lax.rsqrt(meansq + 1e-06) * gain).astype(BF16)


def attend_kernel(
    emb_ref, gain_ref, proj_ref, key_ref, value_ref, bias_ref, keep_ref, send_ref, query_ref, *, heads
):
    count, width = emb_ref.shape
    head_dim = width // heads
    events = key_ref.shape[0]
    half = count // 2
    rows = min(ROWS_AT_ONCE, count)
    per = LANES // head_dim
    step = min(EVENTS_AT_ONCE, events)
    for first in range(0, count, rows):
        normed = normalise(emb_ref[first : first + rows, :], gain_ref[...])
        projected = jnp.dot(normed, proj_ref[:, :width], preferred_element_type=F32)
        query = silu(projected).astype(BF16)
        query_ref[...] = query * jnp.asarray(0.5 * head_dim**-0.5, BF16)
        lane = lax.broadcasted_iota(jnp.int32, (rows, LANES), 1)
        for group in range(heads // per):
            at = slice(group * LANES, (group + 1) * LANES)
            part = query_ref[:, at]
            zero, one = jnp.zeros_like(part), jnp.ones_like(part)
            stacked = []
            for k in range(per):
                own = jnp.where(lane // head_dim == k, part, zero)
                chosen = jnp.where(lane % heads == group * per + k, one, zero)
                stacked.append(jnp.concatenate([own, chosen], axis=1))
            left = jnp.concatenate(stacked, axis=0)
            total = jnp.zeros((per * rows, LANES), F32)
            for j in range(0, events, step):
                right = jnp.concatenate([key_ref[j : j + step, at], bias_ref[j : j + step, :]], axis=1)
                t = lax.dot_general(left, right, NT, preferred_element_type=F32)
                weights = (t + t * jnp.tanh(t)).astype(BF16)
                total = total + jnp.dot(weights, value_ref[j : j + step, at], preferred_element_type=F32)
            out = total[:rows]
            for k in range(1, per):
                out = jnp.where(lane // head_dim == k, total[k * rows : (k + 1) * rows], out)
            if first + rows <= half:
                keep_ref[first : first + rows, at] = out
            elif first >= half:
                send_ref[first - half : first - half + rows, at] = out.astype(BF16)
            else:
                keep_ref[first:half, at] = out[: half - first]
                send_ref[: first + rows - half, at] = out[half - first :].astype(BF16)


def attend(embedded, gain, proj_in, keys, values, bias, heads):
    count, width = embedded.shape
    return pl.pallas_call(
        functools.partial(attend_kernel, heads=heads),
        out_shape=(
            jax.ShapeDtypeStruct((count // 2, width), F32),
            jax.ShapeDtypeStruct((count // 2, width), BF16),
        ),
        in_specs=[VMEM] * 6,
        out_specs=(VMEM, VMEM),
        scratch_shapes=[pltpu.VMEM((min(ROWS_AT_ONCE, count), width), BF16)],
        compiler_params=params(40),
        cost_estimate=pl.CostEstimate(
            flops=8 * count * width * keys.shape[0],
            transcendentals=count * heads * keys.shape[0],
            bytes_accessed=4 * keys.size,
        ),
        name="attend",
    )(embedded, gain, proj_in, keys, values, bias)


def gates_kernel(emb_ref, gain_ref, proj_ref, out_ref):
    width = emb_ref.shape[1]
    normed = normalise(emb_ref[...], gain_ref[...])
    projected = jnp.dot(normed, proj_ref[:, width:], preferred_element_type=F32)
    out_ref[...] = silu(projected).astype(BF16)


def gates_of(embedded, gain, proj_in):
    return pl.pallas_call(
        gates_kernel,
        out_shape=jax.ShapeDtypeStruct(embedded.shape, BF16),
        in_specs=[VMEM] * 3,
        out_specs=VMEM,
        compiler_params=params(16),
        cost_estimate=pl.CostEstimate(flops=1 << 26, transcendentals=1 << 14, bytes_accessed=1 << 22),
        name="gates",
    )(embedded, gain, proj_in)


def finish_kernel(own_ref, *refs):
    *parts, emb_ref, gates_ref, gain_ref, proj_ref, out_ref = refs
    attended = own_ref[...]
    for p in parts:
        attended = attended + p[...].astype(F32)
    centred = attended - jnp.mean(attended, axis=-1, keepdims=True)
    variance = jnp.mean(centred * centred, axis=-1, keepdims=True)
    gated = centred * lax.rsqrt(variance + 1e-05) * gain_ref[...] * gates_ref[...].astype(F32)
    product = jnp.dot(gated.astype(BF16), proj_ref[...], preferred_element_type=F32)
    out_ref[...] = (emb_ref[...].astype(F32) + product).astype(BF16)


def finish(own, parts, embedded, gates, gain, proj_out):
    return pl.pallas_call(
        finish_kernel,
        out_shape=jax.ShapeDtypeStruct(embedded.shape, BF16),
        in_specs=[VMEM] * (len(parts) + 5),
        out_specs=VMEM,
        compiler_params=params(16),
        name="finish",
    )(own, *parts, embedded, gates, gain, proj_out)


def on_device(
    item_ids,
    item_table,
    key_cache,
    value_cache,
    time_buckets,
    window_start,
    norm_gain,
    proj_in,
    time_bias,
    pos_bias,
    out_gain,
    proj_out,
):
    axis = "hist"
    size = lax.axis_size(axis)
    me = lax.axis_index(axis).astype(jnp.int32)
    each = item_ids.shape[0]
    slots = 2 * each
    heads = time_bias.shape[0]
    npos = pos_bias.shape[1]
    events = key_cache.shape[0]
    table_rows = item_table.shape[0]
    gain = norm_gain[None, :]

    def place(turn):
        return jnp.stack([me, jnp.asarray(turn, jnp.int32)])

    here = place(0)
    bias = bias_columns(
        here,
        window_start,
        time_buckets[None, :],
        time_bias,
        jnp.pad(pos_bias, ((0, 0), (0, -npos % 32))),
        npos,
        2 * events * size,
    )
    ids = gather_relative(item_ids[None, :], 1, axis, size, True)

    def fetch(turn):
        return gather_relative(
            lookup(place(turn), ids, item_table, slots, size), 0, axis, size, False
        )

    rows = fetch(0)
    pick, rounds = plan(here, ids, slots, table_rows, size)
    embedded = select(pick, rows)

    def more(state):
        turn, so_far = state
        picked, _ = plan(place(turn), ids, slots, table_rows, size)
        return turn + 1, so_far + select(picked, fetch(turn))

    _, embedded = lax.while_loop(lambda s: s[0] < rounds[0], more, (jnp.int32(1), embedded))

    keep, send = attend(embedded, gain, proj_in, key_cache, value_cache, bias, heads)
    own = embedded[:each]
    gates = gates_of(own, gain, proj_in)

    stages = stage_masks(size, False)[::-1]
    total = keep + swap(send, stages[0][0], axis, size).astype(F32)
    for bits in stages[1:]:
        masks = combos(bits)
        block = total.shape[0] // len(masks)
        parts = [
            swap(total[k * block : (k + 1) * block].astype(BF16), m, axis, size)
            for k, m in enumerate(masks)
            if k
        ]
        if bits is stages[-1]:
            break
        total = sum([p.astype(F32) for p in parts], total[:block])
    return finish(total[:block], parts, own, gates, out_gain[None, :], proj_out)


def solution(mesh):
    placed = (
        P(("grp", "hist")),
        P("hist", None),
        P(("grp", "hist"), None),
        P(("grp", "hist"), None),
        P(("grp", "hist")),
        P("grp"),
        P(),
        P(),
        P(),
        P(),
        P(),
        P(),
    )
    return jax.shard_map(
        on_device, mesh=mesh, in_specs=placed, out_specs=P(("grp", "hist"), None), check_vma=False
    )
```

```python
import functools

import jax
import jax.numpy as jnp
from jax import lax
from jax.experimental import pallas as pl
from jax.experimental.pallas import tpu as pltpu
from jax.sharding import PartitionSpec as P


BF16 = jnp.bfloat16
F32 = jnp.float32
LANES = 128
ROWS_AT_ONCE = 256
EVENTS_AT_ONCE = 512
NT = (((1,), (1,)), ((), ()))
VMEM = pl.BlockSpec(memory_space=pltpu.VMEM)
SMEM = pl.BlockSpec(memory_space=pltpu.SMEM)
HBM = pl.BlockSpec(memory_space=pltpu.HBM)


def params(mib):
    return pltpu.CompilerParams(vmem_limit_bytes=mib << 20)


def stage_masks(size, joined_tail):
    bits = [1 << k for k in range(size.bit_length() - 1)][::-1]
    near = bits[-2:]
    far = bits[:-2]
    stages = [sorted(far[k : k + 2]) for k in range(0, len(far), 2)]
    return stages + ([near] if joined_tail else [[b] for b in near])


def combos(bits):
    out = [0]
    for b in bits:
        out = out + [m | b for m in out]
    return out


def swap(x, mask, axis, size):
    return lax.ppermute(x, axis, [(i, i ^ mask) for i in range(size)])


def gather_relative(x, dim, axis, size, joined_tail):
    stages = stage_masks(size, joined_tail)
    for bits in stages:
        pieces = [x] + [swap(x, m, axis, size) for m in combos(bits)[1:]]
        if bits is not stages[-1]:
            x = jnp.concatenate(pieces, axis=dim)
    return pieces


def position_bits(size):
    return [b for stage in stage_masks(size, False) for b in stage]


def rounds_of(ranks, slots):
    return jnp.max(ranks) // slots + 1


def candidates_info(ids_refs, me, size, table_rows):
    ids = jnp.concatenate([r[...] for r in ids_refs], axis=1)
    count = ids.shape[1]
    each = count // size
    owner = ids // table_rows
    place = lax.broadcasted_iota(jnp.int32, (1, count), 1)
    block = place // each
    mask = jnp.zeros_like(place)
    for k, b in enumerate(position_bits(size)):
        mask = mask + ((block >> k) & 1) * b
    key = owner * count + (mask ^ me) * each + place % each
    return owner, key, ids - owner * table_rows


def to_column(row):
    count = row.shape[1]
    r = lax.broadcasted_iota(jnp.int32, (count, count), 0)
    c = lax.broadcasted_iota(jnp.int32, (count, count), 1)
    return jnp.sum(jnp.where(r == c, row, 0), axis=1, keepdims=True)


def lookup_kernel(place_ref, *refs, size):
    *ids_refs, table_hbm, out_ref, table_ref, sem = refs
    copy = pltpu.make_async_copy(table_hbm, table_ref, sem)
    copy.start()
    me, turn = place_ref[0], place_ref[1]
    slots = out_ref.shape[0]
    rows = table_ref.shape[0]
    owner, key, offset = candidates_info(ids_refs, me, size, rows)
    count = owner.shape[1]
    key_col = to_column(key)
    before = (key_col < key) & (key_col >= owner * count)
    rank = jnp.sum(before.astype(jnp.int32), axis=0, keepdims=True)
    slot = lax.broadcasted_iota(jnp.int32, (slots, count), 0) + turn * slots
    hit = (owner == me) & (rank == slot)
    want = jnp.sum(jnp.where(hit, offset + 1, 0), axis=1, keepdims=True) - 1
    pick = (want == lax.broadcasted_iota(jnp.int32, (slots, rows), 1)).astype(F32).astype(BF16)
    copy.wait()
    out_ref[...] = jnp.dot(pick, table_ref[...], preferred_element_type=F32).astype(BF16)


def lookup(place, ids, table, slots, size):
    return pl.pallas_call(
        functools.partial(lookup_kernel, size=size),
        out_shape=jax.ShapeDtypeStruct((slots, table.shape[1]), BF16),
        in_specs=[SMEM] + [VMEM] * len(ids) + [HBM],
        out_specs=VMEM,
        scratch_shapes=[pltpu.VMEM(table.shape, BF16), pltpu.SemaphoreType.DMA],
        compiler_params=params(24),
        name="lookup",
    )(place, *ids, table)


def plan_kernel(place_ref, *refs, size, slots, table_rows):
    *ids_refs, pick_ref, rounds_ref = refs
    me, turn = place_ref[0], place_ref[1]
    owner, key, _ = candidates_info(ids_refs, me, size, table_rows)
    count = owner.shape[1]
    key_col = to_column(key)
    owner_col = key_col // count
    before = (key < key_col) & (key >= owner_col * count)
    rank = jnp.sum(before.astype(jnp.int32), axis=1, keepdims=True)
    rounds_ref[0] = rounds_of(rank, slots)
    away = owner_col ^ me
    block = jnp.zeros_like(away)
    for k, b in enumerate(position_bits(size)):
        block = block + jnp.where((away & b) != 0, 1 << k, 0)
    mine = rank - turn * slots
    slot = jnp.where((mine >= 0) & (mine < slots), block * slots + mine, -1)
    pick = slot == lax.broadcasted_iota(jnp.int32, pick_ref.shape, 1)
    pick_ref[...] = pick.astype(F32).astype(BF16)


def plan(place, ids, slots, table_rows, size):
    count = sum(i.shape[1] for i in ids)
    return pl.pallas_call(
        functools.partial(plan_kernel, size=size, slots=slots, table_rows=table_rows),
        out_shape=(
            jax.ShapeDtypeStruct((count, size * slots), BF16),
            jax.ShapeDtypeStruct((1,), jnp.int32),
        ),
        in_specs=[SMEM] + [VMEM] * len(ids),
        out_specs=(VMEM, SMEM),
        compiler_params=params(40),
        cost_estimate=pl.CostEstimate(flops=1 << 22, transcendentals=0, bytes_accessed=1 << 20),
        name="plan",
    )(place, *ids)


def select_kernel(pick_ref, rows_ref, out_ref):
    out_ref[...] = jnp.dot(pick_ref[...], rows_ref[...], preferred_element_type=F32).astype(BF16)


def select(pick, pieces):
    rows = jnp.concatenate(pieces, axis=0)
    return pl.pallas_call(
        select_kernel,
        out_shape=jax.ShapeDtypeStruct((pick.shape[0], rows.shape[1]), BF16),
        in_specs=[VMEM, VMEM],
        out_specs=VMEM,
        compiler_params=params(32),
        name="select",
    )(pick, rows)


def three_parts(x):
    high = x.astype(BF16)
    rest = x - high.astype(F32)
    middle = rest.astype(BF16)
    return [high, middle, (rest - middle.astype(F32)).astype(BF16)]


def bias_kernel(place_ref, start_ref, times_ref, time_bias_ref, pos_bias_ref, out_ref, *, npos, history):
    events = times_ref.shape[1]
    first = history - start_ref[0] - place_ref[0] * events
    distance = first - lax.broadcasted_iota(jnp.int32, (1, events), 1)
    bucket = jnp.zeros((1, events), jnp.int32)
    for k in range(1, npos):
        bucket = bucket + (distance >= (1 << k)).astype(jnp.int32)
    columns = []
    for table_ref, index in ((time_bias_ref, times_ref[...]), (pos_bias_ref, bucket)):
        table = jnp.concatenate(three_parts(table_ref[...] * 0.5), axis=0)
        kinds = table.shape[1]
        hot = lax.broadcasted_iota(jnp.int32, (kinds, events), 0) == index
        columns.append(
            jnp.dot(table, hot.astype(F32).astype(BF16), preferred_element_type=F32)
        )
    used = sum(c.shape[0] for c in columns)
    columns.append(jnp.zeros((LANES - used, events), F32))
    out_ref[...] = jnp.concatenate(columns, axis=0).T.astype(BF16)


def bias_columns(place, start, times, time_bias, pos_bias, npos, history):
    return pl.pallas_call(
        functools.partial(bias_kernel, npos=npos, history=history),
        out_shape=jax.ShapeDtypeStruct((times.shape[1], LANES), BF16),
        in_specs=[SMEM, SMEM, VMEM, VMEM, VMEM],
        out_specs=VMEM,
        compiler_params=params(16),
        cost_estimate=pl.CostEstimate(flops=1 << 25, transcendentals=0, bytes_accessed=1 << 20),
        name="bias",
    )(place, start, times, time_bias, pos_bias)


def silu(x):
    return x / (1.0 + jnp.exp(-x))


def normalise(embedded, gain):
    x = embedded.astype(F32)
    meansq = jnp.mean(x * x, axis=-1, keepdims=True)
    return (x * lax.rsqrt(meansq + 1e-06) * gain).astype(BF16)


def attend_kernel(
    rounds_ref, pick_ref, near_ref, far_ref, extra_hbm, gain_ref, proj_hbm, key_hbm, value_hbm, bias_ref,
    own_ref, keep_ref, send_ref, emb_ref, query_ref, proj_ref, key_ref, value_ref, sems, *, heads
):
    count, width = emb_ref.shape
    copies = [
        pltpu.make_async_copy(proj_hbm.at[:, pl.ds(0, width)], proj_ref, sems.at[0]),
        pltpu.make_async_copy(key_hbm, key_ref, sems.at[1]),
        pltpu.make_async_copy(value_hbm, value_ref, sems.at[2]),
    ]
    for c in copies:
        c.start()
    split = near_ref.shape[0]
    picked = jnp.dot(pick_ref[:, :split], near_ref[...], preferred_element_type=F32)
    picked = picked + jnp.dot(pick_ref[:, split:], far_ref[...], preferred_element_type=F32)
    emb_ref[...] = picked.astype(BF16)

    @pl.when(rounds_ref[0] > 1)
    def _():
        extra = pltpu.make_async_copy(extra_hbm, query_ref, sems.at[3])
        extra.start()
        extra.wait()
        emb_ref[...] = emb_ref[...] + query_ref[...]

    own_ref[...] = emb_ref[: own_ref.shape[0], :]
    head_dim = width // heads
    events = key_ref.shape[0]
    half = count // 2
    rows = min(ROWS_AT_ONCE, count)
    per = LANES // head_dim
    step = min(EVENTS_AT_ONCE, events)
    copies[0].wait()
    for first in range(0, count, rows):
        normed = normalise(emb_ref[first : first + rows, :], gain_ref[...])
        projected = jnp.dot(normed, proj_ref[...], preferred_element_type=F32)
        query = silu(projected).astype(BF16)
        query_ref[first : first + rows, :] = query * jnp.asarray(0.5 * head_dim**-0.5, BF16)
        if first == 0:
            copies[1].wait()
            copies[2].wait()
        lane = lax.broadcasted_iota(jnp.int32, (rows, LANES), 1)
        for group in range(heads // per):
            at = slice(group * LANES, (group + 1) * LANES)
            part = query_ref[first : first + rows, at]
            zero, one = jnp.zeros_like(part), jnp.ones_like(part)
            stacked = []
            for k in range(per):
                own = jnp.where(lane // head_dim == k, part, zero)
                chosen = jnp.where(lane % heads == group * per + k, one, zero)
                stacked.append(jnp.concatenate([own, chosen], axis=1))
            left = jnp.concatenate(stacked, axis=0)
            total = jnp.zeros((per * rows, LANES), F32)
            for j in range(0, events, step):
                right = jnp.concatenate([key_ref[j : j + step, at], bias_ref[j : j + step, :]], axis=1)
                t = lax.dot_general(left, right, NT, preferred_element_type=F32)
                weights = (t + t * jnp.tanh(t)).astype(BF16)
                total = total + jnp.dot(weights, value_ref[j : j + step, at], preferred_element_type=F32)
            out = total[:rows]
            for k in range(1, per):
                out = jnp.where(lane // head_dim == k, total[k * rows : (k + 1) * rows], out)
            if first + rows <= half:
                keep_ref[first : first + rows, at] = out
            elif first >= half:
                send_ref[first - half : first - half + rows, at] = out.astype(BF16)
            else:
                keep_ref[first:half, at] = out[: half - first]
                send_ref[: first + rows - half, at] = out[half - first :].astype(BF16)


def attend(rounds, pick, near, far, extra, gain, proj_in, keys, values, bias, heads, each):
    count, width = extra.shape
    return pl.pallas_call(
        functools.partial(attend_kernel, heads=heads),
        out_shape=(
            jax.ShapeDtypeStruct((each, width), BF16),
            jax.ShapeDtypeStruct((count // 2, width), F32),
            jax.ShapeDtypeStruct((count // 2, width), BF16),
        ),
        in_specs=[SMEM, VMEM, VMEM, VMEM, HBM, VMEM, HBM, HBM, HBM, VMEM],
        out_specs=(VMEM, VMEM, VMEM),
        scratch_shapes=[
            pltpu.VMEM((count, width), BF16),
            pltpu.VMEM((count, width), BF16),
            pltpu.VMEM((width, width), BF16),
            pltpu.VMEM(keys.shape, BF16),
            pltpu.VMEM(values.shape, BF16),
            pltpu.SemaphoreType.DMA((4,)),
        ],
        compiler_params=params(48),
        cost_estimate=pl.CostEstimate(
            flops=8 * count * width * keys.shape[0],
            transcendentals=count * heads * keys.shape[0],
            bytes_accessed=4 * keys.size,
        ),
        name="attend",
    )(rounds, pick, near, far, extra, gain, proj_in, keys, values, bias)


def gates_kernel(emb_ref, gain_ref, proj_ref, out_ref):
    normed = normalise(emb_ref[...], gain_ref[...])
    projected = jnp.dot(normed, proj_ref[...], preferred_element_type=F32)
    out_ref[...] = silu(projected).astype(BF16)


def gates_of(embedded, gain, proj_in):
    return pl.pallas_call(
        gates_kernel,
        out_shape=jax.ShapeDtypeStruct(embedded.shape, BF16),
        grid=(1,),
        in_specs=[VMEM, VMEM, pl.BlockSpec(proj_in.shape[:1] * 2, lambda i: (0, 1))],
        out_specs=VMEM,
        compiler_params=params(16),
        cost_estimate=pl.CostEstimate(flops=1 << 26, transcendentals=1 << 14, bytes_accessed=1 << 22),
        name="gates",
    )(embedded, gain, proj_in)


def finish_kernel(own_ref, *refs):
    *parts, emb_ref, gates_ref, gain_ref, proj_ref, out_ref = refs
    attended = own_ref[...]
    for p in parts:
        attended = attended + p[...].astype(F32)
    centred = attended - jnp.mean(attended, axis=-1, keepdims=True)
    variance = jnp.mean(centred * centred, axis=-1, keepdims=True)
    gated = centred * lax.rsqrt(variance + 1e-05) * gain_ref[...] * gates_ref[...].astype(F32)
    product = jnp.dot(gated.astype(BF16), proj_ref[...], preferred_element_type=F32)
    out_ref[...] = (emb_ref[...].astype(F32) + product).astype(BF16)


def finish(own, parts, embedded, gates, gain, proj_out):
    return pl.pallas_call(
        finish_kernel,
        out_shape=jax.ShapeDtypeStruct(embedded.shape, BF16),
        in_specs=[VMEM] * (len(parts) + 5),
        out_specs=VMEM,
        compiler_params=params(16),
        name="finish",
    )(own, *parts, embedded, gates, gain, proj_out)


def on_device(
    item_ids,
    item_table,
    key_cache,
    value_cache,
    time_buckets,
    window_start,
    norm_gain,
    proj_in,
    time_bias,
    pos_bias,
    out_gain,
    proj_out,
):
    axis = "hist"
    size = lax.axis_size(axis)
    me = lax.axis_index(axis).astype(jnp.int32)
    each = item_ids.shape[0]
    slots = 2 * each
    heads = time_bias.shape[0]
    npos = pos_bias.shape[1]
    events = key_cache.shape[0]
    table_rows = item_table.shape[0]
    gain = norm_gain[None, :]

    def place(turn):
        return jnp.stack([me, jnp.asarray(turn, jnp.int32)])

    here = place(0)
    bias = bias_columns(
        here,
        window_start,
        time_buckets[None, :],
        time_bias,
        jnp.pad(pos_bias, ((0, 0), (0, -npos % 32))),
        npos,
        2 * events * size,
    )
    ids = gather_relative(item_ids[None, :], 1, axis, size, True)

    def fetch(turn):
        found = lookup(place(turn), ids, item_table, slots, size)
        return gather_relative(found, 0, axis, size, False)

    near, far = fetch(0)
    pick, rounds = plan(here, ids, slots, table_rows, size)

    def more(state):
        turn, so_far = state
        picked, _ = plan(place(turn), ids, slots, table_rows, size)
        return turn + 1, so_far + select(picked, fetch(turn))

    none = jnp.zeros((each * size, item_table.shape[1]), BF16)
    _, extra = lax.while_loop(lambda s: s[0] < rounds[0], more, (jnp.int32(1), none))

    own, keep, send = attend(
        rounds, pick, near, far, extra, gain, proj_in, key_cache, value_cache, bias, heads, each
    )
    gates = gates_of(own, gain, proj_in)

    stages = stage_masks(size, False)[::-1]
    total = keep + swap(send, stages[0][0], axis, size).astype(F32)
    for bits in stages[1:]:
        masks = combos(bits)
        block = total.shape[0] // len(masks)
        parts = [
            swap(total[k * block : (k + 1) * block].astype(BF16), m, axis, size)
            for k, m in enumerate(masks)
            if k
        ]
        if bits is stages[-1]:
            break
        total = sum([p.astype(F32) for p in parts], total[:block])
    return finish(total[:block], parts, own, gates, out_gain[None, :], proj_out)


def solution(mesh):
    placed = (
        P(("grp", "hist")),
        P("hist", None),
        P(("grp", "hist"), None),
        P(("grp", "hist"), None),
        P(("grp", "hist")),
        P("grp"),
        P(),
        P(),
        P(),
        P(),
        P(),
        P(),
    )

    return jax.shard_map(on_device, mesh=mesh, in_specs=placed, out_specs=P(("grp", "hist"), None), check_vma=False)
```

```python
import functools

import jax
import jax.numpy as jnp
from jax import lax
from jax.experimental import pallas as pl
from jax.experimental.pallas import tpu as pltpu
from jax.sharding import PartitionSpec as P


BF16 = jnp.bfloat16
F32 = jnp.float32
LANES = 128
ROWS_AT_ONCE = 256
EVENTS_AT_ONCE = 512
NT = (((1,), (1,)), ((), ()))
VMEM = pl.BlockSpec(memory_space=pltpu.VMEM)
SMEM = pl.BlockSpec(memory_space=pltpu.SMEM)
HBM = pl.BlockSpec(memory_space=pltpu.HBM)


def params(mib):
    return pltpu.CompilerParams(vmem_limit_bytes=mib << 20)


def stage_masks(size):
    bits = [1 << k for k in range(size.bit_length() - 1)][::-1]
    far = bits[:-2]
    return [sorted(far[k : k + 2]) for k in range(0, len(far), 2)] + [[2], [1]]


def combos(bits):
    out = [0]
    for b in bits:
        out = out + [m | b for m in out]
    return out


def swap(x, mask, axis, size):
    return lax.ppermute(x, axis, [(i, i ^ mask) for i in range(size)])


def gather_far(x, dim, axis, size):
    for bits in stage_masks(size)[:-2]:
        x = jnp.concatenate([x] + [swap(x, m, axis, size) for m in combos(bits)[1:]], axis=dim)
    return x


def gather_relative(x, dim, axis, size, direct):
    x = gather_far(x, dim, axis, size)
    beside = swap(x, 2, axis, size)
    other = swap(x, 1, axis, size)
    if direct:
        return [x, beside, other, swap(x, 3, axis, size)]
    return [x, beside, other, swap(beside, 1, axis, size)]


def position_bits(size):
    return [b for stage in stage_masks(size) for b in stage]


def candidates_info(ids_refs, me, size, table_rows):
    ids = jnp.concatenate([r[...] for r in ids_refs], axis=1)
    count = ids.shape[1]
    each = count // size
    owner = ids // table_rows
    place = lax.broadcasted_iota(jnp.int32, (1, count), 1)
    block = place // each
    mask = jnp.zeros_like(place)
    for k, b in enumerate(position_bits(size)):
        mask = mask + ((block >> k) & 1) * b
    key = owner * count + (mask ^ me) * each + place % each
    return owner, key, ids - owner * table_rows


def to_column(row):
    count = row.shape[1]
    r = lax.broadcasted_iota(jnp.int32, (count, count), 0)
    c = lax.broadcasted_iota(jnp.int32, (count, count), 1)
    return jnp.sum(jnp.where(r == c, row, 0), axis=1, keepdims=True)


def lookup_kernel(place_ref, *refs, size):
    *ids_refs, table_ref, out_ref, rounds_ref = refs
    me, turn = place_ref[0], place_ref[1]
    slots = out_ref.shape[0]
    rows = table_ref.shape[0]
    owner, key, offset = candidates_info(ids_refs, me, size, rows)
    count = owner.shape[1]
    key_col = to_column(key)
    before = (key_col < key) & (key_col >= owner * count)
    rank = jnp.sum(before.astype(jnp.int32), axis=0, keepdims=True)
    slot = lax.broadcasted_iota(jnp.int32, (slots, count), 0) + turn * slots
    hit = (owner == me) & (rank == slot)
    want = jnp.sum(jnp.where(hit, offset + 1, 0), axis=1, keepdims=True) - 1
    pick = (want == lax.broadcasted_iota(jnp.int32, (slots, rows), 1)).astype(F32).astype(BF16)
    rounds_ref[0] = jnp.max(rank) // slots + 1
    out_ref[...] = jnp.dot(pick, table_ref[...], preferred_element_type=F32).astype(BF16)


def lookup(place, ids, table, slots, size):
    return pl.pallas_call(
        functools.partial(lookup_kernel, size=size),
        out_shape=(
            jax.ShapeDtypeStruct((slots, table.shape[1]), BF16),
            jax.ShapeDtypeStruct((1,), jnp.int32),
        ),
        in_specs=[SMEM] + [VMEM] * (len(ids) + 1),
        out_specs=(VMEM, SMEM),
        compiler_params=params(24),
        cost_estimate=pl.CostEstimate(flops=1 << 26, transcendentals=0, bytes_accessed=2 * table.size),
        name="lookup",
    )(place, *ids, table)


def plan_kernel(place_ref, *refs, size, slots, table_rows):
    *ids_refs, pick_ref = refs
    me, turn = place_ref[0], place_ref[1]
    owner, key, _ = candidates_info(ids_refs, me, size, table_rows)
    count = owner.shape[1]
    key_col = to_column(key)
    owner_col = key_col // count
    before = (key < key_col) & (key >= owner_col * count)
    rank = jnp.sum(before.astype(jnp.int32), axis=1, keepdims=True)
    away = owner_col ^ me
    block = jnp.zeros_like(away)
    for k, b in enumerate(position_bits(size)):
        block = block + jnp.where((away & b) != 0, 1 << k, 0)
    mine = rank - turn * slots
    slot = jnp.where((mine >= 0) & (mine < slots), block * slots + mine, -1)
    pick = slot == lax.broadcasted_iota(jnp.int32, pick_ref.shape, 1)
    pick_ref[...] = pick.astype(F32).astype(BF16)


def plan(place, ids, slots, table_rows, size):
    count = sum(i.shape[1] for i in ids)
    return pl.pallas_call(
        functools.partial(plan_kernel, size=size, slots=slots, table_rows=table_rows),
        out_shape=jax.ShapeDtypeStruct((count, size * slots), BF16),
        in_specs=[SMEM] + [VMEM] * len(ids),
        out_specs=VMEM,
        compiler_params=params(40),
        cost_estimate=pl.CostEstimate(flops=1 << 22, transcendentals=0, bytes_accessed=1 << 20),
        name="plan",
    )(place, *ids)


def select_kernel(pick_ref, rows_ref, out_ref):
    out_ref[...] = jnp.dot(pick_ref[...], rows_ref[...], preferred_element_type=F32).astype(BF16)


def select(pick, pieces):
    rows = jnp.concatenate(pieces, axis=0)
    return pl.pallas_call(
        select_kernel,
        out_shape=jax.ShapeDtypeStruct((pick.shape[0], rows.shape[1]), BF16),
        in_specs=[VMEM, VMEM],
        out_specs=VMEM,
        compiler_params=params(32),
        name="select",
    )(pick, rows)


def three_parts(x):
    high = x.astype(BF16)
    rest = x - high.astype(F32)
    middle = rest.astype(BF16)
    return [high, middle, (rest - middle.astype(F32)).astype(BF16)]


def bias_kernel(place_ref, start_ref, times_ref, time_bias_ref, pos_bias_ref, out_ref, *, npos, history):
    events = times_ref.shape[1]
    first = history - start_ref[0] - place_ref[0] * events
    distance = first - lax.broadcasted_iota(jnp.int32, (1, events), 1)
    bucket = jnp.zeros((1, events), jnp.int32)
    for k in range(1, npos):
        bucket = bucket + (distance >= (1 << k)).astype(jnp.int32)
    columns = []
    for table_ref, index in ((time_bias_ref, times_ref[...]), (pos_bias_ref, bucket)):
        table = jnp.concatenate(three_parts(table_ref[...] * 0.5), axis=0)
        kinds = table.shape[1]
        hot = lax.broadcasted_iota(jnp.int32, (kinds, events), 0) == index
        columns.append(
            jnp.dot(table, hot.astype(F32).astype(BF16), preferred_element_type=F32)
        )
    used = sum(c.shape[0] for c in columns)
    columns.append(jnp.zeros((LANES - used, events), F32))
    out_ref[...] = jnp.concatenate(columns, axis=0).T.astype(BF16)


def bias_columns(place, start, times, time_bias, pos_bias, npos, history):
    return pl.pallas_call(
        functools.partial(bias_kernel, npos=npos, history=history),
        out_shape=jax.ShapeDtypeStruct((times.shape[1], LANES), BF16),
        in_specs=[SMEM, SMEM, VMEM, VMEM, VMEM],
        out_specs=VMEM,
        compiler_params=params(16),
        cost_estimate=pl.CostEstimate(flops=1 << 25, transcendentals=0, bytes_accessed=1 << 20),
        name="bias",
    )(place, start, times, time_bias, pos_bias)


def silu(x):
    return x / (1.0 + jnp.exp(-x))


def normalise(embedded, gain):
    x = embedded.astype(F32)
    meansq = jnp.mean(x * x, axis=-1, keepdims=True)
    return (x * lax.rsqrt(meansq + 1e-06) * gain).astype(BF16)


def attend_kernel(
    rounds_ref, pick_ref, *refs, heads
):
    *row_refs, extra_hbm, gain_ref, proj_ref, key_ref, value_ref, bias_ref = refs[:-6]
    own_ref, keep_ref, send_ref, emb_ref, query_ref, sem = refs[-6:]
    count, width = emb_ref.shape
    rows = jnp.concatenate([r[...] for r in row_refs], axis=0)
    emb_ref[...] = jnp.dot(pick_ref[...], rows, preferred_element_type=F32).astype(BF16)

    @pl.when(rounds_ref[0] > 1)
    def _():
        extra = pltpu.make_async_copy(extra_hbm, query_ref, sem)
        extra.start()
        extra.wait()
        emb_ref[...] = emb_ref[...] + query_ref[...]

    own_ref[...] = emb_ref[: own_ref.shape[0], :]
    head_dim = width // heads
    events = key_ref.shape[0]
    half = count // 2
    rows = min(ROWS_AT_ONCE, count)
    per = LANES // head_dim
    step = min(EVENTS_AT_ONCE, events)
    for first in range(0, count, rows):
        normed = normalise(emb_ref[first : first + rows, :], gain_ref[...])
        projected = jnp.dot(normed, proj_ref[:, :width], preferred_element_type=F32)
        query = silu(projected).astype(BF16)
        query_ref[first : first + rows, :] = query * jnp.asarray(0.5 * head_dim**-0.5, BF16)
        lane = lax.broadcasted_iota(jnp.int32, (rows, LANES), 1)
        for group in range(heads // per):
            at = slice(group * LANES, (group + 1) * LANES)
            part = query_ref[first : first + rows, at]
            zero, one = jnp.zeros_like(part), jnp.ones_like(part)
            stacked = []
            for k in range(per):
                own = jnp.where(lane // head_dim == k, part, zero)
                chosen = jnp.where(lane % heads == group * per + k, one, zero)
                stacked.append(jnp.concatenate([own, chosen], axis=1))
            left = jnp.concatenate(stacked, axis=0)
            total = jnp.zeros((per * rows, LANES), F32)
            for j in range(0, events, step):
                right = jnp.concatenate([key_ref[j : j + step, at], bias_ref[j : j + step, :]], axis=1)
                t = lax.dot_general(left, right, NT, preferred_element_type=F32)
                weights = (t + t * jnp.tanh(t)).astype(BF16)
                total = total + jnp.dot(weights, value_ref[j : j + step, at], preferred_element_type=F32)
            out = total[:rows]
            for k in range(1, per):
                out = jnp.where(lane // head_dim == k, total[k * rows : (k + 1) * rows], out)
            if first + rows <= half:
                keep_ref[first : first + rows, at] = out
            elif first >= half:
                send_ref[first - half : first - half + rows, at] = out.astype(BF16)
            else:
                keep_ref[first:half, at] = out[: half - first]
                send_ref[: first + rows - half, at] = out[half - first :].astype(BF16)


def attend(rounds, pick, pieces, extra, gain, proj_in, keys, values, bias, heads, each):
    count, width = extra.shape
    return pl.pallas_call(
        functools.partial(attend_kernel, heads=heads),
        out_shape=(
            jax.ShapeDtypeStruct((each, width), BF16),
            jax.ShapeDtypeStruct((count // 2, width), F32),
            jax.ShapeDtypeStruct((count // 2, width), BF16),
        ),
        in_specs=[SMEM, VMEM] + [VMEM] * len(pieces) + [HBM] + [VMEM] * 5,
        out_specs=(VMEM, VMEM, VMEM),
        scratch_shapes=[
            pltpu.VMEM((count, width), BF16),
            pltpu.VMEM((count, width), BF16),
            pltpu.SemaphoreType.DMA,
        ],
        compiler_params=params(40),
        cost_estimate=pl.CostEstimate(
            flops=8 * count * width * keys.shape[0],
            transcendentals=count * heads * keys.shape[0],
            bytes_accessed=4 * keys.size,
        ),
        name="attend",
    )(rounds, pick, *pieces, extra, gain, proj_in, keys, values, bias)


def gates_kernel(emb_ref, gain_ref, proj_ref, out_ref):
    normed = normalise(emb_ref[...], gain_ref[...])
    projected = jnp.dot(normed, proj_ref[...], preferred_element_type=F32)
    out_ref[...] = silu(projected).astype(BF16)


def gates_of(embedded, gain, proj_in):
    return pl.pallas_call(
        gates_kernel,
        out_shape=jax.ShapeDtypeStruct(embedded.shape, BF16),
        grid=(1,),
        in_specs=[VMEM, VMEM, pl.BlockSpec(proj_in.shape[:1] * 2, lambda i: (0, 1))],
        out_specs=VMEM,
        compiler_params=params(16),
        cost_estimate=pl.CostEstimate(flops=1 << 26, transcendentals=1 << 14, bytes_accessed=1 << 22),
        name="gates",
    )(embedded, gain, proj_in)


def finish_kernel(own_ref, *refs):
    *parts, emb_ref, gates_ref, gain_ref, proj_ref, out_ref = refs
    attended = own_ref[...]
    for p in parts:
        attended = attended + p[...].astype(F32)
    centred = attended - jnp.mean(attended, axis=-1, keepdims=True)
    variance = jnp.mean(centred * centred, axis=-1, keepdims=True)
    gated = centred * lax.rsqrt(variance + 1e-05) * gain_ref[...] * gates_ref[...].astype(F32)
    product = jnp.dot(gated.astype(BF16), proj_ref[...], preferred_element_type=F32)
    out_ref[...] = (emb_ref[...].astype(F32) + product).astype(BF16)


def finish(own, parts, embedded, gates, gain, proj_out):
    return pl.pallas_call(
        finish_kernel,
        out_shape=jax.ShapeDtypeStruct(embedded.shape, BF16),
        in_specs=[VMEM] * (len(parts) + 5),
        out_specs=VMEM,
        compiler_params=params(16),
        name="finish",
    )(own, *parts, embedded, gates, gain, proj_out)


def on_device(
    item_ids,
    item_table,
    key_cache,
    value_cache,
    time_buckets,
    window_start,
    norm_gain,
    proj_in,
    time_bias,
    pos_bias,
    out_gain,
    proj_out,
):
    axis = "hist"
    size = lax.axis_size(axis)
    me = lax.axis_index(axis).astype(jnp.int32)
    each = item_ids.shape[0]
    slots = 2 * each
    heads = time_bias.shape[0]
    npos = pos_bias.shape[1]
    events = key_cache.shape[0]
    table_rows = item_table.shape[0]
    gain = norm_gain[None, :]

    def place(turn):
        return jnp.stack([me, jnp.asarray(turn, jnp.int32)])

    here = place(0)
    bias = bias_columns(
        here,
        window_start,
        time_buckets[None, :],
        time_bias,
        jnp.pad(pos_bias, ((0, 0), (0, -npos % 32))),
        npos,
        2 * events * size,
    )
    ids = gather_relative(item_ids[None, :], 1, axis, size, True)

    def fetch(turn):
        found, rounds = lookup(place(turn), ids, item_table, slots, size)
        return gather_relative(found, 0, axis, size, False), rounds

    pieces, rounds = fetch(0)
    pick = plan(here, ids, slots, table_rows, size)

    def more(state):
        turn, so_far = state
        picked = plan(place(turn), ids, slots, table_rows, size)
        return turn + 1, so_far + select(picked, fetch(turn)[0])

    none = jnp.zeros((each * size, item_table.shape[1]), BF16)
    _, extra = lax.while_loop(lambda s: s[0] < rounds[0], more, (jnp.int32(1), none))

    own, keep, send = attend(
        rounds, pick, pieces, extra, gain, proj_in, key_cache, value_cache, bias, heads, each
    )
    gates = gates_of(own, gain, proj_in)

    stages = stage_masks(size)[::-1]
    total = keep + swap(send, 1, axis, size).astype(F32)
    for bits in stages[1:]:
        masks = combos(bits)
        block = total.shape[0] // len(masks)
        parts = [
            swap(total[k * block : (k + 1) * block].astype(BF16), m, axis, size)
            for k, m in enumerate(masks)
            if k
        ]
        if bits is stages[-1]:
            break
        total = sum([p.astype(F32) for p in parts], total[:block])
    return finish(total[:block], parts, own, gates, out_gain[None, :], proj_out)


def solution(mesh):
    placed = (
        P(("grp", "hist")),
        P("hist", None),
        P(("grp", "hist"), None),
        P(("grp", "hist"), None),
        P(("grp", "hist")),
        P("grp"),
        P(),
        P(),
        P(),
        P(),
        P(),
        P(),
    )

    return jax.shard_map(on_device, mesh=mesh, in_specs=placed, out_specs=P(("grp", "hist"), None), check_vma=False)
```

```python
import functools

import jax
import jax.numpy as jnp
from jax import lax
from jax.experimental import pallas as pl
from jax.experimental.pallas import tpu as pltpu
from jax.sharding import PartitionSpec as P


BF16 = jnp.bfloat16
F32 = jnp.float32
LANES = 128
ROWS_AT_ONCE = 256
EVENTS_AT_ONCE = 512
NT = (((1,), (1,)), ((), ()))
VMEM = pl.BlockSpec(memory_space=pltpu.VMEM)
SMEM = pl.BlockSpec(memory_space=pltpu.SMEM)
HBM = pl.BlockSpec(memory_space=pltpu.HBM)


def params(mib):
    return pltpu.CompilerParams(vmem_limit_bytes=mib << 20)


def stage_masks(size):
    bits = [1 << k for k in range(size.bit_length() - 1)][::-1]
    far = bits[:-2]
    return [sorted(far[k : k + 2]) for k in range(0, len(far), 2)] + [[2], [1]]


def combos(bits):
    out = [0]
    for b in bits:
        out = out + [m | b for m in out]
    return out


def swap(x, mask, axis, size):
    return lax.ppermute(x, axis, [(i, i ^ mask) for i in range(size)])


def join_kernel(*refs):
    *parts, out_ref = refs
    rows = parts[0].shape[0]
    for k, p in enumerate(parts):
        out_ref[k * rows : (k + 1) * rows, :] = p[...]


def join(pieces, dim):
    if dim:
        return jnp.concatenate(pieces, axis=dim)
    rows, width = pieces[0].shape
    return pl.pallas_call(
        join_kernel,
        out_shape=jax.ShapeDtypeStruct((len(pieces) * rows, width), BF16),
        in_specs=[VMEM] * len(pieces),
        out_specs=VMEM,
        compiler_params=params(16),
        name="join",
    )(*pieces)


def gather_far(x, dim, axis, size):
    for bits in stage_masks(size)[:-2]:
        x = join([x] + [swap(x, m, axis, size) for m in combos(bits)[1:]], dim)
    return x


def gather_relative(x, dim, axis, size, direct):
    x = gather_far(x, dim, axis, size)
    beside = swap(x, 2, axis, size)
    other = swap(x, 1, axis, size)
    if direct:
        return [x, beside, other, swap(x, 3, axis, size)]
    return [x, beside, other, swap(beside, 1, axis, size)]


def position_bits(size):
    return [b for stage in stage_masks(size) for b in stage]


def candidates_info(ids_refs, me, size, table_rows):
    ids = jnp.concatenate([r[...] for r in ids_refs], axis=1)
    count = ids.shape[1]
    each = count // size
    owner = ids // table_rows
    place = lax.broadcasted_iota(jnp.int32, (1, count), 1)
    block = place // each
    mask = jnp.zeros_like(place)
    for k, b in enumerate(position_bits(size)):
        mask = mask + ((block >> k) & 1) * b
    key = owner * count + (mask ^ me) * each + place % each
    return owner, key, ids - owner * table_rows


def to_column(row):
    count = row.shape[1]
    r = lax.broadcasted_iota(jnp.int32, (count, count), 0)
    c = lax.broadcasted_iota(jnp.int32, (count, count), 1)
    return jnp.sum(jnp.where(r == c, row, 0), axis=1, keepdims=True)


def lookup_kernel(place_ref, *refs, size):
    *ids_refs, table_ref, out_ref, rounds_ref = refs
    me, turn = place_ref[0], place_ref[1]
    slots = out_ref.shape[0]
    rows = table_ref.shape[0]
    owner, key, offset = candidates_info(ids_refs, me, size, rows)
    count = owner.shape[1]
    key_col = to_column(key)
    before = (key_col < key) & (key_col >= owner * count)
    rank = jnp.sum(before.astype(jnp.int32), axis=0, keepdims=True)
    slot = lax.broadcasted_iota(jnp.int32, (slots, count), 0) + turn * slots
    hit = (owner == me) & (rank == slot)
    want = jnp.sum(jnp.where(hit, offset + 1, 0), axis=1, keepdims=True) - 1
    pick = (want == lax.broadcasted_iota(jnp.int32, (slots, rows), 1)).astype(F32).astype(BF16)
    rounds_ref[0] = jnp.max(rank) // slots + 1
    out_ref[...] = jnp.dot(pick, table_ref[...], preferred_element_type=F32).astype(BF16)


def lookup(place, ids, table, slots, size):
    return pl.pallas_call(
        functools.partial(lookup_kernel, size=size),
        out_shape=(
            jax.ShapeDtypeStruct((slots, table.shape[1]), BF16),
            jax.ShapeDtypeStruct((1,), jnp.int32),
        ),
        in_specs=[SMEM] + [VMEM] * (len(ids) + 1),
        out_specs=(VMEM, SMEM),
        compiler_params=params(24),
        cost_estimate=pl.CostEstimate(flops=1 << 26, transcendentals=0, bytes_accessed=2 * table.size),
        name="lookup",
    )(place, *ids, table)


def plan_kernel(place_ref, *refs, size, slots, table_rows):
    *ids_refs, pick_ref = refs
    me, turn = place_ref[0], place_ref[1]
    owner, key, _ = candidates_info(ids_refs, me, size, table_rows)
    count = owner.shape[1]
    key_col = to_column(key)
    owner_col = key_col // count
    before = (key < key_col) & (key >= owner_col * count)
    rank = jnp.sum(before.astype(jnp.int32), axis=1, keepdims=True)
    away = owner_col ^ me
    block = jnp.zeros_like(away)
    for k, b in enumerate(position_bits(size)):
        block = block + jnp.where((away & b) != 0, 1 << k, 0)
    mine = rank - turn * slots
    slot = jnp.where((mine >= 0) & (mine < slots), block * slots + mine, -1)
    pick = slot == lax.broadcasted_iota(jnp.int32, pick_ref.shape, 1)
    pick_ref[...] = pick.astype(F32).astype(BF16)


def plan(place, ids, slots, table_rows, size):
    count = sum(i.shape[1] for i in ids)
    return pl.pallas_call(
        functools.partial(plan_kernel, size=size, slots=slots, table_rows=table_rows),
        out_shape=jax.ShapeDtypeStruct((count, size * slots), BF16),
        in_specs=[SMEM] + [VMEM] * len(ids),
        out_specs=VMEM,
        compiler_params=params(40),
        cost_estimate=pl.CostEstimate(flops=1 << 22, transcendentals=0, bytes_accessed=1 << 20),
        name="plan",
    )(place, *ids)


def select_kernel(pick_ref, rows_ref, out_ref):
    out_ref[...] = jnp.dot(pick_ref[...], rows_ref[...], preferred_element_type=F32).astype(BF16)


def select(pick, pieces):
    rows = jnp.concatenate(pieces, axis=0)
    return pl.pallas_call(
        select_kernel,
        out_shape=jax.ShapeDtypeStruct((pick.shape[0], rows.shape[1]), BF16),
        in_specs=[VMEM, VMEM],
        out_specs=VMEM,
        compiler_params=params(32),
        name="select",
    )(pick, rows)


def three_parts(x):
    high = x.astype(BF16)
    rest = x - high.astype(F32)
    middle = rest.astype(BF16)
    return [high, middle, (rest - middle.astype(F32)).astype(BF16)]


def bias_kernel(place_ref, start_ref, times_ref, time_bias_ref, pos_bias_ref, out_ref, *, npos, history):
    events = times_ref.shape[1]
    first = history - start_ref[0] - place_ref[0] * events
    distance = first - lax.broadcasted_iota(jnp.int32, (1, events), 1)
    bucket = jnp.zeros((1, events), jnp.int32)
    for k in range(1, npos):
        bucket = bucket + (distance >= (1 << k)).astype(jnp.int32)
    columns = []
    for table_ref, index in ((time_bias_ref, times_ref[...]), (pos_bias_ref, bucket)):
        table = jnp.concatenate(three_parts(table_ref[...] * 0.5), axis=0)
        kinds = table.shape[1]
        hot = lax.broadcasted_iota(jnp.int32, (kinds, events), 0) == index
        columns.append(
            jnp.dot(table, hot.astype(F32).astype(BF16), preferred_element_type=F32)
        )
    used = sum(c.shape[0] for c in columns)
    columns.append(jnp.zeros((LANES - used, events), F32))
    out_ref[...] = jnp.concatenate(columns, axis=0).T.astype(BF16)


def bias_columns(place, start, times, time_bias, pos_bias, npos, history):
    return pl.pallas_call(
        functools.partial(bias_kernel, npos=npos, history=history),
        out_shape=jax.ShapeDtypeStruct((times.shape[1], LANES), BF16),
        in_specs=[SMEM, SMEM, VMEM, VMEM, VMEM],
        out_specs=VMEM,
        compiler_params=params(16),
        cost_estimate=pl.CostEstimate(flops=1 << 25, transcendentals=0, bytes_accessed=1 << 20),
        name="bias",
    )(place, start, times, time_bias, pos_bias)


def silu(x):
    return x / (1.0 + jnp.exp(-x))


def normalise(embedded, gain):
    x = embedded.astype(F32)
    meansq = jnp.mean(x * x, axis=-1, keepdims=True)
    return (x * lax.rsqrt(meansq + 1e-06) * gain).astype(BF16)


def attend_kernel(
    rounds_ref, pick_ref, *refs, heads
):
    *row_refs, extra_hbm, gain_ref, proj_ref, key_ref, value_ref, bias_ref = refs[:-6]
    own_ref, keep_ref, send_ref, emb_ref, query_ref, sem = refs[-6:]
    count, width = emb_ref.shape
    rows = jnp.concatenate([r[...] for r in row_refs], axis=0)
    emb_ref[...] = jnp.dot(pick_ref[...], rows, preferred_element_type=F32).astype(BF16)

    @pl.when(rounds_ref[0] > 1)
    def _():
        extra = pltpu.make_async_copy(extra_hbm, query_ref, sem)
        extra.start()
        extra.wait()
        emb_ref[...] = emb_ref[...] + query_ref[...]

    own_ref[...] = emb_ref[: own_ref.shape[0], :]
    head_dim = width // heads
    events = key_ref.shape[0]
    half = count // 2
    rows = min(ROWS_AT_ONCE, count)
    per = LANES // head_dim
    step = min(EVENTS_AT_ONCE, events)
    for first in range(0, count, rows):
        normed = normalise(emb_ref[first : first + rows, :], gain_ref[...])
        projected = jnp.dot(normed, proj_ref[:, :width], preferred_element_type=F32)
        query = silu(projected).astype(BF16)
        query_ref[first : first + rows, :] = query * jnp.asarray(0.5 * head_dim**-0.5, BF16)
        lane = lax.broadcasted_iota(jnp.int32, (rows, LANES), 1)
        for group in range(heads // per):
            at = slice(group * LANES, (group + 1) * LANES)
            part = query_ref[first : first + rows, at]
            zero, one = jnp.zeros_like(part), jnp.ones_like(part)
            stacked = []
            for k in range(per):
                own = jnp.where(lane // head_dim == k, part, zero)
                chosen = jnp.where(lane % heads == group * per + k, one, zero)
                stacked.append(jnp.concatenate([own, chosen], axis=1))
            left = jnp.concatenate(stacked, axis=0)
            total = jnp.zeros((per * rows, LANES), F32)
            for j in range(0, events, step):
                right = jnp.concatenate([key_ref[j : j + step, at], bias_ref[j : j + step, :]], axis=1)
                t = lax.dot_general(left, right, NT, preferred_element_type=F32)
                weights = (t + t * jnp.tanh(t)).astype(BF16)
                total = total + jnp.dot(weights, value_ref[j : j + step, at], preferred_element_type=F32)
            out = total[:rows]
            for k in range(1, per):
                out = jnp.where(lane // head_dim == k, total[k * rows : (k + 1) * rows], out)
            if first + rows <= half:
                keep_ref[first : first + rows, at] = out
            elif first >= half:
                send_ref[first - half : first - half + rows, at] = out.astype(BF16)
            else:
                keep_ref[first:half, at] = out[: half - first]
                send_ref[: first + rows - half, at] = out[half - first :].astype(BF16)


def attend(rounds, pick, pieces, extra, gain, proj_in, keys, values, bias, heads, each):
    count, width = extra.shape
    return pl.pallas_call(
        functools.partial(attend_kernel, heads=heads),
        out_shape=(
            jax.ShapeDtypeStruct((each, width), BF16),
            jax.ShapeDtypeStruct((count // 2, width), F32),
            jax.ShapeDtypeStruct((count // 2, width), BF16),
        ),
        in_specs=[SMEM, VMEM] + [VMEM] * len(pieces) + [HBM] + [VMEM] * 5,
        out_specs=(VMEM, VMEM, VMEM),
        scratch_shapes=[
            pltpu.VMEM((count, width), BF16),
            pltpu.VMEM((count, width), BF16),
            pltpu.SemaphoreType.DMA,
        ],
        compiler_params=params(40),
        cost_estimate=pl.CostEstimate(
            flops=8 * count * width * keys.shape[0],
            transcendentals=count * heads * keys.shape[0],
            bytes_accessed=4 * keys.size,
        ),
        name="attend",
    )(rounds, pick, *pieces, extra, gain, proj_in, keys, values, bias)


def stage_kernel(proj_hbm, key_hbm, value_hbm, proj_ref, key_ref, value_ref, sems):
    copies = [
        pltpu.make_async_copy(proj_hbm.at[:, pl.ds(0, proj_ref.shape[1])], proj_ref, sems.at[0]),
        pltpu.make_async_copy(key_hbm, key_ref, sems.at[1]),
        pltpu.make_async_copy(value_hbm, value_ref, sems.at[2]),
    ]
    for c in copies:
        c.start()
    for c in copies:
        c.wait()


def stage(proj_in, keys, values):
    width = keys.shape[1]
    return pl.pallas_call(
        stage_kernel,
        out_shape=(
            jax.ShapeDtypeStruct((width, width), BF16),
            jax.ShapeDtypeStruct(keys.shape, BF16),
            jax.ShapeDtypeStruct(values.shape, BF16),
        ),
        in_specs=[HBM] * 3,
        out_specs=(VMEM,) * 3,
        scratch_shapes=[pltpu.SemaphoreType.DMA((3,))],
        compiler_params=params(16),
        name="stage",
    )(*(pltpu.with_memory_space_constraint(a, pltpu.HBM) for a in (proj_in, keys, values)))


def gates_kernel(emb_ref, gain_ref, proj_ref, out_ref):
    normed = normalise(emb_ref[...], gain_ref[...])
    projected = jnp.dot(normed, proj_ref[...], preferred_element_type=F32)
    out_ref[...] = silu(projected).astype(BF16)


def gates_of(embedded, gain, proj_in):
    return pl.pallas_call(
        gates_kernel,
        out_shape=jax.ShapeDtypeStruct(embedded.shape, BF16),
        grid=(1,),
        in_specs=[VMEM, VMEM, pl.BlockSpec(proj_in.shape[:1] * 2, lambda i: (0, 1))],
        out_specs=VMEM,
        compiler_params=params(16),
        cost_estimate=pl.CostEstimate(flops=1 << 26, transcendentals=1 << 14, bytes_accessed=1 << 22),
        name="gates",
    )(embedded, gain, proj_in)


def finish_kernel(own_ref, *refs):
    *parts, emb_ref, gates_ref, gain_ref, proj_ref, out_ref = refs
    attended = own_ref[...]
    for p in parts:
        attended = attended + p[...].astype(F32)
    centred = attended - jnp.mean(attended, axis=-1, keepdims=True)
    variance = jnp.mean(centred * centred, axis=-1, keepdims=True)
    gated = centred * lax.rsqrt(variance + 1e-05) * gain_ref[...] * gates_ref[...].astype(F32)
    product = jnp.dot(gated.astype(BF16), proj_ref[...], preferred_element_type=F32)
    out_ref[...] = (emb_ref[...].astype(F32) + product).astype(BF16)


def finish(own, parts, embedded, gates, gain, proj_out):
    return pl.pallas_call(
        finish_kernel,
        out_shape=jax.ShapeDtypeStruct(embedded.shape, BF16),
        in_specs=[VMEM] * (len(parts) + 5),
        out_specs=VMEM,
        compiler_params=params(16),
        name="finish",
    )(own, *parts, embedded, gates, gain, proj_out)


def on_device(
    item_ids,
    item_table,
    key_cache,
    value_cache,
    time_buckets,
    window_start,
    norm_gain,
    proj_in,
    time_bias,
    pos_bias,
    out_gain,
    proj_out,
):
    axis = "hist"
    size = lax.axis_size(axis)
    me = lax.axis_index(axis).astype(jnp.int32)
    each = item_ids.shape[0]
    slots = 2 * each
    heads = time_bias.shape[0]
    npos = pos_bias.shape[1]
    events = key_cache.shape[0]
    table_rows = item_table.shape[0]
    gain = norm_gain[None, :]

    def place(turn):
        return jnp.stack([me, jnp.asarray(turn, jnp.int32)])

    here = place(0)
    bias = bias_columns(
        here,
        window_start,
        time_buckets[None, :],
        time_bias,
        jnp.pad(pos_bias, ((0, 0), (0, -npos % 32))),
        npos,
        2 * events * size,
    )
    ids = gather_relative(item_ids[None, :], 1, axis, size, True)

    def fetch(turn):
        found, rounds = lookup(place(turn), ids, item_table, slots, size)
        return gather_relative(found, 0, axis, size, False), rounds

    pieces, rounds = fetch(0)
    pick = plan(here, ids, slots, table_rows, size)

    def more(state):
        turn, so_far = state
        picked = plan(place(turn), ids, slots, table_rows, size)
        return turn + 1, so_far + select(picked, fetch(turn)[0])

    none = jnp.zeros((each * size, item_table.shape[1]), BF16)
    _, extra = lax.while_loop(lambda s: s[0] < rounds[0], more, (jnp.int32(1), none))

    staged = stage(proj_in, key_cache, value_cache)
    own, keep, send = attend(rounds, pick, pieces, extra, gain, *staged, bias, heads, each)
    gates = gates_of(own, gain, proj_in)

    stages = stage_masks(size)[::-1]
    total = keep + swap(send, 1, axis, size).astype(F32)
    for bits in stages[1:]:
        masks = combos(bits)
        block = total.shape[0] // len(masks)
        parts = [
            swap(total[k * block : (k + 1) * block].astype(BF16), m, axis, size)
            for k, m in enumerate(masks)
            if k
        ]
        if bits is stages[-1]:
            break
        total = sum([p.astype(F32) for p in parts], total[:block])
    return finish(total[:block], parts, own, gates, out_gain[None, :], proj_out)


def solution(mesh):
    placed = (
        P(("grp", "hist")),
        P("hist", None),
        P(("grp", "hist"), None),
        P(("grp", "hist"), None),
        P(("grp", "hist")),
        P("grp"),
        P(),
        P(),
        P(),
        P(),
        P(),
        P(),
    )

    return jax.shard_map(
        on_device, mesh=mesh, in_specs=placed, out_specs=P(("grp", "hist"), None), check_vma=False
    )
```

```python
import functools

import jax
import jax.numpy as jnp
from jax import lax
from jax.experimental import pallas as pl
from jax.experimental.pallas import tpu as pltpu
from jax.sharding import PartitionSpec as P


BF16 = jnp.bfloat16
F32 = jnp.float32
LANES = 128
ROWS_AT_ONCE = 256
EVENTS_AT_ONCE = 1024
NT = (((1,), (1,)), ((), ()))
VMEM = pl.BlockSpec(memory_space=pltpu.VMEM)
SMEM = pl.BlockSpec(memory_space=pltpu.SMEM)
HBM = pl.BlockSpec(memory_space=pltpu.HBM)


def params(mib):
    return pltpu.CompilerParams(vmem_limit_bytes=mib << 20)


PARTNER = 1


def stage_masks(size):
    bits = [1 << k for k in range(1, size.bit_length() - 1)][::-1]
    far = bits[:-1]
    return [sorted(far[k : k + 2]) for k in range(0, len(far), 2)] + [bits[-1:]]


def combos(bits):
    out = [0]
    for b in bits:
        out = out + [m | b for m in out]
    return out


def swap(x, mask, axis, size):
    return lax.ppermute(x, axis, [(i, i ^ mask) for i in range(size)])


def join_kernel(*refs):
    *parts, out_ref = refs
    rows = parts[0].shape[0]
    for k, p in enumerate(parts):
        out_ref[k * rows : (k + 1) * rows, :] = p[...]


def join(pieces, dim):
    if dim:
        return jnp.concatenate(pieces, axis=dim)
    rows, width = pieces[0].shape
    return pl.pallas_call(
        join_kernel,
        out_shape=jax.ShapeDtypeStruct((len(pieces) * rows, width), BF16),
        in_specs=[VMEM] * len(pieces),
        out_specs=VMEM,
        compiler_params=params(16),
        name="join",
    )(*pieces)


def gather_relative(x, dim, axis, size):
    *far, near = stage_masks(size)
    for bits in far:
        x = join([x] + [swap(x, m, axis, size) for m in combos(bits)[1:]], dim)
    return [x, swap(x, near[0], axis, size)]


def position_bits(size):
    return [b for stage in stage_masks(size) for b in stage]


def candidates_info(ids_refs, me, size, table_rows):
    ids = jnp.concatenate([r[...] for r in ids_refs], axis=1)
    count = ids.shape[1]
    each = count // (size // 2)
    owner = ids // table_rows
    place = lax.broadcasted_iota(jnp.int32, (1, count), 1)
    block = place // each
    mask = jnp.zeros_like(place)
    for k, b in enumerate(position_bits(size)):
        mask = mask + ((block >> k) & 1) * b
    pair = owner >> 1
    key = pair * count + ((mask ^ me) >> 1) * each + place % each
    return pair, key, ids - owner * table_rows + ((owner ^ me) & 1) * table_rows


def to_column(row):
    count = row.shape[1]
    r = lax.broadcasted_iota(jnp.int32, (count, count), 0)
    c = lax.broadcasted_iota(jnp.int32, (count, count), 1)
    return jnp.sum(jnp.where(r == c, row, 0), axis=1, keepdims=True)


def lookup_kernel(place_ref, *refs, size, resident):
    if resident:
        *ids_refs, own_ref, other_ref, out_ref, rounds_ref = refs
        copies = []
    else:
        *ids_refs, own_hbm, other_hbm, out_ref, rounds_ref, own_ref, other_ref, sems = refs
        copies = [
            pltpu.make_async_copy(own_hbm, own_ref, sems.at[0]),
            pltpu.make_async_copy(other_hbm, other_ref, sems.at[1]),
        ]
    for c in copies:
        c.start()
    me, turn = place_ref[0], place_ref[1]
    slots = out_ref.shape[0]
    rows = own_ref.shape[0]
    pair, key, offset = candidates_info(ids_refs, me, size, rows)
    count = pair.shape[1]
    key_col = to_column(key)
    before = (key_col < key) & (key_col >= pair * count)
    rank = jnp.sum(before.astype(jnp.int32), axis=0, keepdims=True)
    slot = lax.broadcasted_iota(jnp.int32, (slots, count), 0) + turn * slots
    hit = (pair == (me >> 1)) & (rank == slot)
    want = jnp.sum(jnp.where(hit, offset + 1, 0), axis=1, keepdims=True) - 1
    row = lax.broadcasted_iota(jnp.int32, (slots, rows), 1)
    rounds_ref[0] = jnp.max(rank) // slots + 1
    for c in copies:
        c.wait()
    found = jnp.dot((want == row).astype(F32).astype(BF16), own_ref[...], preferred_element_type=F32)
    other = (want == row + rows).astype(F32).astype(BF16)
    out_ref[...] = (found + jnp.dot(other, other_ref[...], preferred_element_type=F32)).astype(BF16)


def lookup(place, ids, tables, slots, size, resident):
    if not resident:
        tables = [pltpu.with_memory_space_constraint(t, pltpu.HBM) for t in tables]
    rows, width = tables[0].shape
    return pl.pallas_call(
        functools.partial(lookup_kernel, size=size, resident=resident),
        out_shape=(
            jax.ShapeDtypeStruct((slots, width), BF16),
            jax.ShapeDtypeStruct((1,), jnp.int32),
        ),
        in_specs=[SMEM] + [VMEM] * len(ids) + [VMEM if resident else HBM] * 2,
        out_specs=(VMEM, SMEM),
        scratch_shapes=[]
        if resident
        else [pltpu.VMEM((rows, width), BF16)] * 2 + [pltpu.SemaphoreType.DMA((2,))],
        compiler_params=params(16),
        name="lookup",
    )(place, *ids, *tables)


def plan_kernel(place_ref, *refs, size, slots, table_rows):
    *ids_refs, pick_ref = refs
    me, turn = place_ref[0], place_ref[1]
    pair, key, _ = candidates_info(ids_refs, me, size, table_rows)
    count = pair.shape[1]
    key_col = to_column(key)
    pair_col = key_col // count
    before = (key < key_col) & (key >= pair_col * count)
    rank = jnp.sum(before.astype(jnp.int32), axis=1, keepdims=True)
    away = pair_col ^ (me >> 1)
    block = jnp.zeros_like(away)
    for k, b in enumerate(position_bits(size)):
        block = block + jnp.where((away & (b >> 1)) != 0, 1 << k, 0)
    mine = rank - turn * slots
    slot = jnp.where((mine >= 0) & (mine < slots), block * slots + mine, -1)
    pick = slot == lax.broadcasted_iota(jnp.int32, pick_ref.shape, 1)
    pick_ref[...] = pick.astype(F32).astype(BF16)


def plan(place, ids, slots, table_rows, size):
    count = sum(i.shape[1] for i in ids)
    return pl.pallas_call(
        functools.partial(plan_kernel, size=size, slots=slots, table_rows=table_rows),
        out_shape=jax.ShapeDtypeStruct((count, size // 2 * slots), BF16),
        in_specs=[SMEM] + [VMEM] * len(ids),
        out_specs=VMEM,
        compiler_params=params(16),
        name="plan",
    )(place, *ids)


def select_kernel(pick_ref, rows_ref, out_ref):
    out_ref[...] = jnp.dot(pick_ref[...], rows_ref[...], preferred_element_type=F32).astype(BF16)


def select(pick, pieces):
    rows = jnp.concatenate(pieces, axis=0)
    return pl.pallas_call(
        select_kernel,
        out_shape=jax.ShapeDtypeStruct((pick.shape[0], rows.shape[1]), BF16),
        in_specs=[VMEM, VMEM],
        out_specs=VMEM,
        compiler_params=params(32),
        name="select",
    )(pick, rows)


def three_parts(x):
    high = x.astype(BF16)
    rest = x - high.astype(F32)
    middle = rest.astype(BF16)
    return [high, middle, (rest - middle.astype(F32)).astype(BF16)]


def prepare_kernel(
    place_ref, start_ref, times_hbm, time_bias_hbm, pos_bias_hbm, table_hbm, out_ref, table_ref,
    times_ref, time_bias_ref, pos_bias_ref, sems, *, npos, history
):
    pairs = ((times_hbm, times_ref), (time_bias_hbm, time_bias_ref), (pos_bias_hbm, pos_bias_ref), (table_hbm, table_ref))
    copies = [pltpu.make_async_copy(a, b, sems.at[k]) for k, (a, b) in enumerate(pairs)]
    for c in copies:
        c.start()
    events = times_ref.shape[1]
    first = history - start_ref[0] - place_ref[0] * events
    distance = first - lax.broadcasted_iota(jnp.int32, (1, events), 1)
    bucket = jnp.zeros((1, events), jnp.int32)
    for k in range(1, npos):
        bucket = bucket + (distance >= (1 << k)).astype(jnp.int32)
    for c in copies[:3]:
        c.wait()
    columns = []
    for table_ref_, index in ((time_bias_ref, times_ref[...]), (pos_bias_ref, bucket)):
        table = jnp.concatenate(three_parts(table_ref_[...] * 0.5), axis=0)
        kinds = table.shape[1]
        hot = lax.broadcasted_iota(jnp.int32, (kinds, events), 0) == index
        columns.append(jnp.dot(table, hot.astype(F32).astype(BF16), preferred_element_type=F32))
    used = sum(c.shape[0] for c in columns)
    columns.append(jnp.zeros((LANES - used, events), F32))
    out_ref[...] = jnp.concatenate(columns, axis=0).T.astype(BF16)
    copies[3].wait()


def prepare(place, start, times, time_bias, pos_bias, table, history):
    arrays = [times, time_bias, pos_bias, table]
    return pl.pallas_call(
        functools.partial(prepare_kernel, npos=pos_bias.shape[1], history=history),
        out_shape=(
            jax.ShapeDtypeStruct((times.shape[1], LANES), BF16),
            jax.ShapeDtypeStruct(table.shape, BF16),
        ),
        in_specs=[SMEM, SMEM] + [HBM] * 4,
        out_specs=(VMEM, VMEM),
        scratch_shapes=[pltpu.VMEM(a.shape, a.dtype) for a in arrays[:3]] + [pltpu.SemaphoreType.DMA((4,))],
        compiler_params=params(8),
        name="prepare",
    )(place, start, *(pltpu.with_memory_space_constraint(a, pltpu.HBM) for a in arrays))


def silu(x):
    return x / (1.0 + jnp.exp(-x))


def normalise(embedded, gain):
    x = embedded.astype(F32)
    meansq = jnp.mean(x * x, axis=-1, keepdims=True)
    return (x * lax.rsqrt(meansq + 1e-06) * gain).astype(BF16)


def attend_kernel(rounds_ref, pick_ref, *refs, heads, blocks):
    *row_refs, extra_hbm, gain_ref, proj_ref = refs[: -6 - 3 * blocks]
    caches = refs[-6 - 3 * blocks : -6]
    own_ref, keep_ref, send_ref, emb_ref, query_ref, sem = refs[-6:]
    count, width = emb_ref.shape
    rows = jnp.concatenate([r[...] for r in row_refs], axis=0)
    emb_ref[...] = jnp.dot(pick_ref[...], rows, preferred_element_type=F32).astype(BF16)

    @pl.when(rounds_ref[0] > 1)
    def _():
        extra = pltpu.make_async_copy(extra_hbm, query_ref, sem)
        extra.start()
        extra.wait()
        emb_ref[...] = emb_ref[...] + query_ref[...]

    own_ref[...] = emb_ref[: own_ref.shape[0], :]
    head_dim = width // heads
    half = count // 2
    rows = min(ROWS_AT_ONCE, count)
    per = LANES // head_dim
    for first in range(0, count, rows):
        normed = normalise(emb_ref[first : first + rows, :], gain_ref[...])
        projected = jnp.dot(normed, proj_ref[...], preferred_element_type=F32)
        query = silu(projected).astype(BF16)
        query_ref[first : first + rows, :] = query * jnp.asarray(0.5 * head_dim**-0.5, BF16)
        lane = lax.broadcasted_iota(jnp.int32, (rows, LANES), 1)
        for group in range(heads // per):
            at = slice(group * LANES, (group + 1) * LANES)
            part = query_ref[first : first + rows, at]
            zero, one = jnp.zeros_like(part), jnp.ones_like(part)
            stacked = []
            for k in range(per):
                own = jnp.where(lane // head_dim == k, part, zero)
                chosen = jnp.where(lane % heads == group * per + k, one, zero)
                stacked.append(jnp.concatenate([own, chosen], axis=1))
            left = jnp.concatenate(stacked, axis=0)
            total = jnp.zeros((per * rows, LANES), F32)
            for key_ref, value_ref, bias_ref in zip(*(caches[k * blocks : (k + 1) * blocks] for k in range(3))):
                step = min(EVENTS_AT_ONCE, key_ref.shape[0])
                for j in range(0, key_ref.shape[0], step):
                    right = jnp.concatenate([key_ref[j : j + step, at], bias_ref[j : j + step, :]], axis=1)
                    t = lax.dot_general(left, right, NT, preferred_element_type=F32)
                    weights = (t + t * jnp.tanh(t)).astype(BF16)
                    total = total + jnp.dot(weights, value_ref[j : j + step, at], preferred_element_type=F32)
            out = total[:rows]
            for k in range(1, per):
                out = jnp.where(lane // head_dim == k, total[k * rows : (k + 1) * rows], out)
            if first + rows <= half:
                keep_ref[first : first + rows, at] = out
            elif first >= half:
                send_ref[first - half : first - half + rows, at] = out.astype(BF16)
            else:
                keep_ref[first:half, at] = out[: half - first]
                send_ref[: first + rows - half, at] = out[half - first :].astype(BF16)


def attend(rounds, pick, pieces, extra, gain, proj, keys, values, biases, heads, each):
    count, width = extra.shape
    blocks = len(keys)
    return pl.pallas_call(
        functools.partial(attend_kernel, heads=heads, blocks=blocks),
        out_shape=(
            jax.ShapeDtypeStruct((each, width), BF16),
            jax.ShapeDtypeStruct((count // 2, width), F32),
            jax.ShapeDtypeStruct((count // 2, width), BF16),
        ),
        in_specs=[SMEM, VMEM] + [VMEM] * len(pieces) + [HBM] + [VMEM] * (2 + 3 * blocks),
        out_specs=(VMEM, VMEM, VMEM),
        scratch_shapes=[
            pltpu.VMEM((count, width), BF16),
            pltpu.VMEM((count, width), BF16),
            pltpu.SemaphoreType.DMA,
        ],
        compiler_params=params(24),
        cost_estimate=pl.CostEstimate(
            flops=8 * count * width * blocks * keys[0].shape[0],
            transcendentals=count * heads * blocks * keys[0].shape[0],
            bytes_accessed=4 * blocks * keys[0].size,
        ),
        name="attend",
    )(rounds, pick, *pieces, extra, gain, proj, *keys, *values, *biases)


def stage_kernel(*refs, width):
    *refs, sems = refs
    count = len(refs) // 2
    copies = [
        pltpu.make_async_copy(
            a if a.shape[1] == width else a.at[:, pl.ds(0, width)], b, sems.at[k]
        )
        for k, (a, b) in enumerate(zip(refs[:count], refs[count:]))
    ]
    for c in copies:
        c.start()
    for c in copies:
        c.wait()


def stage(width, *arrays):
    return pl.pallas_call(
        functools.partial(stage_kernel, width=width),
        out_shape=tuple(jax.ShapeDtypeStruct((a.shape[0], width), BF16) for a in arrays),
        in_specs=[HBM] * len(arrays),
        out_specs=(VMEM,) * len(arrays),
        scratch_shapes=[pltpu.SemaphoreType.DMA((len(arrays),))],
        compiler_params=params(4),
        name="stage",
    )(*(pltpu.with_memory_space_constraint(a, pltpu.HBM) for a in arrays))


def gates_kernel(emb_ref, gain_ref, proj_ref, out_ref):
    normed = normalise(emb_ref[...], gain_ref[...])
    projected = jnp.dot(normed, proj_ref[...], preferred_element_type=F32)
    out_ref[...] = silu(projected).astype(BF16)


def gates_of(embedded, gain, proj_in):
    return pl.pallas_call(
        gates_kernel,
        out_shape=jax.ShapeDtypeStruct(embedded.shape, BF16),
        grid=(1,),
        in_specs=[VMEM, VMEM, pl.BlockSpec(proj_in.shape[:1] * 2, lambda i: (0, 1))],
        out_specs=VMEM,
        compiler_params=params(16),
        cost_estimate=pl.CostEstimate(flops=1 << 26, transcendentals=1 << 14, bytes_accessed=1 << 22),
        name="gates",
    )(embedded, gain, proj_in)


def finish_kernel(own_ref, *refs):
    *parts, emb_ref, gates_ref, gain_ref, proj_ref, out_ref = refs
    attended = own_ref[...]
    for p in parts:
        attended = attended + p[...].astype(F32)
    centred = attended - jnp.mean(attended, axis=-1, keepdims=True)
    variance = jnp.mean(centred * centred, axis=-1, keepdims=True)
    gated = centred * lax.rsqrt(variance + 1e-05) * gain_ref[...] * gates_ref[...].astype(F32)
    product = jnp.dot(gated.astype(BF16), proj_ref[...], preferred_element_type=F32)
    out_ref[...] = (emb_ref[...].astype(F32) + product).astype(BF16)


def finish(own, parts, embedded, gates, gain, proj_out):
    return pl.pallas_call(
        finish_kernel,
        out_shape=jax.ShapeDtypeStruct(embedded.shape, BF16),
        in_specs=[VMEM] * (len(parts) + 5),
        out_specs=VMEM,
        compiler_params=params(16),
        name="finish",
    )(own, *parts, embedded, gates, gain, proj_out)


def on_device(
    item_ids,
    item_table,
    key_cache,
    value_cache,
    time_buckets,
    window_start,
    norm_gain,
    proj_in,
    time_bias,
    pos_bias,
    out_gain,
    proj_out,
):
    axis = "hist"
    size = lax.axis_size(axis)
    me = lax.axis_index(axis).astype(jnp.int32)
    each = item_ids.shape[0]
    slots = 2 * each
    heads = time_bias.shape[0]
    events, width = key_cache.shape
    table_rows = item_table.shape[0]
    gain = norm_gain[None, :]

    def place(turn):
        return jnp.stack([me, jnp.asarray(turn, jnp.int32)])

    def partners(x):
        return swap(x, PARTNER, axis, size)

    here = place(0)
    other_table = partners(item_table)
    other_keys = partners(key_cache)
    other_values = partners(value_cache)
    bias, own_table = prepare(
        here, window_start, time_buckets[None, :], time_bias, pos_bias, item_table, 2 * events * size
    )
    other_bias = partners(bias)
    ids = gather_relative(item_ids[None, :], 1, axis, size)

    found, rounds = lookup(here, ids, [own_table, other_table], slots, size, True)
    pieces = gather_relative(found, 0, axis, size)
    pick = plan(here, ids, slots, table_rows, size)

    def more(state):
        turn, so_far = state
        picked = plan(place(turn), ids, slots, table_rows, size)
        found, _ = lookup(place(turn), ids, [item_table, other_table], slots, size, False)
        return turn + 1, so_far + select(picked, gather_relative(found, 0, axis, size))

    none = jnp.zeros((each * (size // 2), width), BF16)
    _, extra = lax.while_loop(lambda s: s[0] < rounds[0], more, (jnp.int32(1), none))

    proj, keys, values = stage(width, proj_in, key_cache, value_cache)
    other_keys, other_values = stage(width, other_keys, other_values)
    own, keep, send = attend(
        rounds, pick, pieces, extra, gain, proj, [keys, other_keys], [values, other_values], [bias, other_bias], heads, each
    )
    gates = gates_of(own, gain, proj_in)

    *far, near = stage_masks(size)
    total = keep + swap(send, near[0], axis, size).astype(F32)
    for bits in far[::-1]:
        masks = combos(bits)
        block = total.shape[0] // len(masks)
        parts = [
            swap(total[k * block : (k + 1) * block].astype(BF16), m, axis, size)
            for k, m in enumerate(masks)
            if k
        ]
        if bits is far[0]:
            break
        total = sum([p.astype(F32) for p in parts], total[:block])
    return finish(total[:block], parts, own, gates, out_gain[None, :], proj_out)


def solution(mesh):
    placed = (
        P(("grp", "hist")),
        P("hist", None),
        P(("grp", "hist"), None),
        P(("grp", "hist"), None),
        P(("grp", "hist")),
        P("grp"),
        P(),
        P(),
        P(),
        P(),
        P(),
        P(),
    )

    return jax.shard_map(on_device, mesh=mesh, in_specs=placed, out_specs=P(("grp", "hist"), None), check_vma=False)
```

```python
import functools

import jax
import jax.numpy as jnp
from jax import lax
from jax.experimental import pallas as pl
from jax.experimental.pallas import tpu as pltpu
from jax.sharding import PartitionSpec as P


BF16 = jnp.bfloat16
F32 = jnp.float32
LANES = 128
ROWS_AT_ONCE = 256
EVENTS_AT_ONCE = 1024
NT = (((1,), (1,)), ((), ()))
VMEM = pl.BlockSpec(memory_space=pltpu.VMEM)
SMEM = pl.BlockSpec(memory_space=pltpu.SMEM)
HBM = pl.BlockSpec(memory_space=pltpu.HBM)


def params(mib):
    return pltpu.CompilerParams(vmem_limit_bytes=mib << 20)


PARTNER = 1


def stage_masks(size):
    bits = [1 << k for k in range(1, size.bit_length() - 1)][::-1]
    far = bits[:-1]
    return [sorted(far[k : k + 2]) for k in range(0, len(far), 2)] + [bits[-1:]]


def combos(bits):
    out = [0]
    for b in bits:
        out = out + [m | b for m in out]
    return out


def swap(x, mask, axis, size):
    return lax.ppermute(x, axis, [(i, i ^ mask) for i in range(size)])


def join_kernel(*refs):
    *parts, out_ref = refs
    rows = parts[0].shape[0]
    for k, p in enumerate(parts):
        out_ref[k * rows : (k + 1) * rows, :] = p[...]


def join(pieces, dim):
    if dim:
        return jnp.concatenate(pieces, axis=dim)
    rows, width = pieces[0].shape
    return pl.pallas_call(
        join_kernel,
        out_shape=jax.ShapeDtypeStruct((len(pieces) * rows, width), BF16),
        in_specs=[VMEM] * len(pieces),
        out_specs=VMEM,
        compiler_params=params(16),
        name="join",
    )(*pieces)


def gather_relative(x, dim, axis, size):
    *far, near = stage_masks(size)
    for bits in far:
        x = join([x] + [swap(x, m, axis, size) for m in combos(bits)[1:]], dim)
    return [x, swap(x, near[0], axis, size)]


def gather_rows(x, axis, size):
    *far, near = stage_masks(size)
    for bits in far[:-1]:
        x = join([x] + [swap(x, m, axis, size) for m in combos(bits)[1:]], 0)
    first, *rest = combos(far[-1])[1:]
    pieces = [x, swap(x, first, axis, size), join([swap(x, m, axis, size) for m in rest], 0)]
    return pieces + [swap(p, near[0], axis, size) for p in pieces]


def position_bits(size):
    return [b for stage in stage_masks(size) for b in stage]


def candidates_info(ids_refs, me, size, table_rows):
    ids = jnp.concatenate([r[...] for r in ids_refs], axis=1)
    count = ids.shape[1]
    each = count // (size // 2)
    owner = ids // table_rows
    place = lax.broadcasted_iota(jnp.int32, (1, count), 1)
    block = place // each
    mask = jnp.zeros_like(place)
    for k, b in enumerate(position_bits(size)):
        mask = mask + ((block >> k) & 1) * b
    pair = owner >> 1
    key = pair * count + ((mask ^ me) >> 1) * each + place % each
    return pair, key, ids - owner * table_rows + ((owner ^ me) & 1) * table_rows


def to_column(row):
    count = row.shape[1]
    r = lax.broadcasted_iota(jnp.int32, (count, count), 0)
    c = lax.broadcasted_iota(jnp.int32, (count, count), 1)
    return jnp.sum(jnp.where(r == c, row, 0), axis=1, keepdims=True)


def lookup_kernel(place_ref, *refs, size, resident):
    if resident:
        *ids_refs, own_ref, other_ref, out_ref, rounds_ref = refs
        copies = []
    else:
        *ids_refs, own_hbm, other_hbm, out_ref, rounds_ref, own_ref, other_ref, sems = refs
        copies = [
            pltpu.make_async_copy(own_hbm, own_ref, sems.at[0]),
            pltpu.make_async_copy(other_hbm, other_ref, sems.at[1]),
        ]
    for c in copies:
        c.start()
    me, turn = place_ref[0], place_ref[1]
    slots = out_ref.shape[0]
    rows = own_ref.shape[0]
    pair, key, offset = candidates_info(ids_refs, me, size, rows)
    count = pair.shape[1]
    key_col = to_column(key)
    before = (key_col < key) & (key_col >= pair * count)
    rank = jnp.sum(before.astype(jnp.int32), axis=0, keepdims=True)
    slot = lax.broadcasted_iota(jnp.int32, (slots, count), 0) + turn * slots
    hit = (pair == (me >> 1)) & (rank == slot)
    want = jnp.sum(jnp.where(hit, offset + 1, 0), axis=1, keepdims=True) - 1
    row = lax.broadcasted_iota(jnp.int32, (slots, rows), 1)
    rounds_ref[0] = jnp.max(rank) // slots + 1
    for c in copies:
        c.wait()
    found = jnp.dot((want == row).astype(F32).astype(BF16), own_ref[...], preferred_element_type=F32)
    other = (want == row + rows).astype(F32).astype(BF16)
    out_ref[...] = (found + jnp.dot(other, other_ref[...], preferred_element_type=F32)).astype(BF16)


def lookup(place, ids, tables, slots, size, resident):
    if not resident:
        tables = [pltpu.with_memory_space_constraint(t, pltpu.HBM) for t in tables]
    rows, width = tables[0].shape
    return pl.pallas_call(
        functools.partial(lookup_kernel, size=size, resident=resident),
        out_shape=(
            jax.ShapeDtypeStruct((slots, width), BF16),
            jax.ShapeDtypeStruct((1,), jnp.int32),
        ),
        in_specs=[SMEM] + [VMEM] * len(ids) + [VMEM if resident else HBM] * 2,
        out_specs=(VMEM, SMEM),
        scratch_shapes=[]
        if resident
        else [pltpu.VMEM((rows, width), BF16)] * 2 + [pltpu.SemaphoreType.DMA((2,))],
        compiler_params=params(16),
        name="lookup",
    )(place, *ids, *tables)


def plan_kernel(place_ref, *refs, size, slots, table_rows):
    *ids_refs, pick_ref = refs
    me, turn = place_ref[0], place_ref[1]
    pair, key, _ = candidates_info(ids_refs, me, size, table_rows)
    count = pair.shape[1]
    key_col = to_column(key)
    pair_col = key_col // count
    before = (key < key_col) & (key >= pair_col * count)
    rank = jnp.sum(before.astype(jnp.int32), axis=1, keepdims=True)
    away = pair_col ^ (me >> 1)
    block = jnp.zeros_like(away)
    for k, b in enumerate(position_bits(size)):
        block = block + jnp.where((away & (b >> 1)) != 0, 1 << k, 0)
    mine = rank - turn * slots
    slot = jnp.where((mine >= 0) & (mine < slots), block * slots + mine, -1)
    pick = slot == lax.broadcasted_iota(jnp.int32, pick_ref.shape, 1)
    pick_ref[...] = pick.astype(F32).astype(BF16)


def plan(place, ids, slots, table_rows, size):
    count = sum(i.shape[1] for i in ids)
    return pl.pallas_call(
        functools.partial(plan_kernel, size=size, slots=slots, table_rows=table_rows),
        out_shape=jax.ShapeDtypeStruct((count, size // 2 * slots), BF16),
        in_specs=[SMEM] + [VMEM] * len(ids),
        out_specs=VMEM,
        compiler_params=params(16),
        name="plan",
    )(place, *ids)


def select_kernel(pick_ref, rows_ref, out_ref):
    out_ref[...] = jnp.dot(pick_ref[...], rows_ref[...], preferred_element_type=F32).astype(BF16)


def select(pick, pieces):
    rows = jnp.concatenate(pieces, axis=0)
    return pl.pallas_call(
        select_kernel,
        out_shape=jax.ShapeDtypeStruct((pick.shape[0], rows.shape[1]), BF16),
        in_specs=[VMEM, VMEM],
        out_specs=VMEM,
        compiler_params=params(32),
        name="select",
    )(pick, rows)


def three_parts(x):
    high = x.astype(BF16)
    rest = x - high.astype(F32)
    middle = rest.astype(BF16)
    return [high, middle, (rest - middle.astype(F32)).astype(BF16)]


def prepare_kernel(
    place_ref, start_ref, times_hbm, time_bias_hbm, pos_bias_hbm, table_hbm, out_ref, table_ref,
    times_ref, time_bias_ref, pos_bias_ref, sems, *, npos, history
):
    pairs = ((times_hbm, times_ref), (time_bias_hbm, time_bias_ref), (pos_bias_hbm, pos_bias_ref), (table_hbm, table_ref))
    copies = [pltpu.make_async_copy(a, b, sems.at[k]) for k, (a, b) in enumerate(pairs)]
    for c in copies:
        c.start()
    events = times_ref.shape[1]
    first = history - start_ref[0] - place_ref[0] * events
    distance = first - lax.broadcasted_iota(jnp.int32, (1, events), 1)
    bucket = jnp.zeros((1, events), jnp.int32)
    for k in range(1, npos):
        bucket = bucket + (distance >= (1 << k)).astype(jnp.int32)
    for c in copies[:3]:
        c.wait()
    columns = []
    for table_ref_, index in ((time_bias_ref, times_ref[...]), (pos_bias_ref, bucket)):
        table = jnp.concatenate(three_parts(table_ref_[...] * 0.5), axis=0)
        kinds = table.shape[1]
        hot = lax.broadcasted_iota(jnp.int32, (kinds, events), 0) == index
        columns.append(jnp.dot(table, hot.astype(F32).astype(BF16), preferred_element_type=F32))
    used = sum(c.shape[0] for c in columns)
    columns.append(jnp.zeros((LANES - used, events), F32))
    out_ref[...] = jnp.concatenate(columns, axis=0).T.astype(BF16)
    copies[3].wait()


def prepare(place, start, times, time_bias, pos_bias, table, history):
    arrays = [times, time_bias, pos_bias, table]
    return pl.pallas_call(
        functools.partial(prepare_kernel, npos=pos_bias.shape[1], history=history),
        out_shape=(
            jax.ShapeDtypeStruct((times.shape[1], LANES), BF16),
            jax.ShapeDtypeStruct(table.shape, BF16),
        ),
        in_specs=[SMEM, SMEM] + [HBM] * 4,
        out_specs=(VMEM, VMEM),
        scratch_shapes=[pltpu.VMEM(a.shape, a.dtype) for a in arrays[:3]] + [pltpu.SemaphoreType.DMA((4,))],
        compiler_params=params(8),
        name="prepare",
    )(place, start, *(pltpu.with_memory_space_constraint(a, pltpu.HBM) for a in arrays))


def silu(x):
    return x / (1.0 + jnp.exp(-x))


def normalise(embedded, gain):
    x = embedded.astype(F32)
    meansq = jnp.mean(x * x, axis=-1, keepdims=True)
    return (x * lax.rsqrt(meansq + 1e-06) * gain).astype(BF16)


def attend_kernel(rounds_ref, pick_ref, *refs, heads, blocks):
    last = 5 * blocks + 7
    *row_refs, extra_hbm, gain_ref, proj_ref = refs[:-last]
    refs = refs[-last:]
    *caches, own_ref, keep_ref, send_ref, emb_ref, query_ref, sem = refs[: -1 - 2 * blocks]
    chip = refs[-1 - 2 * blocks : -1]
    sems = refs[-1]
    count, width = emb_ref.shape
    groups = width // LANES
    copies = [
        [
            pltpu.make_async_copy(a.at[:, pl.ds(g * LANES, LANES)], b.at[:, pl.ds(g * LANES, LANES)], sems.at[g, k])
            for k, (a, b) in enumerate(zip(caches[: 2 * blocks], chip))
        ]
        for g in range(groups)
    ]
    for group in copies:
        for c in group:
            c.start()
    key_refs, value_refs, bias_refs = chip[:blocks], chip[blocks:], caches[2 * blocks :]
    rows = jnp.concatenate([r[...] for r in row_refs], axis=0)
    emb_ref[...] = jnp.dot(pick_ref[...], rows, preferred_element_type=F32).astype(BF16)

    @pl.when(rounds_ref[0] > 1)
    def _():
        extra = pltpu.make_async_copy(extra_hbm, query_ref, sem)
        extra.start()
        extra.wait()
        emb_ref[...] = emb_ref[...] + query_ref[...]

    own_ref[...] = emb_ref[: own_ref.shape[0], :]
    head_dim = width // heads
    half = count // 2
    rows = min(ROWS_AT_ONCE, count)
    per = LANES // head_dim
    for first in range(0, count, rows):
        normed = normalise(emb_ref[first : first + rows, :], gain_ref[...])
        projected = jnp.dot(normed, proj_ref[...], preferred_element_type=F32)
        query = silu(projected).astype(BF16)
        query_ref[first : first + rows, :] = query * jnp.asarray(0.5 * head_dim**-0.5, BF16)
        lane = lax.broadcasted_iota(jnp.int32, (rows, LANES), 1)
        for group in range(groups):
            if first == 0:
                for c in copies[group]:
                    c.wait()
            at = slice(group * LANES, (group + 1) * LANES)
            part = query_ref[first : first + rows, at]
            zero, one = jnp.zeros_like(part), jnp.ones_like(part)
            stacked = []
            for k in range(per):
                own = jnp.where(lane // head_dim == k, part, zero)
                chosen = jnp.where(lane % heads == group * per + k, one, zero)
                stacked.append(jnp.concatenate([own, chosen], axis=1))
            left = jnp.concatenate(stacked, axis=0)
            total = jnp.zeros((per * rows, LANES), F32)
            for key_ref, value_ref, bias_ref in zip(key_refs, value_refs, bias_refs):
                step = min(EVENTS_AT_ONCE, key_ref.shape[0])
                for j in range(0, key_ref.shape[0], step):
                    right = jnp.concatenate([key_ref[j : j + step, at], bias_ref[j : j + step, :]], axis=1)
                    t = lax.dot_general(left, right, NT, preferred_element_type=F32)
                    weights = (t + t * jnp.tanh(t)).astype(BF16)
                    total = total + jnp.dot(weights, value_ref[j : j + step, at], preferred_element_type=F32)
            out = total[:rows]
            for k in range(1, per):
                out = jnp.where(lane // head_dim == k, total[k * rows : (k + 1) * rows], out)
            if first + rows <= half:
                keep_ref[first : first + rows, at] = out
            elif first >= half:
                send_ref[first - half : first - half + rows, at] = out.astype(BF16)
            else:
                keep_ref[first:half, at] = out[: half - first]
                send_ref[: first + rows - half, at] = out[half - first :].astype(BF16)


def attend(rounds, pick, pieces, extra, gain, proj, keys, values, biases, heads, each):
    count, width = extra.shape
    blocks = len(keys)
    caches = [pltpu.with_memory_space_constraint(c, pltpu.HBM) for c in [*keys, *values]]
    return pl.pallas_call(
        functools.partial(attend_kernel, heads=heads, blocks=blocks),
        out_shape=(
            jax.ShapeDtypeStruct((each, width), BF16),
            jax.ShapeDtypeStruct((count // 2, width), F32),
            jax.ShapeDtypeStruct((count // 2, width), BF16),
        ),
        in_specs=[SMEM, VMEM] + [VMEM] * len(pieces) + [HBM, VMEM, VMEM] + [HBM] * 2 * blocks + [VMEM] * blocks,
        out_specs=(VMEM, VMEM, VMEM),
        scratch_shapes=[
            pltpu.VMEM((count, width), BF16),
            pltpu.VMEM((count, width), BF16),
            pltpu.SemaphoreType.DMA,
        ]
        + [pltpu.VMEM(c.shape, BF16) for c in caches]
        + [pltpu.SemaphoreType.DMA((width // LANES, len(caches)))],
        compiler_params=params(40),
        cost_estimate=pl.CostEstimate(
            flops=8 * count * width * blocks * keys[0].shape[0],
            transcendentals=count * heads * blocks * keys[0].shape[0],
            bytes_accessed=4 * blocks * keys[0].size,
        ),
        name="attend",
    )(rounds, pick, *pieces, extra, gain, proj, *caches, *biases)


def stage_kernel(*refs, width):
    *refs, sems = refs
    count = len(refs) // 2
    copies = [
        pltpu.make_async_copy(
            a if a.shape[1] == width else a.at[:, pl.ds(0, width)], b, sems.at[k]
        )
        for k, (a, b) in enumerate(zip(refs[:count], refs[count:]))
    ]
    for c in copies:
        c.start()
    for c in copies:
        c.wait()


def stage(width, *arrays, held=True):
    return pl.pallas_call(
        functools.partial(stage_kernel, width=width),
        out_shape=tuple(jax.ShapeDtypeStruct((a.shape[0], width), BF16) for a in arrays),
        in_specs=[HBM if held else pl.BlockSpec(memory_space=pl.ANY)] * len(arrays),
        out_specs=(VMEM,) * len(arrays),
        scratch_shapes=[pltpu.SemaphoreType.DMA((len(arrays),))],
        compiler_params=params(4),
        name="stage",
    )(*(pltpu.with_memory_space_constraint(a, pltpu.HBM) if held else a for a in arrays))


def gates_kernel(emb_ref, gain_ref, proj_ref, out_ref):
    normed = normalise(emb_ref[...], gain_ref[...])
    projected = jnp.dot(normed, proj_ref[...], preferred_element_type=F32)
    out_ref[...] = silu(projected).astype(BF16)


def gates_of(embedded, gain, proj_in):
    return pl.pallas_call(
        gates_kernel,
        out_shape=jax.ShapeDtypeStruct(embedded.shape, BF16),
        grid=(1,),
        in_specs=[VMEM, VMEM, pl.BlockSpec(proj_in.shape[:1] * 2, lambda i: (0, 1))],
        out_specs=VMEM,
        compiler_params=params(16),
        cost_estimate=pl.CostEstimate(flops=1 << 26, transcendentals=1 << 14, bytes_accessed=1 << 22),
        name="gates",
    )(embedded, gain, proj_in)


def finish_kernel(own_ref, *refs):
    *parts, emb_ref, gates_ref, gain_ref, proj_ref, out_ref = refs
    attended = own_ref[...]
    for p in parts:
        attended = attended + p[...].astype(F32)
    centred = attended - jnp.mean(attended, axis=-1, keepdims=True)
    variance = jnp.mean(centred * centred, axis=-1, keepdims=True)
    gated = centred * lax.rsqrt(variance + 1e-05) * gain_ref[...] * gates_ref[...].astype(F32)
    product = jnp.dot(gated.astype(BF16), proj_ref[...], preferred_element_type=F32)
    out_ref[...] = (emb_ref[...].astype(F32) + product).astype(BF16)


def finish(own, parts, embedded, gates, gain, proj_out):
    return pl.pallas_call(
        finish_kernel,
        out_shape=jax.ShapeDtypeStruct(embedded.shape, BF16),
        in_specs=[VMEM] * (len(parts) + 5),
        out_specs=VMEM,
        compiler_params=params(16),
        name="finish",
    )(own, *parts, embedded, gates, gain, proj_out)


def on_device(
    item_ids,
    item_table,
    key_cache,
    value_cache,
    time_buckets,
    window_start,
    norm_gain,
    proj_in,
    time_bias,
    pos_bias,
    out_gain,
    proj_out,
):
    axis = "hist"
    size = lax.axis_size(axis)
    me = lax.axis_index(axis).astype(jnp.int32)
    each = item_ids.shape[0]
    slots = 2 * each
    heads = time_bias.shape[0]
    events, width = key_cache.shape
    table_rows = item_table.shape[0]
    gain = norm_gain[None, :]

    def place(turn):
        return jnp.stack([me, jnp.asarray(turn, jnp.int32)])

    def partners(x):
        return swap(x, PARTNER, axis, size)

    here = place(0)
    other_table = partners(item_table)
    other_keys = partners(key_cache)
    other_values = partners(value_cache)
    bias, own_table = prepare(
        here, window_start, time_buckets[None, :], time_bias, pos_bias, item_table, 2 * events * size
    )
    other_bias = partners(bias)
    ids = gather_relative(item_ids[None, :], 1, axis, size)

    (near_table,) = stage(width, other_table, held=False)
    found, rounds = lookup(here, ids, [own_table, near_table], slots, size, True)
    pieces = gather_rows(found, axis, size)
    pick = plan(here, ids, slots, table_rows, size)

    def more(state):
        turn, so_far = state
        picked = plan(place(turn), ids, slots, table_rows, size)
        found, _ = lookup(place(turn), ids, [item_table, other_table], slots, size, False)
        return turn + 1, so_far + select(picked, gather_rows(found, axis, size))

    none = jnp.zeros((each * (size // 2), width), BF16)
    _, extra = lax.while_loop(lambda s: s[0] < rounds[0], more, (jnp.int32(1), none))

    (proj,) = stage(width, proj_in)
    own, keep, send = attend(
        rounds,
        pick,
        pieces,
        extra,
        gain,
        proj,
        [key_cache, other_keys],
        [value_cache, other_values],
        [bias, other_bias],
        heads,
        each,
    )
    gates = gates_of(own, gain, proj_in)

    *far, near = stage_masks(size)
    total = keep + swap(send, near[0], axis, size).astype(F32)
    for bits in far[::-1]:
        masks = combos(bits)
        block = total.shape[0] // len(masks)
        parts = [
            swap(total[k * block : (k + 1) * block].astype(BF16), m, axis, size)
            for k, m in enumerate(masks)
            if k
        ]
        if bits is far[0]:
            break
        total = sum([p.astype(F32) for p in parts], total[:block])
    return finish(total[:block], parts, own, gates, out_gain[None, :], proj_out)


def solution(mesh):
    placed = (
        P(("grp", "hist")),
        P("hist", None),
        P(("grp", "hist"), None),
        P(("grp", "hist"), None),
        P(("grp", "hist")),
        P("grp"),
        P(),
        P(),
        P(),
        P(),
        P(),
        P(),
    )

    return jax.shard_map(on_device, mesh=mesh, in_specs=placed, out_specs=P(("grp", "hist"), None), check_vma=False)
```

```python
import functools

import jax
import jax.numpy as jnp
from jax import lax
from jax.experimental import pallas as pl
from jax.experimental.pallas import tpu as pltpu
from jax.sharding import PartitionSpec as P


BF16 = jnp.bfloat16
F32 = jnp.float32
LANES = 128
ROWS_AT_ONCE = 256
EVENTS_AT_ONCE = 1024
NT = (((1,), (1,)), ((), ()))
VMEM = pl.BlockSpec(memory_space=pltpu.VMEM)
SMEM = pl.BlockSpec(memory_space=pltpu.SMEM)
HBM = pl.BlockSpec(memory_space=pltpu.HBM)


def params(mib):
    return pltpu.CompilerParams(vmem_limit_bytes=mib << 20)


PARTNER = 1


def stage_masks(size):
    bits = [1 << k for k in range(1, size.bit_length() - 1)][::-1]
    far = bits[:-1]
    return [sorted(far[k : k + 2]) for k in range(0, len(far), 2)] + [bits[-1:]]


def combos(bits):
    out = [0]
    for b in bits:
        out = out + [m | b for m in out]
    return out


def swap(x, mask, axis, size):
    return lax.ppermute(x, axis, [(i, i ^ mask) for i in range(size)])


def join_kernel(*refs):
    *parts, out_ref = refs
    rows = parts[0].shape[0]
    for k, p in enumerate(parts):
        out_ref[k * rows : (k + 1) * rows, :] = p[...]


def join(pieces, dim):
    if dim:
        return jnp.concatenate(pieces, axis=dim)
    rows, width = pieces[0].shape
    return pl.pallas_call(
        join_kernel,
        out_shape=jax.ShapeDtypeStruct((len(pieces) * rows, width), BF16),
        in_specs=[VMEM] * len(pieces),
        out_specs=VMEM,
        compiler_params=params(16),
        name="join",
    )(*pieces)


def gather_relative(x, dim, axis, size):
    *far, near = stage_masks(size)
    for bits in far:
        x = join([x] + [swap(x, m, axis, size) for m in combos(bits)[1:]], dim)
    return [x, swap(x, near[0], axis, size)]


def gather_rows(x, axis, size):
    *far, near = stage_masks(size)
    for bits in far[:-1]:
        x = join([x] + [swap(x, m, axis, size) for m in combos(bits)[1:]], 0)
    pieces = [x, join([swap(x, m, axis, size) for m in combos(far[-1])[1:]], 0)]
    return pieces + [swap(p, near[0], axis, size) for p in pieces]


def position_bits(size):
    return [b for stage in stage_masks(size) for b in stage]


def candidates_info(ids_refs, me, size, table_rows):
    ids = jnp.concatenate([r[...] for r in ids_refs], axis=1)
    count = ids.shape[1]
    each = count // (size // 2)
    owner = ids // table_rows
    place = lax.broadcasted_iota(jnp.int32, (1, count), 1)
    block = place // each
    mask = jnp.zeros_like(place)
    for k, b in enumerate(position_bits(size)):
        mask = mask + ((block >> k) & 1) * b
    pair = owner >> 1
    key = pair * count + ((mask ^ me) >> 1) * each + place % each
    return pair, key, ids - owner * table_rows + ((owner ^ me) & 1) * table_rows


def to_column(row):
    count = row.shape[1]
    r = lax.broadcasted_iota(jnp.int32, (count, count), 0)
    c = lax.broadcasted_iota(jnp.int32, (count, count), 1)
    return jnp.sum(jnp.where(r == c, row, 0), axis=1, keepdims=True)


def lookup_kernel(place_ref, *refs, size, resident):
    if resident:
        *ids_refs, own_ref, other_ref, out_ref, rounds_ref = refs
        copies = []
    else:
        *ids_refs, own_hbm, other_hbm, out_ref, rounds_ref, own_ref, other_ref, sems = refs
        copies = [
            pltpu.make_async_copy(own_hbm, own_ref, sems.at[0]),
            pltpu.make_async_copy(other_hbm, other_ref, sems.at[1]),
        ]
    for c in copies:
        c.start()
    me, turn = place_ref[0], place_ref[1]
    slots = out_ref.shape[0]
    rows = own_ref.shape[0]
    pair, key, offset = candidates_info(ids_refs, me, size, rows)
    count = pair.shape[1]
    key_col = to_column(key)
    before = (key_col < key) & (key_col >= pair * count)
    rank = jnp.sum(before.astype(jnp.int32), axis=0, keepdims=True)
    slot = lax.broadcasted_iota(jnp.int32, (slots, count), 0) + turn * slots
    hit = (pair == (me >> 1)) & (rank == slot)
    want = jnp.sum(jnp.where(hit, offset + 1, 0), axis=1, keepdims=True) - 1
    row = lax.broadcasted_iota(jnp.int32, (slots, rows), 1)
    rounds_ref[0] = jnp.max(rank) // slots + 1
    for c in copies:
        c.wait()
    found = jnp.dot((want == row).astype(F32).astype(BF16), own_ref[...], preferred_element_type=F32)
    other = (want == row + rows).astype(F32).astype(BF16)
    out_ref[...] = (found + jnp.dot(other, other_ref[...], preferred_element_type=F32)).astype(BF16)


def lookup(place, ids, tables, slots, size, resident):
    if not resident:
        tables = [pltpu.with_memory_space_constraint(t, pltpu.HBM) for t in tables]
    rows, width = tables[0].shape
    return pl.pallas_call(
        functools.partial(lookup_kernel, size=size, resident=resident),
        out_shape=(
            jax.ShapeDtypeStruct((slots, width), BF16),
            jax.ShapeDtypeStruct((1,), jnp.int32),
        ),
        in_specs=[SMEM] + [VMEM] * len(ids) + [VMEM if resident else HBM] * 2,
        out_specs=(VMEM, SMEM),
        scratch_shapes=[]
        if resident
        else [pltpu.VMEM((rows, width), BF16)] * 2 + [pltpu.SemaphoreType.DMA((2,))],
        compiler_params=params(16),
        name="lookup",
    )(place, *ids, *tables)


def plan_kernel(place_ref, *refs, size, slots, table_rows):
    *ids_refs, pick_ref = refs
    me, turn = place_ref[0], place_ref[1]
    pair, key, _ = candidates_info(ids_refs, me, size, table_rows)
    count = pair.shape[1]
    key_col = to_column(key)
    pair_col = key_col // count
    before = (key < key_col) & (key >= pair_col * count)
    rank = jnp.sum(before.astype(jnp.int32), axis=1, keepdims=True)
    away = pair_col ^ (me >> 1)
    block = jnp.zeros_like(away)
    for k, b in enumerate(position_bits(size)):
        block = block + jnp.where((away & (b >> 1)) != 0, 1 << k, 0)
    mine = rank - turn * slots
    slot = jnp.where((mine >= 0) & (mine < slots), block * slots + mine, -1)
    pick = slot == lax.broadcasted_iota(jnp.int32, pick_ref.shape, 1)
    pick_ref[...] = pick.astype(F32).astype(BF16)


def plan(place, ids, slots, table_rows, size):
    count = sum(i.shape[1] for i in ids)
    return pl.pallas_call(
        functools.partial(plan_kernel, size=size, slots=slots, table_rows=table_rows),
        out_shape=jax.ShapeDtypeStruct((count, size // 2 * slots), BF16),
        in_specs=[SMEM] + [VMEM] * len(ids),
        out_specs=VMEM,
        compiler_params=params(16),
        name="plan",
    )(place, *ids)


def select_kernel(pick_ref, rows_ref, out_ref):
    out_ref[...] = jnp.dot(pick_ref[...], rows_ref[...], preferred_element_type=F32).astype(BF16)


def select(pick, pieces):
    rows = jnp.concatenate(pieces, axis=0)
    return pl.pallas_call(
        select_kernel,
        out_shape=jax.ShapeDtypeStruct((pick.shape[0], rows.shape[1]), BF16),
        in_specs=[VMEM, VMEM],
        out_specs=VMEM,
        compiler_params=params(12),
        name="select",
    )(pick, rows)


def three_parts(x):
    high = x.astype(BF16)
    rest = x - high.astype(F32)
    middle = rest.astype(BF16)
    return [high, middle, (rest - middle.astype(F32)).astype(BF16)]


def prepare_kernel(
    place_ref, start_ref, times_hbm, time_bias_hbm, pos_bias_hbm, table_hbm, out_ref, table_ref,
    times_ref, time_bias_ref, pos_bias_ref, sems, *, npos, history
):
    pairs = ((times_hbm, times_ref), (time_bias_hbm, time_bias_ref), (pos_bias_hbm, pos_bias_ref), (table_hbm, table_ref))
    copies = [pltpu.make_async_copy(a, b, sems.at[k]) for k, (a, b) in enumerate(pairs)]
    for c in copies:
        c.start()
    events = times_ref.shape[1]
    first = history - start_ref[0] - place_ref[0] * events
    distance = first - lax.broadcasted_iota(jnp.int32, (1, events), 1)
    bucket = jnp.zeros((1, events), jnp.int32)
    for k in range(1, npos):
        bucket = bucket + (distance >= (1 << k)).astype(jnp.int32)
    for c in copies[:3]:
        c.wait()
    columns = []
    for table_ref_, index in ((time_bias_ref, times_ref[...]), (pos_bias_ref, bucket)):
        table = jnp.concatenate(three_parts(table_ref_[...] * 0.5), axis=0)
        kinds = table.shape[1]
        hot = lax.broadcasted_iota(jnp.int32, (kinds, events), 0) == index
        columns.append(jnp.dot(table, hot.astype(F32).astype(BF16), preferred_element_type=F32))
    used = sum(c.shape[0] for c in columns)
    columns.append(jnp.zeros((LANES - used, events), F32))
    out_ref[...] = jnp.concatenate(columns, axis=0).T.astype(BF16)
    copies[3].wait()


def prepare(place, start, times, time_bias, pos_bias, table, history):
    arrays = [times, time_bias, pos_bias, table]
    return pl.pallas_call(
        functools.partial(prepare_kernel, npos=pos_bias.shape[1], history=history),
        out_shape=(
            jax.ShapeDtypeStruct((times.shape[1], LANES), BF16),
            jax.ShapeDtypeStruct(table.shape, BF16),
        ),
        in_specs=[SMEM, SMEM] + [HBM] * 4,
        out_specs=(VMEM, VMEM),
        scratch_shapes=[pltpu.VMEM(a.shape, a.dtype) for a in arrays[:3]] + [pltpu.SemaphoreType.DMA((4,))],
        compiler_params=params(8),
        name="prepare",
    )(place, start, *(pltpu.with_memory_space_constraint(a, pltpu.HBM) for a in arrays))


def silu(x):
    return x / (1.0 + jnp.exp(-x))


def normalise(embedded, gain):
    x = embedded.astype(F32)
    meansq = jnp.mean(x * x, axis=-1, keepdims=True)
    return (x * lax.rsqrt(meansq + 1e-06) * gain).astype(BF16)


def attend_kernel(rounds_ref, pick_ref, *refs, heads, blocks):
    *row_refs, extra_hbm, gain_ref, proj_ref = refs[: -6 - 3 * blocks]
    caches = refs[-6 - 3 * blocks : -6]
    own_ref, keep_ref, send_ref, emb_ref, query_ref, sem = refs[-6:]
    count, width = emb_ref.shape
    rows = jnp.concatenate([r[...] for r in row_refs], axis=0)
    emb_ref[...] = jnp.dot(pick_ref[...], rows, preferred_element_type=F32).astype(BF16)

    @pl.when(rounds_ref[0] > 1)
    def _():
        extra = pltpu.make_async_copy(extra_hbm, query_ref, sem)
        extra.start()
        extra.wait()
        emb_ref[...] = emb_ref[...] + query_ref[...]

    own_ref[...] = emb_ref[: own_ref.shape[0], :]
    head_dim = width // heads
    half = count // 2
    rows = min(ROWS_AT_ONCE, count)
    per = LANES // head_dim
    for first in range(0, count, rows):
        normed = normalise(emb_ref[first : first + rows, :], gain_ref[...])
        projected = jnp.dot(normed, proj_ref[...], preferred_element_type=F32)
        query = silu(projected).astype(BF16)
        query_ref[first : first + rows, :] = query * jnp.asarray(0.5 * head_dim**-0.5, BF16)
        lane = lax.broadcasted_iota(jnp.int32, (rows, LANES), 1)
        for group in range(width // LANES):
            at = slice(group * LANES, (group + 1) * LANES)
            part = query_ref[first : first + rows, at]
            zero, one = jnp.zeros_like(part), jnp.ones_like(part)
            stacked = []
            for k in range(per):
                own = jnp.where(lane // head_dim == k, part, zero)
                chosen = jnp.where(lane % heads == group * per + k, one, zero)
                stacked.append(jnp.concatenate([own, chosen], axis=1))
            left = jnp.concatenate(stacked, axis=0)
            total = jnp.zeros((per * rows, LANES), F32)
            for key_ref, value_ref, bias_ref in zip(*(caches[k * blocks : (k + 1) * blocks] for k in range(3))):
                step = min(EVENTS_AT_ONCE, key_ref.shape[0])
                for j in range(0, key_ref.shape[0], step):
                    right = jnp.concatenate([key_ref[j : j + step, at], bias_ref[j : j + step, :]], axis=1)
                    t = lax.dot_general(left, right, NT, preferred_element_type=F32)
                    weights = (t + t * jnp.tanh(t)).astype(BF16)
                    total = total + jnp.dot(weights, value_ref[j : j + step, at], preferred_element_type=F32)
            out = total[:rows]
            for k in range(1, per):
                out = jnp.where(lane // head_dim == k, total[k * rows : (k + 1) * rows], out)
            if first + rows <= half:
                keep_ref[first : first + rows, at] = out
            elif first >= half:
                send_ref[first - half : first - half + rows, at] = out.astype(BF16)
            else:
                keep_ref[first:half, at] = out[: half - first]
                send_ref[: first + rows - half, at] = out[half - first :].astype(BF16)


def attend(rounds, pick, pieces, extra, gain, proj, keys, values, biases, heads, each):
    count, width = extra.shape
    blocks = len(keys)
    return pl.pallas_call(
        functools.partial(attend_kernel, heads=heads, blocks=blocks),
        out_shape=(
            jax.ShapeDtypeStruct((each, width), BF16),
            jax.ShapeDtypeStruct((count // 2, width), F32),
            jax.ShapeDtypeStruct((count // 2, width), BF16),
        ),
        in_specs=[SMEM, VMEM] + [VMEM] * len(pieces) + [HBM] + [VMEM] * (2 + 3 * blocks),
        out_specs=(VMEM, VMEM, VMEM),
        scratch_shapes=[
            pltpu.VMEM((count, width), BF16),
            pltpu.VMEM((count, width), BF16),
            pltpu.SemaphoreType.DMA,
        ],
        compiler_params=params(20),
        cost_estimate=pl.CostEstimate(
            flops=8 * count * width * blocks * keys[0].shape[0],
            transcendentals=count * heads * blocks * keys[0].shape[0],
            bytes_accessed=4 * blocks * keys[0].size,
        ),
        name="attend",
    )(rounds, pick, *pieces, extra, gain, proj, *keys, *values, *biases)


def stage_kernel(*refs, width):
    *refs, sems = refs
    count = len(refs) // 2
    copies = [
        pltpu.make_async_copy(
            a if a.shape[1] == width else a.at[:, pl.ds(0, width)], b, sems.at[k]
        )
        for k, (a, b) in enumerate(zip(refs[:count], refs[count:]))
    ]
    for c in copies:
        c.start()
    for c in copies:
        c.wait()


def stage(width, *arrays, held=True):
    return pl.pallas_call(
        functools.partial(stage_kernel, width=width),
        out_shape=tuple(jax.ShapeDtypeStruct((a.shape[0], width), BF16) for a in arrays),
        in_specs=[HBM if held else pl.BlockSpec(memory_space=pl.ANY)] * len(arrays),
        out_specs=(VMEM,) * len(arrays),
        scratch_shapes=[pltpu.SemaphoreType.DMA((len(arrays),))],
        compiler_params=params(4),
        name="stage",
    )(*(pltpu.with_memory_space_constraint(a, pltpu.HBM) if held else a for a in arrays))


def gates_kernel(emb_ref, gain_ref, proj_ref, out_ref):
    normed = normalise(emb_ref[...], gain_ref[...])
    projected = jnp.dot(normed, proj_ref[...], preferred_element_type=F32)
    out_ref[...] = silu(projected).astype(BF16)


def gates_of(embedded, gain, proj_in):
    return pl.pallas_call(
        gates_kernel,
        out_shape=jax.ShapeDtypeStruct(embedded.shape, BF16),
        grid=(1,),
        in_specs=[VMEM, VMEM, pl.BlockSpec(proj_in.shape[:1] * 2, lambda i: (0, 1))],
        out_specs=VMEM,
        compiler_params=params(16),
        cost_estimate=pl.CostEstimate(flops=1 << 26, transcendentals=1 << 14, bytes_accessed=1 << 22),
        name="gates",
    )(embedded, gain, proj_in)


def finish_kernel(own_ref, *refs):
    *parts, emb_ref, gates_ref, gain_ref, proj_ref, out_ref = refs
    attended = own_ref[...]
    for p in parts:
        attended = attended + p[...].astype(F32)
    centred = attended - jnp.mean(attended, axis=-1, keepdims=True)
    variance = jnp.mean(centred * centred, axis=-1, keepdims=True)
    gated = centred * lax.rsqrt(variance + 1e-05) * gain_ref[...] * gates_ref[...].astype(F32)
    product = jnp.dot(gated.astype(BF16), proj_ref[...], preferred_element_type=F32)
    out_ref[...] = (emb_ref[...].astype(F32) + product).astype(BF16)


def finish(own, parts, embedded, gates, gain, proj_out):
    return pl.pallas_call(
        finish_kernel,
        out_shape=jax.ShapeDtypeStruct(embedded.shape, BF16),
        in_specs=[VMEM] * (len(parts) + 5),
        out_specs=VMEM,
        compiler_params=params(16),
        name="finish",
    )(own, *parts, embedded, gates, gain, proj_out)


def on_device(
    item_ids,
    item_table,
    key_cache,
    value_cache,
    time_buckets,
    window_start,
    norm_gain,
    proj_in,
    time_bias,
    pos_bias,
    out_gain,
    proj_out,
):
    axis = "hist"
    size = lax.axis_size(axis)
    me = lax.axis_index(axis).astype(jnp.int32)
    each = item_ids.shape[0]
    slots = 2 * each
    heads = time_bias.shape[0]
    events, width = key_cache.shape
    table_rows = item_table.shape[0]
    gain = norm_gain[None, :]

    def place(turn):
        return jnp.stack([me, jnp.asarray(turn, jnp.int32)])

    def partners(x):
        return swap(x, PARTNER, axis, size)

    here = place(0)
    other_table = partners(item_table)
    other_keys = partners(key_cache)
    other_values = partners(value_cache)
    bias, own_table = prepare(
        here, window_start, time_buckets[None, :], time_bias, pos_bias, item_table, 2 * events * size
    )
    other_bias = partners(bias)
    ids = gather_relative(item_ids[None, :], 1, axis, size)

    (near_table,) = stage(width, other_table, held=False)
    found, rounds = lookup(here, ids, [own_table, near_table], slots, size, True)
    pieces = gather_rows(found, axis, size)
    pick = plan(here, ids, slots, table_rows, size)

    def more(state):
        turn, so_far = state
        picked = plan(place(turn), ids, slots, table_rows, size)
        found, _ = lookup(place(turn), ids, [item_table, other_table], slots, size, False)
        return turn + 1, so_far + select(picked, gather_rows(found, axis, size))

    none = jnp.zeros((each * (size // 2), width), BF16)
    _, extra = lax.while_loop(lambda s: s[0] < rounds[0], more, (jnp.int32(1), none))

    keys, values = stage(width, key_cache, value_cache)
    proj, other_keys, other_values = stage(width, proj_in, other_keys, other_values)
    own, keep, send = attend(
        rounds,
        pick,
        pieces,
        extra,
        gain,
        proj,
        [keys, other_keys],
        [values, other_values],
        [bias, other_bias],
        heads,
        each,
    )
    gates = gates_of(own, gain, proj_in)

    *far, near = stage_masks(size)
    total = keep + swap(send, near[0], axis, size).astype(F32)
    for bits in far[::-1]:
        masks = combos(bits)
        block = total.shape[0] // len(masks)
        parts = [
            swap(total[k * block : (k + 1) * block].astype(BF16), m, axis, size)
            for k, m in enumerate(masks)
            if k
        ]
        if bits is far[0]:
            break
        total = sum([p.astype(F32) for p in parts], total[:block])
    return finish(total[:block], parts, own, gates, out_gain[None, :], proj_out)


def solution(mesh):
    placed = (
        P(("grp", "hist")),
        P("hist", None),
        P(("grp", "hist"), None),
        P(("grp", "hist"), None),
        P(("grp", "hist")),
        P("grp"),
        P(),
        P(),
        P(),
        P(),
        P(),
        P(),
    )

    return jax.shard_map(on_device, mesh=mesh, in_specs=placed, out_specs=P(("grp", "hist"), None), check_vma=False)
```

```python
import functools

import jax
import jax.numpy as jnp
from jax import lax
from jax.experimental import pallas as pl
from jax.experimental.pallas import tpu as pltpu
from jax.sharding import PartitionSpec as P


BF16 = jnp.bfloat16
F32 = jnp.float32
LANES = 128
ROWS_AT_ONCE = 128
EVENTS_AT_ONCE = 512
STEPS_AHEAD = 2
BLOCK = 16
TN = (((0,), (0,)), ((), ()))
NT = (((1,), (1,)), ((), ()))
VMEM = pl.BlockSpec(memory_space=pltpu.VMEM)
SMEM = pl.BlockSpec(memory_space=pltpu.SMEM)
HBM = pl.BlockSpec(memory_space=pltpu.HBM)


def params(mib):
    return pltpu.CompilerParams(vmem_limit_bytes=mib << 20)


PARTNER = 1


def stage_masks(size):
    bits = [1 << k for k in range(1, size.bit_length() - 1)][::-1]
    far = bits[:-1]
    return [sorted(far[k : k + 2]) for k in range(0, len(far), 2)] + [bits[-1:]]


def combos(bits):
    out = [0]
    for b in bits:
        out = out + [m | b for m in out]
    return out


def swap(x, mask, axis, size):
    return lax.ppermute(x, axis, [(i, i ^ mask) for i in range(size)])


def join_kernel(*refs):
    *parts, out_ref = refs
    rows = parts[0].shape[0]
    for k, p in enumerate(parts):
        out_ref[k * rows : (k + 1) * rows, :] = p[...]


def join(pieces, dim):
    if dim:
        return jnp.concatenate(pieces, axis=dim)
    rows, width = pieces[0].shape
    return pl.pallas_call(
        join_kernel,
        out_shape=jax.ShapeDtypeStruct((len(pieces) * rows, width), BF16),
        in_specs=[VMEM] * len(pieces),
        out_specs=VMEM,
        compiler_params=params(16),
        name="join",
    )(*pieces)


def gather_relative(x, dim, axis, size):
    *far, near = stage_masks(size)
    for bits in far:
        x = join([x] + [swap(x, m, axis, size) for m in combos(bits)[1:]], dim)
    return [x, swap(x, near[0], axis, size)]


def gather_rows(x, axis, size):
    *far, near = stage_masks(size)
    for bits in far[:-1]:
        x = join([x] + [swap(x, m, axis, size) for m in combos(bits)[1:]], 0)
    pieces = [x, join([swap(x, m, axis, size) for m in combos(far[-1])[1:]], 0)]
    return pieces + [swap(p, near[0], axis, size) for p in pieces]


def position_bits(size):
    return [b for stage in stage_masks(size) for b in stage]


def candidates_info(ids_refs, me, size, table_rows):
    ids = jnp.concatenate([r[...] for r in ids_refs], axis=1)
    count = ids.shape[1]
    each = count // (size // 2)
    owner = ids // table_rows
    place = lax.broadcasted_iota(jnp.int32, (1, count), 1)
    block = place // each
    mask = jnp.zeros_like(place)
    for k, b in enumerate(position_bits(size)):
        mask = mask + ((block >> k) & 1) * b
    pair = owner >> 1
    key = pair * count + ((mask ^ me) >> 1) * each + place % each
    return pair, key, ids - owner * table_rows + ((owner ^ me) & 1) * table_rows


def to_column(row):
    count = row.shape[1]
    r = lax.broadcasted_iota(jnp.int32, (count, count), 0)
    c = lax.broadcasted_iota(jnp.int32, (count, count), 1)
    return jnp.sum(jnp.where(r == c, row, 0), axis=1, keepdims=True)


def lookup_kernel(place_ref, *refs, size, resident):
    if resident:
        *ids_refs, own_ref, other_ref, out_ref, rounds_ref, blocks_ref = refs
        copies = []
    else:
        *ids_refs, own_hbm, other_hbm, out_ref, rounds_ref, blocks_ref, own_ref, other_ref, sems = refs
        copies = [
            pltpu.make_async_copy(own_hbm, own_ref, sems.at[0]),
            pltpu.make_async_copy(other_hbm, other_ref, sems.at[1]),
        ]
    for c in copies:
        c.start()
    me, turn = place_ref[0], place_ref[1]
    slots = out_ref.shape[0]
    rows = own_ref.shape[0]
    pair, key, offset = candidates_info(ids_refs, me, size, rows)
    count = pair.shape[1]
    key_col = to_column(key)
    before = (key_col < key) & (key_col >= pair * count)
    rank = jnp.sum(before.astype(jnp.int32), axis=0, keepdims=True)
    slot = lax.broadcasted_iota(jnp.int32, (slots, count), 0) + turn * slots
    hit = (pair == (me >> 1)) & (rank == slot)
    want = jnp.sum(jnp.where(hit, offset + 1, 0), axis=1, keepdims=True) - 1
    rounds_ref[0] = jnp.max(rank) // slots + 1
    for c in copies:
        c.wait()
    near = jnp.where(want < 0, 0, want // BLOCK)
    for k in range(slots):
        block = near[k, 0]
        in_own = block < rows // BLOCK
        at = pl.multiple_of((block - jnp.where(in_own, 0, rows // BLOCK)) * BLOCK, BLOCK)
        own, other = own_ref[pl.ds(at, BLOCK), :], other_ref[pl.ds(at, BLOCK), :]
        blocks_ref[k * BLOCK : (k + 1) * BLOCK, :] = jnp.where(in_own, own, other)
    column = lax.broadcasted_iota(jnp.int32, (slots, slots * BLOCK), 1)
    line = lax.broadcasted_iota(jnp.int32, (slots, slots * BLOCK), 0)
    pick = (want >= 0) & (column == line * BLOCK + (want - near * BLOCK))
    found = jnp.dot(pick.astype(F32).astype(BF16), blocks_ref[...], preferred_element_type=F32)
    out_ref[...] = found.astype(BF16)


def lookup(place, ids, tables, slots, size, resident):
    if not resident:
        tables = [pltpu.with_memory_space_constraint(t, pltpu.HBM) for t in tables]
    rows, width = tables[0].shape
    return pl.pallas_call(
        functools.partial(lookup_kernel, size=size, resident=resident),
        out_shape=(
            jax.ShapeDtypeStruct((slots, width), BF16),
            jax.ShapeDtypeStruct((1,), jnp.int32),
        ),
        in_specs=[SMEM] + [VMEM] * len(ids) + [VMEM if resident else HBM] * 2,
        out_specs=(VMEM, SMEM),
        scratch_shapes=[pltpu.VMEM((slots * BLOCK, width), BF16)]
        + ([] if resident else [pltpu.VMEM((rows, width), BF16)] * 2 + [pltpu.SemaphoreType.DMA((2,))]),
        compiler_params=params(16),
        name="lookup",
    )(place, *ids, *tables)


def plan_kernel(place_ref, *refs, size, slots, table_rows):
    *ids_refs, pick_ref = refs
    me, turn = place_ref[0], place_ref[1]
    pair, key, _ = candidates_info(ids_refs, me, size, table_rows)
    count = pair.shape[1]
    key_col = to_column(key)
    pair_col = key_col // count
    before = (key < key_col) & (key >= pair_col * count)
    rank = jnp.sum(before.astype(jnp.int32), axis=1, keepdims=True)
    away = pair_col ^ (me >> 1)
    block = jnp.zeros_like(away)
    for k, b in enumerate(position_bits(size)):
        block = block + jnp.where((away & (b >> 1)) != 0, 1 << k, 0)
    mine = rank - turn * slots
    slot = jnp.where((mine >= 0) & (mine < slots), block * slots + mine, -1)
    pick = slot == lax.broadcasted_iota(jnp.int32, pick_ref.shape, 1)
    pick_ref[...] = pick.astype(F32).astype(BF16)


def plan(place, ids, slots, table_rows, size):
    count = sum(i.shape[1] for i in ids)
    return pl.pallas_call(
        functools.partial(plan_kernel, size=size, slots=slots, table_rows=table_rows),
        out_shape=jax.ShapeDtypeStruct((count, size // 2 * slots), BF16),
        in_specs=[SMEM] + [VMEM] * len(ids),
        out_specs=VMEM,
        compiler_params=params(16),
        name="plan",
    )(place, *ids)


def select_kernel(pick_ref, rows_ref, out_ref):
    out_ref[...] = jnp.dot(pick_ref[...], rows_ref[...], preferred_element_type=F32).astype(BF16)


def select(pick, pieces):
    rows = jnp.concatenate(pieces, axis=0)
    return pl.pallas_call(
        select_kernel,
        out_shape=jax.ShapeDtypeStruct((pick.shape[0], rows.shape[1]), BF16),
        in_specs=[VMEM, VMEM],
        out_specs=VMEM,
        compiler_params=params(12),
        name="select",
    )(pick, rows)


def three_parts(x):
    high = x.astype(BF16)
    rest = x - high.astype(F32)
    middle = rest.astype(BF16)
    return [high, middle, (rest - middle.astype(F32)).astype(BF16)]


def prepare_kernel(
    place_ref, start_ref, times_hbm, time_bias_hbm, pos_bias_hbm, table_hbm, out_ref, table_ref,
    times_ref, time_bias_ref, pos_bias_ref, sems, *, npos, history
):
    pairs = ((times_hbm, times_ref), (time_bias_hbm, time_bias_ref), (pos_bias_hbm, pos_bias_ref), (table_hbm, table_ref))
    copies = [pltpu.make_async_copy(a, b, sems.at[k]) for k, (a, b) in enumerate(pairs)]
    for c in copies:
        c.start()
    events = times_ref.shape[1]
    first = history - start_ref[0] - place_ref[0] * events
    distance = first - lax.broadcasted_iota(jnp.int32, (1, events), 1)
    bucket = jnp.zeros((1, events), jnp.int32)
    for k in range(1, npos):
        bucket = bucket + (distance >= (1 << k)).astype(jnp.int32)
    for c in copies[:3]:
        c.wait()
    columns = []
    for table_ref_, index in ((time_bias_ref, times_ref[...]), (pos_bias_ref, bucket)):
        table = jnp.concatenate(three_parts(table_ref_[...] * 0.5), axis=0)
        kinds = table.shape[1]
        hot = lax.broadcasted_iota(jnp.int32, (kinds, events), 0) == index
        columns.append(jnp.dot(table, hot.astype(F32).astype(BF16), preferred_element_type=F32))
    used = sum(c.shape[0] for c in columns)
    columns.append(jnp.zeros((LANES - used, events), F32))
    out_ref[...] = jnp.concatenate(columns, axis=0).T.astype(BF16)
    copies[3].wait()


def prepare(place, start, times, time_bias, pos_bias, table, history):
    arrays = [times, time_bias, pos_bias, table]
    return pl.pallas_call(
        functools.partial(prepare_kernel, npos=pos_bias.shape[1], history=history),
        out_shape=(
            jax.ShapeDtypeStruct((times.shape[1], LANES), BF16),
            jax.ShapeDtypeStruct(table.shape, BF16),
        ),
        in_specs=[SMEM, SMEM] + [HBM] * 4,
        out_specs=(VMEM, VMEM),
        scratch_shapes=[pltpu.VMEM(a.shape, a.dtype) for a in arrays[:3]] + [pltpu.SemaphoreType.DMA((4,))],
        compiler_params=params(8),
        name="prepare",
    )(place, start, *(pltpu.with_memory_space_constraint(a, pltpu.HBM) for a in arrays))


def silu(x):
    return x / (1.0 + jnp.exp(-x))


def normalise(embedded, gain):
    x = embedded.astype(F32)
    meansq = jnp.mean(x * x, axis=-1, keepdims=True)
    return (x * lax.rsqrt(meansq + 1e-06) * gain).astype(BF16)


def attend_kernel(rounds_ref, pick_ref, *refs, heads, blocks):
    *row_refs, extra_hbm, gain_ref, proj_ref = refs[: -6 - 3 * blocks]
    caches = refs[-6 - 3 * blocks : -6]
    own_ref, keep_ref, send_ref, emb_ref, query_ref, sem = refs[-6:]
    count, width = emb_ref.shape
    rows = jnp.concatenate([r[...] for r in row_refs], axis=0)
    emb_ref[...] = jnp.dot(pick_ref[...], rows, preferred_element_type=F32).astype(BF16)

    @pl.when(rounds_ref[0] > 1)
    def _():
        extra = pltpu.make_async_copy(extra_hbm, query_ref, sem)
        extra.start()
        extra.wait()
        emb_ref[...] = emb_ref[...] + query_ref[...]

    own_ref[...] = emb_ref[: own_ref.shape[0], :]
    head_dim = width // heads
    half = count // 2
    rows = min(ROWS_AT_ONCE, count)
    per = LANES // head_dim
    for first in range(0, count, rows):
        normed = normalise(emb_ref[first : first + rows, :], gain_ref[...])
        projected = jnp.dot(normed, proj_ref[...], preferred_element_type=F32)
        query = silu(projected).astype(BF16)
        query_ref[first : first + rows, :] = query * jnp.asarray(0.5 * head_dim**-0.5, BF16)
        lane = lax.broadcasted_iota(jnp.int32, (rows, LANES), 1)
        stacks = {}

        def stack(group):
            if group not in stacks:
                part = query_ref[first : first + rows, group * LANES : (group + 1) * LANES]
                zero, one = jnp.zeros_like(part), jnp.ones_like(part)
                blocks_of = []
                for k in range(per):
                    own = jnp.where(lane // head_dim == k, part, zero)
                    chosen = jnp.where(lane % heads == group * per + k, one, zero)
                    blocks_of.append(jnp.concatenate([own, chosen], axis=1))
                stacks[group] = jnp.concatenate(blocks_of, axis=0)
            return stacks[group]

        def halves(group, block, j):
            at = slice(group * LANES, (group + 1) * LANES)
            keys = jnp.concatenate(
                [caches[block][j : j + step, at], caches[2 * blocks + block][j : j + step, :]], axis=1
            )
            return lax.dot_general(keys, stack(group), NT, preferred_element_type=F32)

        events = caches[0].shape[0]
        step = min(EVENTS_AT_ONCE, events)
        steps = [
            (group, block, j)
            for group in range(width // LANES)
            for block in range(blocks)
            for j in range(0, events, step)
        ]
        ahead = [halves(*s) for s in steps[:STEPS_AHEAD]]
        total = None
        for n, (group, block, j) in enumerate(steps):
            if n + STEPS_AHEAD < len(steps):
                ahead.append(halves(*steps[n + STEPS_AHEAD]))
            t = ahead.pop(0)
            weights = (t + t * jnp.tanh(t)).astype(BF16)
            at = slice(group * LANES, (group + 1) * LANES)
            term = lax.dot_general(
                caches[blocks + block][j : j + step, at], weights, TN, preferred_element_type=F32
            )
            total = term if total is None else total + term
            if n + 1 < len(steps) and steps[n + 1][0] == group:
                continue
            out = jnp.concatenate(
                [
                    total[k * head_dim : (k + 1) * head_dim, k * rows : (k + 1) * rows]
                    for k in range(per)
                ],
                axis=0,
            ).T
            total = None
            if first + rows <= half:
                keep_ref[first : first + rows, at] = out
            elif first >= half:
                send_ref[first - half : first - half + rows, at] = out.astype(BF16)
            else:
                keep_ref[first:half, at] = out[: half - first]
                send_ref[: first + rows - half, at] = out[half - first :].astype(BF16)


def attend(rounds, pick, pieces, extra, gain, proj, keys, values, biases, heads, each):
    count, width = extra.shape
    blocks = len(keys)
    return pl.pallas_call(
        functools.partial(attend_kernel, heads=heads, blocks=blocks),
        out_shape=(
            jax.ShapeDtypeStruct((each, width), BF16),
            jax.ShapeDtypeStruct((count // 2, width), F32),
            jax.ShapeDtypeStruct((count // 2, width), BF16),
        ),
        in_specs=[SMEM, VMEM] + [VMEM] * len(pieces) + [HBM] + [VMEM] * (2 + 3 * blocks),
        out_specs=(VMEM, VMEM, VMEM),
        scratch_shapes=[
            pltpu.VMEM((count, width), BF16),
            pltpu.VMEM((count, width), BF16),
            pltpu.SemaphoreType.DMA,
        ],
        compiler_params=params(20),
        cost_estimate=pl.CostEstimate(
            flops=8 * count * width * blocks * keys[0].shape[0],
            transcendentals=count * heads * blocks * keys[0].shape[0],
            bytes_accessed=4 * blocks * keys[0].size,
        ),
        name="attend",
    )(rounds, pick, *pieces, extra, gain, proj, *keys, *values, *biases)


def stage_kernel(*refs, width):
    *refs, sems = refs
    count = len(refs) // 2
    copies = [
        pltpu.make_async_copy(
            a if a.shape[1] == width else a.at[:, pl.ds(0, width)], b, sems.at[k]
        )
        for k, (a, b) in enumerate(zip(refs[:count], refs[count:]))
    ]
    for c in copies:
        c.start()
    for c in copies:
        c.wait()


def stage(width, *arrays, held=True):
    return pl.pallas_call(
        functools.partial(stage_kernel, width=width),
        out_shape=tuple(jax.ShapeDtypeStruct((a.shape[0], width), BF16) for a in arrays),
        in_specs=[HBM if held else pl.BlockSpec(memory_space=pl.ANY)] * len(arrays),
        out_specs=(VMEM,) * len(arrays),
        scratch_shapes=[pltpu.SemaphoreType.DMA((len(arrays),))],
        compiler_params=params(4),
        name="stage",
    )(*(pltpu.with_memory_space_constraint(a, pltpu.HBM) if held else a for a in arrays))


def gates_kernel(emb_ref, gain_ref, proj_ref, out_ref):
    normed = normalise(emb_ref[...], gain_ref[...])
    projected = jnp.dot(normed, proj_ref[...], preferred_element_type=F32)
    out_ref[...] = silu(projected).astype(BF16)


def gates_of(embedded, gain, proj_in):
    return pl.pallas_call(
        gates_kernel,
        out_shape=jax.ShapeDtypeStruct(embedded.shape, BF16),
        grid=(1,),
        in_specs=[VMEM, VMEM, pl.BlockSpec(proj_in.shape[:1] * 2, lambda i: (0, 1))],
        out_specs=VMEM,
        compiler_params=params(16),
        cost_estimate=pl.CostEstimate(flops=1 << 26, transcendentals=1 << 14, bytes_accessed=1 << 22),
        name="gates",
    )(embedded, gain, proj_in)


def finish_kernel(own_ref, *refs):
    *parts, emb_ref, gates_ref, gain_ref, proj_ref, out_ref = refs
    attended = own_ref[...]
    for p in parts:
        attended = attended + p[...].astype(F32)
    centred = attended - jnp.mean(attended, axis=-1, keepdims=True)
    variance = jnp.mean(centred * centred, axis=-1, keepdims=True)
    gated = centred * lax.rsqrt(variance + 1e-05) * gain_ref[...] * gates_ref[...].astype(F32)
    product = jnp.dot(gated.astype(BF16), proj_ref[...], preferred_element_type=F32)
    out_ref[...] = (emb_ref[...].astype(F32) + product).astype(BF16)


def finish(own, parts, embedded, gates, gain, proj_out):
    return pl.pallas_call(
        finish_kernel,
        out_shape=jax.ShapeDtypeStruct(embedded.shape, BF16),
        in_specs=[VMEM] * (len(parts) + 5),
        out_specs=VMEM,
        compiler_params=params(16),
        name="finish",
    )(own, *parts, embedded, gates, gain, proj_out)


def on_device(
    item_ids,
    item_table,
    key_cache,
    value_cache,
    time_buckets,
    window_start,
    norm_gain,
    proj_in,
    time_bias,
    pos_bias,
    out_gain,
    proj_out,
):
    axis = "hist"
    size = lax.axis_size(axis)
    me = lax.axis_index(axis).astype(jnp.int32)
    each = item_ids.shape[0]
    slots = 2 * each
    heads = time_bias.shape[0]
    events, width = key_cache.shape
    table_rows = item_table.shape[0]
    gain = norm_gain[None, :]

    def place(turn):
        return jnp.stack([me, jnp.asarray(turn, jnp.int32)])

    def partners(x):
        return swap(x, PARTNER, axis, size)

    here = place(0)
    other_table = partners(item_table)
    other_keys = partners(key_cache)
    other_values = partners(value_cache)
    bias, own_table = prepare(
        here, window_start, time_buckets[None, :], time_bias, pos_bias, item_table, 2 * events * size
    )
    other_bias = partners(bias)
    ids = gather_relative(item_ids[None, :], 1, axis, size)

    (near_table,) = stage(width, other_table, held=False)
    found, rounds = lookup(here, ids, [own_table, near_table], slots, size, True)
    pieces = gather_rows(found, axis, size)
    pick = plan(here, ids, slots, table_rows, size)

    def more(state):
        turn, so_far = state
        picked = plan(place(turn), ids, slots, table_rows, size)
        found, _ = lookup(place(turn), ids, [item_table, other_table], slots, size, False)
        return turn + 1, so_far + select(picked, gather_rows(found, axis, size))

    none = jnp.zeros((each * (size // 2), width), BF16)
    _, extra = lax.while_loop(lambda s: s[0] < rounds[0], more, (jnp.int32(1), none))

    keys, values = stage(width, key_cache, value_cache)
    proj, other_keys, other_values = stage(width, proj_in, other_keys, other_values)
    own, keep, send = attend(
        rounds,
        pick,
        pieces,
        extra,
        gain,
        proj,
        [keys, other_keys],
        [values, other_values],
        [bias, other_bias],
        heads,
        each,
    )
    gates = gates_of(own, gain, proj_in)

    *far, near = stage_masks(size)
    total = keep + swap(send, near[0], axis, size).astype(F32)
    for bits in far[::-1]:
        masks = combos(bits)
        block = total.shape[0] // len(masks)
        parts = [
            swap(total[k * block : (k + 1) * block].astype(BF16), m, axis, size)
            for k, m in enumerate(masks)
            if k
        ]
        if bits is far[0]:
            break
        total = sum([p.astype(F32) for p in parts], total[:block])
    return finish(total[:block], parts, own, gates, out_gain[None, :], proj_out)


def solution(mesh):
    placed = (
        P(("grp", "hist")),
        P("hist", None),
        P(("grp", "hist"), None),
        P(("grp", "hist"), None),
        P(("grp", "hist")),
        P("grp"),
        P(),
        P(),
        P(),
        P(),
        P(),
        P(),
    )

    return jax.shard_map(on_device, mesh=mesh, in_specs=placed, out_specs=P(("grp", "hist"), None), check_vma=False)
```

```python
import functools

import jax
import jax.numpy as jnp
from jax import lax
from jax.experimental import pallas as pl
from jax.experimental.pallas import tpu as pltpu
from jax.sharding import PartitionSpec as P


BF16 = jnp.bfloat16
F32 = jnp.float32
LANES = 128
ROWS_AT_ONCE = 128
EVENTS_AT_ONCE = 512
STEPS_AHEAD = 2
BLOCK = 16
TN = (((0,), (0,)), ((), ()))
NT = (((1,), (1,)), ((), ()))
VMEM = pl.BlockSpec(memory_space=pltpu.VMEM)
SMEM = pl.BlockSpec(memory_space=pltpu.SMEM)
HBM = pl.BlockSpec(memory_space=pltpu.HBM)


def params(mib):
    return pltpu.CompilerParams(vmem_limit_bytes=mib << 20)


PARTNER = 1


def stage_masks(size):
    bits = [1 << k for k in range(1, size.bit_length() - 1)][::-1]
    far = bits[:-1]
    return [sorted(far[k : k + 2]) for k in range(0, len(far), 2)] + [bits[-1:]]


def combos(bits):
    out = [0]
    for b in bits:
        out = out + [m | b for m in out]
    return out


def swap(x, mask, axis, size):
    return lax.ppermute(x, axis, [(i, i ^ mask) for i in range(size)])


def join_kernel(*refs):
    *parts, out_ref = refs
    rows = parts[0].shape[0]
    for k, p in enumerate(parts):
        out_ref[k * rows : (k + 1) * rows, :] = p[...]


def join(pieces, dim):
    if dim:
        return jnp.concatenate(pieces, axis=dim)
    rows, width = pieces[0].shape
    return pl.pallas_call(
        join_kernel,
        out_shape=jax.ShapeDtypeStruct((len(pieces) * rows, width), BF16),
        in_specs=[VMEM] * len(pieces),
        out_specs=VMEM,
        compiler_params=params(16),
        name="join",
    )(*pieces)


def gather_relative(x, dim, axis, size):
    *far, near = stage_masks(size)
    for bits in far:
        x = join([x] + [swap(x, m, axis, size) for m in combos(bits)[1:]], dim)
    return [x, swap(x, near[0], axis, size)]


def gather_rows(x, axis, size):
    *far, near = stage_masks(size)
    for bits in far[:-1]:
        x = join([x] + [swap(x, m, axis, size) for m in combos(bits)[1:]], 0)
    pieces = [x, join([swap(x, m, axis, size) for m in combos(far[-1])[1:]], 0)]
    return pieces + [swap(p, near[0], axis, size) for p in pieces]


def position_bits(size):
    return [b for stage in stage_masks(size) for b in stage]


def candidates_info(ids_refs, me, size, table_rows):
    ids = jnp.concatenate([r[...] for r in ids_refs], axis=1)
    count = ids.shape[1]
    each = count // (size // 2)
    owner = ids // table_rows
    place = lax.broadcasted_iota(jnp.int32, (1, count), 1)
    block = place // each
    mask = jnp.zeros_like(place)
    for k, b in enumerate(position_bits(size)):
        mask = mask + ((block >> k) & 1) * b
    pair = owner >> 1
    key = pair * count + ((mask ^ me) >> 1) * each + place % each
    return pair, key, ids - owner * table_rows + ((owner ^ me) & 1) * table_rows


def to_column(row):
    count = row.shape[1]
    r = lax.broadcasted_iota(jnp.int32, (count, count), 0)
    c = lax.broadcasted_iota(jnp.int32, (count, count), 1)
    return jnp.sum(jnp.where(r == c, row, 0), axis=1, keepdims=True)


def lookup_kernel(place_ref, *refs, size, resident):
    if resident:
        *ids_refs, own_ref, other_ref, out_ref, rounds_ref, blocks_ref = refs
        copies = []
    else:
        *ids_refs, own_hbm, other_hbm, out_ref, rounds_ref, blocks_ref, own_ref, other_ref, sems = refs
        copies = [
            pltpu.make_async_copy(own_hbm, own_ref, sems.at[0]),
            pltpu.make_async_copy(other_hbm, other_ref, sems.at[1]),
        ]
    for c in copies:
        c.start()
    me, turn = place_ref[0], place_ref[1]
    slots = out_ref.shape[0]
    rows = own_ref.shape[0]
    pair, key, offset = candidates_info(ids_refs, me, size, rows)
    count = pair.shape[1]
    key_col = to_column(key)
    before = (key_col < key) & (key_col >= pair * count)
    rank = jnp.sum(before.astype(jnp.int32), axis=0, keepdims=True)
    slot = lax.broadcasted_iota(jnp.int32, (slots, count), 0) + turn * slots
    hit = (pair == (me >> 1)) & (rank == slot)
    want = jnp.sum(jnp.where(hit, offset + 1, 0), axis=1, keepdims=True) - 1
    rounds_ref[0] = jnp.max(rank) // slots + 1
    for c in copies:
        c.wait()
    near = jnp.where(want < 0, 0, want // BLOCK)
    for k in range(slots):
        block = near[k, 0]
        in_own = block < rows // BLOCK
        at = pl.multiple_of((block - jnp.where(in_own, 0, rows // BLOCK)) * BLOCK, BLOCK)
        own, other = own_ref[pl.ds(at, BLOCK), :], other_ref[pl.ds(at, BLOCK), :]
        blocks_ref[k * BLOCK : (k + 1) * BLOCK, :] = jnp.where(in_own, own, other)
    column = lax.broadcasted_iota(jnp.int32, (slots, slots * BLOCK), 1)
    line = lax.broadcasted_iota(jnp.int32, (slots, slots * BLOCK), 0)
    pick = (want >= 0) & (column == line * BLOCK + (want - near * BLOCK))
    found = jnp.dot(pick.astype(F32).astype(BF16), blocks_ref[...], preferred_element_type=F32)
    out_ref[...] = found.astype(BF16)


def lookup(place, ids, tables, slots, size, resident):
    if not resident:
        tables = [pltpu.with_memory_space_constraint(t, pltpu.HBM) for t in tables]
    rows, width = tables[0].shape
    return pl.pallas_call(
        functools.partial(lookup_kernel, size=size, resident=resident),
        out_shape=(
            jax.ShapeDtypeStruct((slots, width), BF16),
            jax.ShapeDtypeStruct((1,), jnp.int32),
        ),
        in_specs=[SMEM] + [VMEM] * len(ids) + [VMEM if resident else HBM] * 2,
        out_specs=(VMEM, SMEM),
        scratch_shapes=[pltpu.VMEM((slots * BLOCK, width), BF16)]
        + ([] if resident else [pltpu.VMEM((rows, width), BF16)] * 2 + [pltpu.SemaphoreType.DMA((2,))]),
        compiler_params=params(16),
        name="lookup",
    )(place, *ids, *tables)


def plan_kernel(place_ref, *refs, size, slots, table_rows):
    *ids_refs, pick_ref = refs
    me, turn = place_ref[0], place_ref[1]
    pair, key, _ = candidates_info(ids_refs, me, size, table_rows)
    count = pair.shape[1]
    key_col = to_column(key)
    pair_col = key_col // count
    before = (key < key_col) & (key >= pair_col * count)
    rank = jnp.sum(before.astype(jnp.int32), axis=1, keepdims=True)
    away = pair_col ^ (me >> 1)
    block = jnp.zeros_like(away)
    for k, b in enumerate(position_bits(size)):
        block = block + jnp.where((away & (b >> 1)) != 0, 1 << k, 0)
    mine = rank - turn * slots
    slot = jnp.where((mine >= 0) & (mine < slots), block * slots + mine, -1)
    pick = slot == lax.broadcasted_iota(jnp.int32, pick_ref.shape, 1)
    pick_ref[...] = pick.astype(F32).astype(BF16)


def plan(place, ids, slots, table_rows, size):
    count = sum(i.shape[1] for i in ids)
    return pl.pallas_call(
        functools.partial(plan_kernel, size=size, slots=slots, table_rows=table_rows),
        out_shape=jax.ShapeDtypeStruct((count, size // 2 * slots), BF16),
        in_specs=[SMEM] + [VMEM] * len(ids),
        out_specs=VMEM,
        compiler_params=params(16),
        name="plan",
    )(place, *ids)


def select_kernel(pick_ref, rows_ref, out_ref):
    out_ref[...] = jnp.dot(pick_ref[...], rows_ref[...], preferred_element_type=F32).astype(BF16)


def select(pick, pieces):
    rows = jnp.concatenate(pieces, axis=0)
    return pl.pallas_call(
        select_kernel,
        out_shape=jax.ShapeDtypeStruct((pick.shape[0], rows.shape[1]), BF16),
        in_specs=[VMEM, VMEM],
        out_specs=VMEM,
        compiler_params=params(12),
        name="select",
    )(pick, rows)


def three_parts(x):
    high = x.astype(BF16)
    rest = x - high.astype(F32)
    middle = rest.astype(BF16)
    return [high, middle, (rest - middle.astype(F32)).astype(BF16)]


def prepare_kernel(
    place_ref, start_ref, times_hbm, time_bias_hbm, pos_bias_hbm, table_hbm, out_ref, table_ref,
    times_ref, time_bias_ref, pos_bias_ref, sems, *, npos, history
):
    pairs = ((times_hbm, times_ref), (time_bias_hbm, time_bias_ref), (pos_bias_hbm, pos_bias_ref), (table_hbm, table_ref))
    copies = [pltpu.make_async_copy(a, b, sems.at[k]) for k, (a, b) in enumerate(pairs)]
    for c in copies:
        c.start()
    events = times_ref.shape[1]
    first = history - start_ref[0] - place_ref[0] * events
    distance = first - lax.broadcasted_iota(jnp.int32, (1, events), 1)
    bucket = jnp.zeros((1, events), jnp.int32)
    for k in range(1, npos):
        bucket = bucket + (distance >= (1 << k)).astype(jnp.int32)
    for c in copies[:3]:
        c.wait()
    columns = []
    for table_ref_, index in ((time_bias_ref, times_ref[...]), (pos_bias_ref, bucket)):
        table = jnp.concatenate(three_parts(table_ref_[...] * 0.5), axis=0)
        kinds = table.shape[1]
        hot = lax.broadcasted_iota(jnp.int32, (kinds, events), 0) == index
        columns.append(jnp.dot(table, hot.astype(F32).astype(BF16), preferred_element_type=F32))
    used = sum(c.shape[0] for c in columns)
    columns.append(jnp.zeros((LANES - used, events), F32))
    out_ref[...] = jnp.concatenate(columns, axis=0).T.astype(BF16)
    copies[3].wait()


def prepare(place, start, times, time_bias, pos_bias, table, history):
    arrays = [times, time_bias, pos_bias, table]
    return pl.pallas_call(
        functools.partial(prepare_kernel, npos=pos_bias.shape[1], history=history),
        out_shape=(
            jax.ShapeDtypeStruct((times.shape[1], LANES), BF16),
            jax.ShapeDtypeStruct(table.shape, BF16),
        ),
        in_specs=[SMEM, SMEM] + [HBM] * 4,
        out_specs=(VMEM, VMEM),
        scratch_shapes=[pltpu.VMEM(a.shape, a.dtype) for a in arrays[:3]] + [pltpu.SemaphoreType.DMA((4,))],
        compiler_params=params(8),
        name="prepare",
    )(place, start, *(pltpu.with_memory_space_constraint(a, pltpu.HBM) for a in arrays))


def silu(x):
    return x / (1.0 + jnp.exp(-x))


def normalise(embedded, gain):
    x = embedded.astype(F32)
    meansq = jnp.mean(x * x, axis=-1, keepdims=True)
    return (x * lax.rsqrt(meansq + 1e-06) * gain).astype(BF16)


def attend_groups(query_ref, caches, groups, heads, keep_ref, send_ref):
    keys, values, biases = caches
    count = query_ref.shape[0]
    width = keys[0].shape[1]
    head_dim = width // heads
    per = LANES // head_dim
    half = count // 2
    rows = min(ROWS_AT_ONCE, count)
    events = keys[0].shape[0]
    step = min(EVENTS_AT_ONCE, events)
    base = groups[0]
    for first in range(0, count, rows):
        lane = lax.broadcasted_iota(jnp.int32, (rows, LANES), 1)
        stacks = {}

        def stack(group):
            if group not in stacks:
                at = (group - base) * LANES
                part = query_ref[first : first + rows, at : at + LANES]
                zero, one = jnp.zeros_like(part), jnp.ones_like(part)
                blocks = []
                for k in range(per):
                    own = jnp.where(lane // head_dim == k, part, zero)
                    chosen = jnp.where(lane % heads == group * per + k, one, zero)
                    blocks.append(jnp.concatenate([own, chosen], axis=1))
                stacks[group] = jnp.concatenate(blocks, axis=0)
            return stacks[group]

        def halves(group, block, j):
            at = slice(group * LANES, (group + 1) * LANES)
            left = jnp.concatenate([keys[block][j : j + step, at], biases[block][j : j + step, :]], axis=1)
            return lax.dot_general(left, stack(group), NT, preferred_element_type=F32)

        steps = [
            (group, block, j) for group in groups for block in range(len(keys)) for j in range(0, events, step)
        ]
        ahead = [halves(*s) for s in steps[:STEPS_AHEAD]]
        total = None
        for n, (group, block, j) in enumerate(steps):
            if n + STEPS_AHEAD < len(steps):
                ahead.append(halves(*steps[n + STEPS_AHEAD]))
            t = ahead.pop(0)
            weights = (t + t * jnp.tanh(t)).astype(BF16)
            at = slice(group * LANES, (group + 1) * LANES)
            term = lax.dot_general(values[block][j : j + step, at], weights, TN, preferred_element_type=F32)
            total = term if total is None else total + term
            if n + 1 < len(steps) and steps[n + 1][0] == group:
                continue
            out = jnp.concatenate(
                [total[k * head_dim : (k + 1) * head_dim, k * rows : (k + 1) * rows] for k in range(per)], axis=0
            ).T
            total = None
            at = slice((group - base) * LANES, (group - base + 1) * LANES)
            if first + rows <= half:
                keep_ref[first : first + rows, at] = out
            elif first >= half:
                send_ref[first - half : first - half + rows, at] = out.astype(BF16)
            else:
                keep_ref[first:half, at] = out[: half - first]
                send_ref[: first + rows - half, at] = out[half - first :].astype(BF16)


def attend_first_kernel(rounds_ref, pick_ref, *refs, heads, blocks, split):
    *row_refs, extra_hbm, gain_ref, proj_ref = refs[: -7 - 3 * blocks]
    caches = refs[-7 - 3 * blocks : -7]
    own_ref, keep_ref, send_ref, later_ref, emb_ref, query_ref, sem = refs[-7:]
    count, width = emb_ref.shape
    rows = jnp.concatenate([r[...] for r in row_refs], axis=0)
    emb_ref[...] = jnp.dot(pick_ref[...], rows, preferred_element_type=F32).astype(BF16)

    @pl.when(rounds_ref[0] > 1)
    def _():
        extra = pltpu.make_async_copy(extra_hbm, query_ref, sem)
        extra.start()
        extra.wait()
        emb_ref[...] = emb_ref[...] + query_ref[...]

    own_ref[...] = emb_ref[: own_ref.shape[0], :]
    head_dim = width // heads
    rows = min(ROWS_AT_ONCE, count)
    for first in range(0, count, rows):
        normed = normalise(emb_ref[first : first + rows, :], gain_ref[...])
        projected = jnp.dot(normed, proj_ref[:, :width], preferred_element_type=F32)
        query = silu(projected).astype(BF16) * jnp.asarray(0.5 * head_dim**-0.5, BF16)
        query_ref[first : first + rows, :] = query
        later_ref[first : first + rows, :] = query[:, split * LANES :]
    parts = [caches[k * blocks : (k + 1) * blocks] for k in range(3)]
    attend_groups(query_ref, parts, range(split), heads, keep_ref, send_ref)


def attend_later_kernel(query_ref, *refs, heads, blocks, split):
    *caches, keep_ref, send_ref = refs
    parts = [caches[k * blocks : (k + 1) * blocks] for k in range(3)]
    attend_groups(query_ref, parts, range(split, parts[0][0].shape[1] // LANES), heads, keep_ref, send_ref)


def attention_cost(count, columns, keys, head_dim):
    events = len(keys) * keys[0].shape[0]
    return pl.CostEstimate(
        flops=8 * count * columns * events,
        transcendentals=count * columns // head_dim * events,
        bytes_accessed=4 * columns * events,
    )


def attend_first(rounds, pick, pieces, extra, gain, proj, keys, values, biases, heads, each, split):
    count, width = extra.shape
    columns = split * LANES
    blocks = len(keys)
    return pl.pallas_call(
        functools.partial(attend_first_kernel, heads=heads, blocks=blocks, split=split),
        out_shape=(
            jax.ShapeDtypeStruct((each, width), BF16),
            jax.ShapeDtypeStruct((count // 2, columns), F32),
            jax.ShapeDtypeStruct((count // 2, columns), BF16),
            jax.ShapeDtypeStruct((count, width - columns), BF16),
        ),
        in_specs=[SMEM, VMEM] + [VMEM] * len(pieces) + [HBM] + [VMEM] * (2 + 3 * blocks),
        out_specs=(VMEM,) * 4,
        scratch_shapes=[
            pltpu.VMEM((count, width), BF16),
            pltpu.VMEM((count, width), BF16),
            pltpu.SemaphoreType.DMA,
        ],
        compiler_params=params(20),
        cost_estimate=attention_cost(count, columns, keys, width // heads),
        name="attend_first",
    )(rounds, pick, *pieces, extra, gain, proj, *keys, *values, *biases)


def attend_later(queries, keys, values, biases, heads, split):
    count, columns = queries.shape
    blocks = len(keys)
    return pl.pallas_call(
        functools.partial(attend_later_kernel, heads=heads, blocks=blocks, split=split),
        out_shape=(
            jax.ShapeDtypeStruct((count // 2, columns), F32),
            jax.ShapeDtypeStruct((count // 2, columns), BF16),
        ),
        in_specs=[VMEM] * (1 + 3 * blocks),
        out_specs=(VMEM, VMEM),
        compiler_params=params(20),
        cost_estimate=attention_cost(count, columns, keys, keys[0].shape[1] // heads),
        name="attend_later",
    )(queries, *keys, *values, *biases)


def combine_kernel(*refs, count):
    halves, (own_ref, *go_refs) = refs[:count], refs[count:]
    rows = own_ref.shape[0]
    for k, out_ref in enumerate([own_ref, *go_refs]):
        at = 0
        for keep_ref, came_ref in zip(halves[::2], halves[1::2]):
            to = at + keep_ref.shape[1]
            block = slice(k * rows, (k + 1) * rows)
            total = keep_ref[block, :] + came_ref[block, :].astype(F32)
            out_ref[:, at:to] = total.astype(out_ref.dtype)
            at = to


def combine(halves, blocks):
    rows = halves[0].shape[0] // blocks
    width = sum(h.shape[1] for h in halves[::2])
    return pl.pallas_call(
        functools.partial(combine_kernel, count=len(halves)),
        out_shape=tuple(jax.ShapeDtypeStruct((rows, width), BF16 if k else F32) for k in range(blocks)),
        in_specs=[VMEM] * len(halves),
        out_specs=(VMEM,) * blocks,
        compiler_params=params(12),
        name="combine",
    )(*halves)


def stage_kernel(*refs, width):
    *refs, sems = refs
    count = len(refs) // 2
    copies = [
        pltpu.make_async_copy(
            a if a.shape[1] == width else a.at[:, pl.ds(0, width)], b, sems.at[k]
        )
        for k, (a, b) in enumerate(zip(refs[:count], refs[count:]))
    ]
    for c in copies:
        c.start()
    for c in copies:
        c.wait()


def stage(width, *arrays, held=True):
    return pl.pallas_call(
        functools.partial(stage_kernel, width=width),
        out_shape=tuple(jax.ShapeDtypeStruct((a.shape[0], width), BF16) for a in arrays),
        in_specs=[HBM if held else pl.BlockSpec(memory_space=pl.ANY)] * len(arrays),
        out_specs=(VMEM,) * len(arrays),
        scratch_shapes=[pltpu.SemaphoreType.DMA((len(arrays),))],
        compiler_params=params(4),
        name="stage",
    )(*(pltpu.with_memory_space_constraint(a, pltpu.HBM) if held else a for a in arrays))


def gates_kernel(emb_ref, gain_ref, proj_ref, out_ref):
    normed = normalise(emb_ref[...], gain_ref[...])
    projected = jnp.dot(normed, proj_ref[...], preferred_element_type=F32)
    out_ref[...] = silu(projected).astype(BF16)


def gates_of(embedded, gain, proj_in):
    return pl.pallas_call(
        gates_kernel,
        out_shape=jax.ShapeDtypeStruct(embedded.shape, BF16),
        grid=(1,),
        in_specs=[VMEM, VMEM, pl.BlockSpec(proj_in.shape[:1] * 2, lambda i: (0, 1))],
        out_specs=VMEM,
        compiler_params=params(16),
        cost_estimate=pl.CostEstimate(flops=1 << 26, transcendentals=1 << 14, bytes_accessed=1 << 22),
        name="gates",
    )(embedded, gain, proj_in)


def finish_kernel(own_ref, *refs):
    *parts, emb_ref, gates_ref, gain_ref, proj_ref, out_ref = refs
    attended = own_ref[...]
    for p in parts:
        attended = attended + p[...].astype(F32)
    centred = attended - jnp.mean(attended, axis=-1, keepdims=True)
    variance = jnp.mean(centred * centred, axis=-1, keepdims=True)
    gated = centred * lax.rsqrt(variance + 1e-05) * gain_ref[...] * gates_ref[...].astype(F32)
    product = jnp.dot(gated.astype(BF16), proj_ref[...], preferred_element_type=F32)
    out_ref[...] = (emb_ref[...].astype(F32) + product).astype(BF16)


def finish(own, parts, embedded, gates, gain, proj_out):
    return pl.pallas_call(
        finish_kernel,
        out_shape=jax.ShapeDtypeStruct(embedded.shape, BF16),
        in_specs=[VMEM] * (len(parts) + 5),
        out_specs=VMEM,
        compiler_params=params(16),
        name="finish",
    )(own, *parts, embedded, gates, gain, proj_out)


def on_device(
    item_ids,
    item_table,
    key_cache,
    value_cache,
    time_buckets,
    window_start,
    norm_gain,
    proj_in,
    time_bias,
    pos_bias,
    out_gain,
    proj_out,
):
    axis = "hist"
    size = lax.axis_size(axis)
    me = lax.axis_index(axis).astype(jnp.int32)
    each = item_ids.shape[0]
    slots = 2 * each
    heads = time_bias.shape[0]
    events, width = key_cache.shape
    table_rows = item_table.shape[0]
    gain = norm_gain[None, :]

    def place(turn):
        return jnp.stack([me, jnp.asarray(turn, jnp.int32)])

    def partners(x):
        return swap(x, PARTNER, axis, size)

    here = place(0)
    other_table = partners(item_table)
    other_keys = partners(key_cache)
    other_values = partners(value_cache)
    bias, own_table = prepare(
        here, window_start, time_buckets[None, :], time_bias, pos_bias, item_table, 2 * events * size
    )
    other_bias = partners(bias)
    ids = gather_relative(item_ids[None, :], 1, axis, size)

    (near_table,) = stage(width, other_table, held=False)
    found, rounds = lookup(here, ids, [own_table, near_table], slots, size, True)
    pieces = gather_rows(found, axis, size)
    pick = plan(here, ids, slots, table_rows, size)

    def more(state):
        turn, so_far = state
        picked = plan(place(turn), ids, slots, table_rows, size)
        found, _ = lookup(place(turn), ids, [item_table, other_table], slots, size, False)
        return turn + 1, so_far + select(picked, gather_rows(found, axis, size))

    none = jnp.zeros((each * (size // 2), width), BF16)
    _, extra = lax.while_loop(lambda s: s[0] < rounds[0], more, (jnp.int32(1), none))

    keys, values = stage(width, key_cache, value_cache)
    proj, other_keys, other_values = stage(width, proj_in, other_keys, other_values)
    caches = ([keys, other_keys], [values, other_values], [bias, other_bias])
    *far, near = stage_masks(size)
    split = max(1, width // LANES * 7 // 8)
    own, keep, send, later = attend_first(rounds, pick, pieces, extra, gain, proj, *caches, heads, each, split)
    halves = [keep, swap(send, near[0], axis, size)]
    keep, send = attend_later(later, *caches, heads, split)
    halves += [keep, swap(send, near[0], axis, size)]
    gates = gates_of(own, gain, proj_in)

    total, *going = combine(halves, len(combos(far[-1])))
    for bits in far[::-1]:
        parts = [swap(g, m, axis, size) for g, m in zip(going, combos(bits)[1:])]
        if bits is far[0]:
            break
        total, *going = combine([total, sum(p.astype(F32) for p in parts)], len(combos(bits)))
    return finish(total, parts, own, gates, out_gain[None, :], proj_out)


def solution(mesh):
    placed = (
        P(("grp", "hist")),
        P("hist", None),
        P(("grp", "hist"), None),
        P(("grp", "hist"), None),
        P(("grp", "hist")),
        P("grp"),
        P(),
        P(),
        P(),
        P(),
        P(),
        P(),
    )

    return jax.shard_map(on_device, mesh=mesh, in_specs=placed, out_specs=P(("grp", "hist"), None), check_vma=False)
```

```python
import functools

import jax
import jax.numpy as jnp
from jax import lax
from jax.experimental import pallas as pl
from jax.experimental.pallas import tpu as pltpu
from jax.sharding import PartitionSpec as P


BF16 = jnp.bfloat16
F32 = jnp.float32
LANES = 128
ROWS_AT_ONCE = 128
EVENTS_AT_ONCE = 512
STEPS_AHEAD = 2
BLOCK = 16
TN = (((0,), (0,)), ((), ()))
NT = (((1,), (1,)), ((), ()))
VMEM = pl.BlockSpec(memory_space=pltpu.VMEM)
SMEM = pl.BlockSpec(memory_space=pltpu.SMEM)
HBM = pl.BlockSpec(memory_space=pltpu.HBM)


def params(mib):
    return pltpu.CompilerParams(vmem_limit_bytes=mib << 20)


PARTNER = 1


def stage_masks(size):
    bits = [1 << k for k in range(1, size.bit_length() - 1)][::-1]
    far = bits[:-1]
    return [sorted(far[k : k + 2]) for k in range(0, len(far), 2)] + [bits[-1:]]


def combos(bits):
    out = [0]
    for b in bits:
        out = out + [m | b for m in out]
    return out


def swap(x, mask, axis, size):
    return lax.ppermute(x, axis, [(i, i ^ mask) for i in range(size)])


def join_kernel(*refs):
    *parts, out_ref = refs
    rows = parts[0].shape[0]
    for k, p in enumerate(parts):
        out_ref[k * rows : (k + 1) * rows, :] = p[...]


def join(pieces, dim):
    if dim:
        return jnp.concatenate(pieces, axis=dim)
    rows, width = pieces[0].shape
    return pl.pallas_call(
        join_kernel,
        out_shape=jax.ShapeDtypeStruct((len(pieces) * rows, width), BF16),
        in_specs=[VMEM] * len(pieces),
        out_specs=VMEM,
        compiler_params=params(16),
        name="join",
    )(*pieces)


def gather_relative(x, dim, axis, size):
    *far, near = stage_masks(size)
    for bits in far:
        x = join([x] + [swap(x, m, axis, size) for m in combos(bits)[1:]], dim)
    return [x, swap(x, near[0], axis, size)]


def gather_rows(x, axis, size):
    *far, near = stage_masks(size)
    for bits in far[:-1]:
        x = join([x] + [swap(x, m, axis, size) for m in combos(bits)[1:]], 0)
    pieces = [x, join([swap(x, m, axis, size) for m in combos(far[-1])[1:]], 0)]
    return pieces + [swap(p, near[0], axis, size) for p in pieces]


def position_bits(size):
    return [b for stage in stage_masks(size) for b in stage]


def candidates_info(ids_refs, me, size, table_rows):
    ids = jnp.concatenate([r[...] for r in ids_refs], axis=1)
    count = ids.shape[1]
    each = count // (size // 2)
    owner = ids // table_rows
    place = lax.broadcasted_iota(jnp.int32, (1, count), 1)
    block = place // each
    mask = jnp.zeros_like(place)
    for k, b in enumerate(position_bits(size)):
        mask = mask + ((block >> k) & 1) * b
    pair = owner >> 1
    key = pair * count + ((mask ^ me) >> 1) * each + place % each
    return pair, key, ids - owner * table_rows + ((owner ^ me) & 1) * table_rows


def to_column(row):
    count = row.shape[1]
    r = lax.broadcasted_iota(jnp.int32, (count, count), 0)
    c = lax.broadcasted_iota(jnp.int32, (count, count), 1)
    return jnp.sum(jnp.where(r == c, row, 0), axis=1, keepdims=True)


def lookup_kernel(*refs, axis, size, first_turn):
    if first_turn:
        *ids_refs, own_ref, other_ref, out_ref, blocks_ref = refs
        turn, copies = 0, []
    else:
        turn_ref, *ids_refs, own_hbm, other_hbm, out_ref, blocks_ref, own_ref, other_ref, sems = refs
        turn = turn_ref[0]
        copies = [
            pltpu.make_async_copy(own_hbm, own_ref, sems.at[0]),
            pltpu.make_async_copy(other_hbm, other_ref, sems.at[1]),
        ]
    for c in copies:
        c.start()
    me = lax.axis_index(axis)
    slots = out_ref.shape[0]
    rows = own_ref.shape[0]
    pair, key, offset = candidates_info(ids_refs, me, size, rows)
    count = pair.shape[1]
    key_col = to_column(key)
    before = (key_col < key) & (key_col >= pair * count)
    rank = jnp.sum(before.astype(jnp.int32), axis=0, keepdims=True)
    slot = lax.broadcasted_iota(jnp.int32, (slots, count), 0) + turn * slots
    hit = (pair == (me >> 1)) & (rank == slot)
    want = jnp.sum(jnp.where(hit, offset + 1, 0), axis=1, keepdims=True) - 1
    for c in copies:
        c.wait()
    near = jnp.where(want < 0, 0, want // BLOCK)
    for k in range(slots):
        block = near[k, 0]
        in_own = block < rows // BLOCK
        at = pl.multiple_of((block - jnp.where(in_own, 0, rows // BLOCK)) * BLOCK, BLOCK)
        own, other = own_ref[pl.ds(at, BLOCK), :], other_ref[pl.ds(at, BLOCK), :]
        blocks_ref[k * BLOCK : (k + 1) * BLOCK, :] = jnp.where(in_own, own, other)
    column = lax.broadcasted_iota(jnp.int32, (slots, slots * BLOCK), 1)
    line = lax.broadcasted_iota(jnp.int32, (slots, slots * BLOCK), 0)
    pick = (want >= 0) & (column == line * BLOCK + (want - near * BLOCK))
    found = jnp.dot(pick.astype(F32).astype(BF16), blocks_ref[...], preferred_element_type=F32)
    out_ref[...] = found.astype(BF16)


def lookup(ids, tables, slots, axis, size, turn=None):
    first_turn = turn is None
    if not first_turn:
        tables = [pltpu.with_memory_space_constraint(t, pltpu.HBM) for t in tables]
    rows, width = tables[0].shape
    return pl.pallas_call(
        functools.partial(lookup_kernel, axis=axis, size=size, first_turn=first_turn),
        out_shape=jax.ShapeDtypeStruct((slots, width), BF16),
        in_specs=([] if first_turn else [SMEM]) + [VMEM] * len(ids) + [VMEM if first_turn else HBM] * 2,
        out_specs=VMEM,
        scratch_shapes=[pltpu.VMEM((slots * BLOCK, width), BF16)]
        + ([] if first_turn else [pltpu.VMEM((rows, width), BF16)] * 2 + [pltpu.SemaphoreType.DMA((2,))]),
        compiler_params=params(16),
        name="lookup",
    )(*([] if first_turn else [turn]), *ids, *tables)


def plan_kernel(*refs, axis, size, slots, table_rows, first_turn):
    if first_turn:
        *ids_refs, pick_ref, rounds_ref = refs
        turn = 0
    else:
        turn_ref, *ids_refs, pick_ref, rounds_ref = refs
        turn = turn_ref[0]
    me = lax.axis_index(axis)
    pair, key, _ = candidates_info(ids_refs, me, size, table_rows)
    count = pair.shape[1]
    key_col = to_column(key)
    pair_col = key_col // count
    before = (key < key_col) & (key >= pair_col * count)
    rank = jnp.sum(before.astype(jnp.int32), axis=1, keepdims=True)
    rounds_ref[0] = jnp.max(rank) // slots + 1
    away = pair_col ^ (me >> 1)
    block = jnp.zeros_like(away)
    for k, b in enumerate(position_bits(size)):
        block = block + jnp.where((away & (b >> 1)) != 0, 1 << k, 0)
    mine = rank - turn * slots
    slot = jnp.where((mine >= 0) & (mine < slots), block * slots + mine, -1)
    pick = slot == lax.broadcasted_iota(jnp.int32, pick_ref.shape, 1)
    pick_ref[...] = pick.astype(F32).astype(BF16)


def plan(ids, slots, table_rows, axis, size, turn=None):
    count = sum(i.shape[1] for i in ids)
    first_turn = turn is None
    return pl.pallas_call(
        functools.partial(
            plan_kernel, axis=axis, size=size, slots=slots, table_rows=table_rows, first_turn=first_turn
        ),
        out_shape=(
            jax.ShapeDtypeStruct((count, size // 2 * slots), BF16),
            jax.ShapeDtypeStruct((1,), jnp.int32),
        ),
        in_specs=([] if first_turn else [SMEM]) + [VMEM] * len(ids),
        out_specs=(VMEM, SMEM),
        compiler_params=params(16),
        name="plan",
    )(*([] if first_turn else [turn]), *ids)


def select_kernel(pick_ref, rows_ref, out_ref):
    out_ref[...] = jnp.dot(pick_ref[...], rows_ref[...], preferred_element_type=F32).astype(BF16)


def select(pick, pieces):
    rows = jnp.concatenate(pieces, axis=0)
    return pl.pallas_call(
        select_kernel,
        out_shape=jax.ShapeDtypeStruct((pick.shape[0], rows.shape[1]), BF16),
        in_specs=[VMEM, VMEM],
        out_specs=VMEM,
        compiler_params=params(12),
        name="select",
    )(pick, rows)


def three_parts(x):
    high = x.astype(BF16)
    rest = x - high.astype(F32)
    middle = rest.astype(BF16)
    return [high, middle, (rest - middle.astype(F32)).astype(BF16)]


def prepare_kernel(
    start_ref, times_hbm, time_bias_hbm, pos_bias_hbm, table_hbm, out_ref, table_ref,
    times_ref, time_bias_ref, pos_bias_ref, sems, *, axis, npos, history
):
    pairs = ((times_hbm, times_ref), (time_bias_hbm, time_bias_ref), (pos_bias_hbm, pos_bias_ref), (table_hbm, table_ref))
    copies = [pltpu.make_async_copy(a, b, sems.at[k]) for k, (a, b) in enumerate(pairs)]
    for c in copies:
        c.start()
    events = times_ref.shape[1]
    first = history - start_ref[0] - lax.axis_index(axis) * events
    distance = first - lax.broadcasted_iota(jnp.int32, (1, events), 1)
    bucket = jnp.zeros((1, events), jnp.int32)
    for k in range(1, npos):
        bucket = bucket + (distance >= (1 << k)).astype(jnp.int32)
    for c in copies[:3]:
        c.wait()
    columns = []
    for table_ref_, index in ((time_bias_ref, times_ref[...]), (pos_bias_ref, bucket)):
        table = jnp.concatenate(three_parts(table_ref_[...] * 0.5), axis=0)
        kinds = table.shape[1]
        hot = lax.broadcasted_iota(jnp.int32, (kinds, events), 0) == index
        columns.append(jnp.dot(table, hot.astype(F32).astype(BF16), preferred_element_type=F32))
    used = sum(c.shape[0] for c in columns)
    columns.append(jnp.zeros((LANES - used, events), F32))
    out_ref[...] = jnp.concatenate(columns, axis=0).T.astype(BF16)
    copies[3].wait()


def prepare(start, times, time_bias, pos_bias, table, axis, history):
    arrays = [times, time_bias, pos_bias, table]
    return pl.pallas_call(
        functools.partial(prepare_kernel, axis=axis, npos=pos_bias.shape[1], history=history),
        out_shape=(
            jax.ShapeDtypeStruct((times.shape[1], LANES), BF16),
            jax.ShapeDtypeStruct(table.shape, BF16),
        ),
        in_specs=[SMEM] + [HBM] * 4,
        out_specs=(VMEM, VMEM),
        scratch_shapes=[pltpu.VMEM(a.shape, a.dtype) for a in arrays[:3]] + [pltpu.SemaphoreType.DMA((4,))],
        compiler_params=params(8),
        name="prepare",
    )(start, *(pltpu.with_memory_space_constraint(a, pltpu.HBM) for a in arrays))


def silu(x):
    return x / (1.0 + jnp.exp(-x))


def normalise(embedded, gain):
    x = embedded.astype(F32)
    meansq = jnp.mean(x * x, axis=-1, keepdims=True)
    return (x * lax.rsqrt(meansq + 1e-06) * gain).astype(BF16)


def attend_groups(query_ref, caches, groups, heads, keep_ref, send_ref):
    keys, values, biases = caches
    count = query_ref.shape[0]
    width = keys[0].shape[1]
    head_dim = width // heads
    per = LANES // head_dim
    half = count // 2
    rows = min(ROWS_AT_ONCE, count)
    events = keys[0].shape[0]
    step = min(EVENTS_AT_ONCE, events)
    base = groups[0]
    for first in range(0, count, rows):
        lane = lax.broadcasted_iota(jnp.int32, (rows, LANES), 1)
        stacks = {}

        def stack(group):
            if group not in stacks:
                at = (group - base) * LANES
                part = query_ref[first : first + rows, at : at + LANES]
                zero, one = jnp.zeros_like(part), jnp.ones_like(part)
                blocks = []
                for k in range(per):
                    own = jnp.where(lane // head_dim == k, part, zero)
                    chosen = jnp.where(lane % heads == group * per + k, one, zero)
                    blocks.append(jnp.concatenate([own, chosen], axis=1))
                stacks[group] = jnp.concatenate(blocks, axis=0)
            return stacks[group]

        def halves(group, block, j):
            at = slice(group * LANES, (group + 1) * LANES)
            left = jnp.concatenate([keys[block][j : j + step, at], biases[block][j : j + step, :]], axis=1)
            return lax.dot_general(left, stack(group), NT, preferred_element_type=F32)

        steps = [
            (group, block, j) for group in groups for block in range(len(keys)) for j in range(0, events, step)
        ]
        ahead = [halves(*s) for s in steps[:STEPS_AHEAD]]
        total = None
        for n, (group, block, j) in enumerate(steps):
            if n + STEPS_AHEAD < len(steps):
                ahead.append(halves(*steps[n + STEPS_AHEAD]))
            t = ahead.pop(0)
            weights = (t + t * jnp.tanh(t)).astype(BF16)
            at = slice(group * LANES, (group + 1) * LANES)
            term = lax.dot_general(values[block][j : j + step, at], weights, TN, preferred_element_type=F32)
            total = term if total is None else total + term
            if n + 1 < len(steps) and steps[n + 1][0] == group:
                continue
            out = jnp.concatenate(
                [total[k * head_dim : (k + 1) * head_dim, k * rows : (k + 1) * rows] for k in range(per)], axis=0
            ).T
            total = None
            at = slice((group - base) * LANES, (group - base + 1) * LANES)
            if first + rows <= half:
                keep_ref[first : first + rows, at] = out
            elif first >= half:
                send_ref[first - half : first - half + rows, at] = out.astype(BF16)
            else:
                keep_ref[first:half, at] = out[: half - first]
                send_ref[: first + rows - half, at] = out[half - first :].astype(BF16)


def attend_first_kernel(rounds_hbm, pick_ref, *refs, heads, blocks, split):
    *row_refs, extra_hbm, gain_ref, proj_ref = refs[: -8 - 3 * blocks]
    caches = refs[-8 - 3 * blocks : -8]
    own_ref, keep_ref, send_ref, later_ref, emb_ref, query_ref, rounds_ref, sems = refs[-8:]
    count, width = emb_ref.shape
    told = pltpu.make_async_copy(rounds_hbm, rounds_ref, sems.at[0])
    told.start()
    rows = jnp.concatenate([r[...] for r in row_refs], axis=0)
    emb_ref[...] = jnp.dot(pick_ref[...], rows, preferred_element_type=F32).astype(BF16)

    told.wait()

    @pl.when(rounds_ref[0] > 1)
    def _():
        extra = pltpu.make_async_copy(extra_hbm, query_ref, sems.at[1])
        extra.start()
        extra.wait()
        emb_ref[...] = emb_ref[...] + query_ref[...]

    own_ref[...] = emb_ref[: own_ref.shape[0], :]
    head_dim = width // heads
    rows = min(ROWS_AT_ONCE, count)
    for first in range(0, count, rows):
        normed = normalise(emb_ref[first : first + rows, :], gain_ref[...])
        projected = jnp.dot(normed, proj_ref[:, :width], preferred_element_type=F32)
        query = silu(projected).astype(BF16) * jnp.asarray(0.5 * head_dim**-0.5, BF16)
        query_ref[first : first + rows, :] = query
        later_ref[first : first + rows, :] = query[:, split * LANES :]
    parts = [caches[k * blocks : (k + 1) * blocks] for k in range(3)]
    attend_groups(query_ref, parts, range(split), heads, keep_ref, send_ref)


def attend_later_kernel(query_ref, *refs, heads, blocks, split):
    *caches, keep_ref, send_ref = refs
    parts = [caches[k * blocks : (k + 1) * blocks] for k in range(3)]
    attend_groups(query_ref, parts, range(split, parts[0][0].shape[1] // LANES), heads, keep_ref, send_ref)


def attention_cost(count, columns, keys, head_dim):
    events = len(keys) * keys[0].shape[0]
    return pl.CostEstimate(
        flops=8 * count * columns * events,
        transcendentals=count * columns // head_dim * events,
        bytes_accessed=4 * columns * events,
    )


def attend_first(rounds, pick, pieces, extra, gain, proj, keys, values, biases, heads, each, split):
    count, width = extra.shape
    columns = split * LANES
    blocks = len(keys)
    return pl.pallas_call(
        functools.partial(attend_first_kernel, heads=heads, blocks=blocks, split=split),
        out_shape=(
            jax.ShapeDtypeStruct((each, width), BF16),
            jax.ShapeDtypeStruct((count // 2, columns), F32),
            jax.ShapeDtypeStruct((count // 2, columns), BF16),
            jax.ShapeDtypeStruct((count, width - columns), BF16),
        ),
        in_specs=[HBM, VMEM] + [VMEM] * len(pieces) + [HBM] + [VMEM] * (2 + 3 * blocks),
        out_specs=(VMEM,) * 4,
        scratch_shapes=[
            pltpu.VMEM((count, width), BF16),
            pltpu.VMEM((count, width), BF16),
            pltpu.SMEM((1,), jnp.int32),
            pltpu.SemaphoreType.DMA((2,)),
        ],
        compiler_params=params(20),
        cost_estimate=attention_cost(count, columns, keys, width // heads),
        name="attend_first",
    )(rounds, pick, *pieces, extra, gain, proj, *keys, *values, *biases)


def attend_later(queries, keys, values, biases, heads, split):
    count, columns = queries.shape
    blocks = len(keys)
    return pl.pallas_call(
        functools.partial(attend_later_kernel, heads=heads, blocks=blocks, split=split),
        out_shape=(
            jax.ShapeDtypeStruct((count // 2, columns), F32),
            jax.ShapeDtypeStruct((count // 2, columns), BF16),
        ),
        in_specs=[VMEM] * (1 + 3 * blocks),
        out_specs=(VMEM, VMEM),
        compiler_params=params(20),
        cost_estimate=attention_cost(count, columns, keys, keys[0].shape[1] // heads),
        name="attend_later",
    )(queries, *keys, *values, *biases)


def combine_kernel(*refs, count):
    halves, (own_ref, *go_refs) = refs[:count], refs[count:]
    rows = own_ref.shape[0]
    for k, out_ref in enumerate([own_ref, *go_refs]):
        at = 0
        for keep_ref, came_ref in zip(halves[::2], halves[1::2]):
            to = at + keep_ref.shape[1]
            block = slice(k * rows, (k + 1) * rows)
            total = keep_ref[block, :] + came_ref[block, :].astype(F32)
            out_ref[:, at:to] = total.astype(out_ref.dtype)
            at = to


def combine(halves, blocks):
    rows = halves[0].shape[0] // blocks
    width = sum(h.shape[1] for h in halves[::2])
    return pl.pallas_call(
        functools.partial(combine_kernel, count=len(halves)),
        out_shape=tuple(jax.ShapeDtypeStruct((rows, width), BF16 if k else F32) for k in range(blocks)),
        in_specs=[VMEM] * len(halves),
        out_specs=(VMEM,) * blocks,
        compiler_params=params(12),
        name="combine",
    )(*halves)


def stage_kernel(*refs, width):
    *refs, sems = refs
    count = len(refs) // 2
    copies = [
        pltpu.make_async_copy(
            a if a.shape[1] == width else a.at[:, pl.ds(0, width)], b, sems.at[k]
        )
        for k, (a, b) in enumerate(zip(refs[:count], refs[count:]))
    ]
    for c in copies:
        c.start()
    for c in copies:
        c.wait()


def stage(width, *arrays, held=True):
    return pl.pallas_call(
        functools.partial(stage_kernel, width=width),
        out_shape=tuple(jax.ShapeDtypeStruct((a.shape[0], width), BF16) for a in arrays),
        in_specs=[HBM if held else pl.BlockSpec(memory_space=pl.ANY)] * len(arrays),
        out_specs=(VMEM,) * len(arrays),
        scratch_shapes=[pltpu.SemaphoreType.DMA((len(arrays),))],
        compiler_params=params(4),
        name="stage",
    )(*(pltpu.with_memory_space_constraint(a, pltpu.HBM) if held else a for a in arrays))


def gates_kernel(emb_ref, gain_ref, proj_ref, out_ref):
    normed = normalise(emb_ref[...], gain_ref[...])
    projected = jnp.dot(normed, proj_ref[...], preferred_element_type=F32)
    out_ref[...] = silu(projected).astype(BF16)


def gates_of(embedded, gain, proj_in):
    return pl.pallas_call(
        gates_kernel,
        out_shape=jax.ShapeDtypeStruct(embedded.shape, BF16),
        grid=(1,),
        in_specs=[VMEM, VMEM, pl.BlockSpec(proj_in.shape[:1] * 2, lambda i: (0, 1))],
        out_specs=VMEM,
        compiler_params=params(16),
        cost_estimate=pl.CostEstimate(flops=1 << 26, transcendentals=1 << 14, bytes_accessed=1 << 22),
        name="gates",
    )(embedded, gain, proj_in)


def finish_kernel(own_ref, *refs):
    *parts, emb_ref, gates_ref, gain_ref, proj_ref, out_ref = refs
    attended = own_ref[...]
    for p in parts:
        attended = attended + p[...].astype(F32)
    centred = attended - jnp.mean(attended, axis=-1, keepdims=True)
    variance = jnp.mean(centred * centred, axis=-1, keepdims=True)
    gated = centred * lax.rsqrt(variance + 1e-05) * gain_ref[...] * gates_ref[...].astype(F32)
    product = jnp.dot(gated.astype(BF16), proj_ref[...], preferred_element_type=F32)
    out_ref[...] = (emb_ref[...].astype(F32) + product).astype(BF16)


def finish(own, parts, embedded, gates, gain, proj_out):
    return pl.pallas_call(
        finish_kernel,
        out_shape=jax.ShapeDtypeStruct(embedded.shape, BF16),
        in_specs=[VMEM] * (len(parts) + 5),
        out_specs=VMEM,
        compiler_params=params(16),
        name="finish",
    )(own, *parts, embedded, gates, gain, proj_out)


def on_device(
    item_ids,
    item_table,
    key_cache,
    value_cache,
    time_buckets,
    window_start,
    norm_gain,
    proj_in,
    time_bias,
    pos_bias,
    out_gain,
    proj_out,
):
    axis = "hist"
    size = lax.axis_size(axis)
    each = item_ids.shape[0]
    slots = 2 * each
    heads = time_bias.shape[0]
    events, width = key_cache.shape
    table_rows = item_table.shape[0]
    gain = norm_gain[None, :]

    def partners(x):
        return swap(x, PARTNER, axis, size)

    other_table = partners(item_table)
    other_keys = partners(key_cache)
    other_values = partners(value_cache)
    bias, own_table = prepare(
        window_start, time_buckets[None, :], time_bias, pos_bias, item_table, axis, 2 * events * size
    )
    other_bias = partners(bias)
    ids = gather_relative(item_ids[None, :], 1, axis, size)

    (near_table,) = stage(width, other_table, held=False)
    found = lookup(ids, [own_table, near_table], slots, axis, size)
    pieces = gather_rows(found, axis, size)
    pick, rounds = plan(ids, slots, table_rows, axis, size)

    def more(state):
        turn, so_far = state
        picked, _ = plan(ids, slots, table_rows, axis, size, turn[None])
        found = lookup(ids, [item_table, other_table], slots, axis, size, turn[None])
        return turn + 1, so_far + select(picked, gather_rows(found, axis, size))

    none = jnp.zeros((each * (size // 2), width), BF16)
    _, extra = lax.while_loop(lambda s: s[0] < rounds[0], more, (jnp.int32(1), none))

    (keys,) = stage(width, key_cache)
    proj, values, other_keys, other_values = stage(width, proj_in, value_cache, other_keys, other_values)
    caches = ([keys, other_keys], [values, other_values], [bias, other_bias])
    *far, near = stage_masks(size)
    split = max(1, width // LANES * 7 // 8)
    own, keep, send, later = attend_first(rounds, pick, pieces, extra, gain, proj, *caches, heads, each, split)
    halves = [keep, swap(send, near[0], axis, size)]
    keep, send = attend_later(later, *caches, heads, split)
    halves += [keep, swap(send, near[0], axis, size)]
    gates = gates_of(own, gain, proj_in)

    total, *going = combine(halves, len(combos(far[-1])))
    for bits in far[::-1]:
        parts = [swap(g, m, axis, size) for g, m in zip(going, combos(bits)[1:])]
        if bits is far[0]:
            break
        total, *going = combine([total, sum(p.astype(F32) for p in parts)], len(combos(bits)))
    return finish(total, parts, own, gates, out_gain[None, :], proj_out)


def solution(mesh):
    placed = (
        P(("grp", "hist")),
        P("hist", None),
        P(("grp", "hist"), None),
        P(("grp", "hist"), None),
        P(("grp", "hist")),
        P("grp"),
        P(),
        P(),
        P(),
        P(),
        P(),
        P(),
    )

    return jax.shard_map(on_device, mesh=mesh, in_specs=placed, out_specs=P(("grp", "hist"), None), check_vma=False)
```

```python
import functools

import jax
import jax.numpy as jnp
from jax import lax
from jax.experimental import pallas as pl
from jax.experimental.pallas import tpu as pltpu
from jax.sharding import PartitionSpec as P


BF16 = jnp.bfloat16
F32 = jnp.float32
LANES = 128
ROWS_AT_ONCE = 128
EVENTS_AT_ONCE = 512
STEPS_AHEAD = 2
BLOCK = 16
TN = (((0,), (0,)), ((), ()))
NT = (((1,), (1,)), ((), ()))
VMEM = pl.BlockSpec(memory_space=pltpu.VMEM)
SMEM = pl.BlockSpec(memory_space=pltpu.SMEM)
HBM = pl.BlockSpec(memory_space=pltpu.HBM)


def params(mib):
    return pltpu.CompilerParams(vmem_limit_bytes=mib << 20)


PARTNER = 1


def stage_masks(size):
    bits = [1 << k for k in range(1, size.bit_length() - 1)][::-1]
    far = bits[:-1]
    return [sorted(far[k : k + 2]) for k in range(0, len(far), 2)] + [bits[-1:]]


def combos(bits):
    out = [0]
    for b in bits:
        out = out + [m | b for m in out]
    return out


def swap(x, mask, axis, size):
    return lax.ppermute(x, axis, [(i, i ^ mask) for i in range(size)])


def join_kernel(*refs):
    *parts, out_ref = refs
    rows = parts[0].shape[0]
    for k, p in enumerate(parts):
        out_ref[k * rows : (k + 1) * rows, :] = p[...]


def join(pieces, dim):
    if dim:
        return jnp.concatenate(pieces, axis=dim)
    rows, width = pieces[0].shape
    return pl.pallas_call(
        join_kernel,
        out_shape=jax.ShapeDtypeStruct((len(pieces) * rows, width), BF16),
        in_specs=[VMEM] * len(pieces),
        out_specs=VMEM,
        compiler_params=params(16),
        name="join",
    )(*pieces)


def gather_relative(x, dim, axis, size):
    *far, near = stage_masks(size)
    for bits in far:
        x = join([x] + [swap(x, m, axis, size) for m in combos(bits)[1:]], dim)
    return [x, swap(x, near[0], axis, size)]


def gather_rows(x, axis, size):
    *far, near = stage_masks(size)
    for bits in far[:-1]:
        x = join([x] + [swap(x, m, axis, size) for m in combos(bits)[1:]], 0)
    pieces = [x, join([swap(x, m, axis, size) for m in combos(far[-1])[1:]], 0)]
    return pieces + [swap(p, near[0], axis, size) for p in pieces]


def position_bits(size):
    return [b for stage in stage_masks(size) for b in stage]


def candidates_info(ids_refs, me, size, table_rows):
    ids = jnp.concatenate([r[...] for r in ids_refs], axis=1)
    count = ids.shape[1]
    each = count // (size // 2)
    owner = ids // table_rows
    place = lax.broadcasted_iota(jnp.int32, (1, count), 1)
    block = place // each
    mask = jnp.zeros_like(place)
    for k, b in enumerate(position_bits(size)):
        mask = mask + ((block >> k) & 1) * b
    pair = owner >> 1
    key = pair * count + ((mask ^ me) >> 1) * each + place % each
    return pair, key, ids - owner * table_rows + ((owner ^ me) & 1) * table_rows


def to_column(row):
    count = row.shape[1]
    r = lax.broadcasted_iota(jnp.int32, (count, count), 0)
    c = lax.broadcasted_iota(jnp.int32, (count, count), 1)
    return jnp.sum(jnp.where(r == c, row, 0), axis=1, keepdims=True)


def lookup_kernel(*refs, axis, size, first_turn):
    if first_turn:
        *ids_refs, own_ref, other_ref, out_ref, blocks_ref = refs
        turn, copies = 0, []
    else:
        turn_ref, *ids_refs, own_hbm, other_hbm, out_ref, blocks_ref, own_ref, other_ref, sems = refs
        turn = turn_ref[0]
        copies = [
            pltpu.make_async_copy(own_hbm, own_ref, sems.at[0]),
            pltpu.make_async_copy(other_hbm, other_ref, sems.at[1]),
        ]
    for c in copies:
        c.start()
    me = lax.axis_index(axis)
    slots = out_ref.shape[0]
    rows = own_ref.shape[0]
    pair, key, offset = candidates_info(ids_refs, me, size, rows)
    count = pair.shape[1]
    key_col = to_column(key)
    before = (key_col < key) & (key_col >= pair * count)
    rank = jnp.sum(before.astype(jnp.int32), axis=0, keepdims=True)
    slot = lax.broadcasted_iota(jnp.int32, (slots, count), 0) + turn * slots
    hit = (pair == (me >> 1)) & (rank == slot)
    want = jnp.sum(jnp.where(hit, offset + 1, 0), axis=1, keepdims=True) - 1
    for c in copies:
        c.wait()
    near = jnp.where(want < 0, 0, want // BLOCK)
    for k in range(slots):
        block = near[k, 0]
        in_own = block < rows // BLOCK
        at = pl.multiple_of((block - jnp.where(in_own, 0, rows // BLOCK)) * BLOCK, BLOCK)
        own, other = own_ref[pl.ds(at, BLOCK), :], other_ref[pl.ds(at, BLOCK), :]
        blocks_ref[k * BLOCK : (k + 1) * BLOCK, :] = jnp.where(in_own, own, other)
    column = lax.broadcasted_iota(jnp.int32, (slots, slots * BLOCK), 1)
    line = lax.broadcasted_iota(jnp.int32, (slots, slots * BLOCK), 0)
    pick = (want >= 0) & (column == line * BLOCK + (want - near * BLOCK))
    found = jnp.dot(pick.astype(F32).astype(BF16), blocks_ref[...], preferred_element_type=F32)
    out_ref[...] = found.astype(BF16)


def lookup(ids, tables, slots, axis, size, turn=None):
    first_turn = turn is None
    if not first_turn:
        tables = [pltpu.with_memory_space_constraint(t, pltpu.HBM) for t in tables]
    rows, width = tables[0].shape
    return pl.pallas_call(
        functools.partial(lookup_kernel, axis=axis, size=size, first_turn=first_turn),
        out_shape=jax.ShapeDtypeStruct((slots, width), BF16),
        in_specs=([] if first_turn else [SMEM]) + [VMEM] * len(ids) + [VMEM if first_turn else HBM] * 2,
        out_specs=VMEM,
        scratch_shapes=[pltpu.VMEM((slots * BLOCK, width), BF16)]
        + ([] if first_turn else [pltpu.VMEM((rows, width), BF16)] * 2 + [pltpu.SemaphoreType.DMA((2,))]),
        compiler_params=params(16),
        name="lookup",
    )(*([] if first_turn else [turn]), *ids, *tables)


def plan_kernel(*refs, axis, size, slots, table_rows, first_turn):
    if first_turn:
        *ids_refs, pick_ref, rounds_ref = refs
        turn = 0
    else:
        turn_ref, *ids_refs, pick_ref, rounds_ref = refs
        turn = turn_ref[0]
    me = lax.axis_index(axis)
    pair, key, _ = candidates_info(ids_refs, me, size, table_rows)
    count = pair.shape[1]
    key_col = to_column(key)
    pair_col = key_col // count
    before = (key < key_col) & (key >= pair_col * count)
    rank = jnp.sum(before.astype(jnp.int32), axis=1, keepdims=True)
    rounds_ref[0] = jnp.max(rank) // slots + 1
    away = pair_col ^ (me >> 1)
    block = jnp.zeros_like(away)
    for k, b in enumerate(position_bits(size)):
        block = block + jnp.where((away & (b >> 1)) != 0, 1 << k, 0)
    mine = rank - turn * slots
    slot = jnp.where((mine >= 0) & (mine < slots), block * slots + mine, -1)
    pick = slot == lax.broadcasted_iota(jnp.int32, pick_ref.shape, 1)
    pick_ref[...] = pick.astype(F32).astype(BF16)


def plan(ids, slots, table_rows, axis, size, turn=None):
    count = sum(i.shape[1] for i in ids)
    first_turn = turn is None
    return pl.pallas_call(
        functools.partial(
            plan_kernel, axis=axis, size=size, slots=slots, table_rows=table_rows, first_turn=first_turn
        ),
        out_shape=(
            jax.ShapeDtypeStruct((count, size // 2 * slots), BF16),
            jax.ShapeDtypeStruct((1,), jnp.int32),
        ),
        in_specs=([] if first_turn else [SMEM]) + [VMEM] * len(ids),
        out_specs=(VMEM, SMEM),
        compiler_params=params(16),
        name="plan",
    )(*([] if first_turn else [turn]), *ids)


def select_kernel(pick_ref, rows_ref, out_ref):
    out_ref[...] = jnp.dot(pick_ref[...], rows_ref[...], preferred_element_type=F32).astype(BF16)


def select(pick, pieces):
    rows = jnp.concatenate(pieces, axis=0)
    return pl.pallas_call(
        select_kernel,
        out_shape=jax.ShapeDtypeStruct((pick.shape[0], rows.shape[1]), BF16),
        in_specs=[VMEM, VMEM],
        out_specs=VMEM,
        compiler_params=params(12),
        name="select",
    )(pick, rows)


def three_parts(x):
    high = x.astype(BF16)
    rest = x - high.astype(F32)
    middle = rest.astype(BF16)
    return [high, middle, (rest - middle.astype(F32)).astype(BF16)]


def prepare_kernel(
    start_ref, times_hbm, time_bias_hbm, pos_bias_hbm, table_hbm, out_ref, table_ref,
    times_ref, time_bias_ref, pos_bias_ref, sems, *, axis, npos, history
):
    pairs = ((times_hbm, times_ref), (time_bias_hbm, time_bias_ref), (pos_bias_hbm, pos_bias_ref), (table_hbm, table_ref))
    copies = [pltpu.make_async_copy(a, b, sems.at[k]) for k, (a, b) in enumerate(pairs)]
    for c in copies:
        c.start()
    events = times_ref.shape[1]
    first = history - start_ref[0] - lax.axis_index(axis) * events
    distance = first - lax.broadcasted_iota(jnp.int32, (1, events), 1)
    bucket = jnp.zeros((1, events), jnp.int32)
    for k in range(1, npos):
        bucket = bucket + (distance >= (1 << k)).astype(jnp.int32)
    for c in copies[:3]:
        c.wait()
    columns = []
    for table_ref_, index in ((time_bias_ref, times_ref[...]), (pos_bias_ref, bucket)):
        table = jnp.concatenate(three_parts(table_ref_[...] * 0.5), axis=0)
        kinds = table.shape[1]
        hot = lax.broadcasted_iota(jnp.int32, (kinds, events), 0) == index
        columns.append(jnp.dot(table, hot.astype(F32).astype(BF16), preferred_element_type=F32))
    used = sum(c.shape[0] for c in columns)
    columns.append(jnp.zeros((LANES - used, events), F32))
    out_ref[...] = jnp.concatenate(columns, axis=0).T.astype(BF16)
    copies[3].wait()


def prepare(start, times, time_bias, pos_bias, table, axis, history):
    arrays = [times, time_bias, pos_bias, table]
    return pl.pallas_call(
        functools.partial(prepare_kernel, axis=axis, npos=pos_bias.shape[1], history=history),
        out_shape=(
            jax.ShapeDtypeStruct((times.shape[1], LANES), BF16),
            jax.ShapeDtypeStruct(table.shape, BF16),
        ),
        in_specs=[SMEM] + [HBM] * 4,
        out_specs=(VMEM, VMEM),
        scratch_shapes=[pltpu.VMEM(a.shape, a.dtype) for a in arrays[:3]] + [pltpu.SemaphoreType.DMA((4,))],
        compiler_params=params(8),
        name="prepare",
    )(start, *(pltpu.with_memory_space_constraint(a, pltpu.HBM) for a in arrays))


def silu(x):
    return x / (1.0 + jnp.exp(-x))


def normalise(embedded, gain):
    x = embedded.astype(F32)
    meansq = jnp.mean(x * x, axis=-1, keepdims=True)
    return (x * lax.rsqrt(meansq + 1e-06) * gain).astype(BF16)


def attend_groups(query_ref, caches, groups, heads, keep_ref, send_ref):
    keys, values, biases = caches
    count = query_ref.shape[0]
    width = keys[0].shape[1]
    head_dim = width // heads
    per = LANES // head_dim
    half = count // 2
    rows = min(ROWS_AT_ONCE, count)
    events = keys[0].shape[0]
    step = min(EVENTS_AT_ONCE, events)
    base = groups[0]
    for first in range(0, count, rows):
        lane = lax.broadcasted_iota(jnp.int32, (rows, LANES), 1)
        stacks = {}

        def stack(group):
            if group not in stacks:
                at = (group - base) * LANES
                part = query_ref[first : first + rows, at : at + LANES]
                zero, one = jnp.zeros_like(part), jnp.ones_like(part)
                blocks = []
                for k in range(per):
                    own = jnp.where(lane // head_dim == k, part, zero)
                    chosen = jnp.where(lane % heads == group * per + k, one, zero)
                    blocks.append(jnp.concatenate([own, chosen], axis=1))
                stacks[group] = jnp.concatenate(blocks, axis=0)
            return stacks[group]

        def halves(group, block, j):
            at = slice(group * LANES, (group + 1) * LANES)
            left = jnp.concatenate([keys[block][j : j + step, at], biases[block][j : j + step, :]], axis=1)
            return lax.dot_general(left, stack(group), NT, preferred_element_type=F32)

        steps = [
            (group, block, j) for group in groups for block in range(len(keys)) for j in range(0, events, step)
        ]
        ahead = [halves(*s) for s in steps[:STEPS_AHEAD]]
        total = None
        for n, (group, block, j) in enumerate(steps):
            if n + STEPS_AHEAD < len(steps):
                ahead.append(halves(*steps[n + STEPS_AHEAD]))
            t = ahead.pop(0)
            weights = (t + t * jnp.tanh(t)).astype(BF16)
            at = slice(group * LANES, (group + 1) * LANES)
            term = lax.dot_general(values[block][j : j + step, at], weights, TN, preferred_element_type=F32)
            total = term if total is None else total + term
            if n + 1 < len(steps) and steps[n + 1][0] == group:
                continue
            out = jnp.concatenate(
                [total[k * head_dim : (k + 1) * head_dim, k * rows : (k + 1) * rows] for k in range(per)], axis=0
            ).T
            total = None
            at = slice((group - base) * LANES, (group - base + 1) * LANES)
            if first + rows <= half:
                keep_ref[first : first + rows, at] = out
            elif first >= half:
                send_ref[first - half : first - half + rows, at] = out.astype(BF16)
            else:
                keep_ref[first:half, at] = out[: half - first]
                send_ref[: first + rows - half, at] = out[half - first :].astype(BF16)


def attend_first_kernel(rounds_ref, pick_ref, *refs, heads, blocks, split):
    *row_refs, extra_hbm, gain_ref, proj_ref = refs[: -7 - 3 * blocks]
    caches = refs[-7 - 3 * blocks : -7]
    own_ref, keep_ref, send_ref, later_ref, emb_ref, query_ref, sem = refs[-7:]
    count, width = emb_ref.shape
    rows = jnp.concatenate([r[...] for r in row_refs], axis=0)
    emb_ref[...] = jnp.dot(pick_ref[...], rows, preferred_element_type=F32).astype(BF16)


    @pl.when(rounds_ref[0] > 1)
    def _():
        extra = pltpu.make_async_copy(extra_hbm, query_ref, sem)
        extra.start()
        extra.wait()
        emb_ref[...] = emb_ref[...] + query_ref[...]

    own_ref[...] = emb_ref[: own_ref.shape[0], :]
    head_dim = width // heads
    rows = min(ROWS_AT_ONCE, count)
    for first in range(0, count, rows):
        normed = normalise(emb_ref[first : first + rows, :], gain_ref[...])
        projected = jnp.dot(normed, proj_ref[:, :width], preferred_element_type=F32)
        query = silu(projected).astype(BF16) * jnp.asarray(0.5 * head_dim**-0.5, BF16)
        query_ref[first : first + rows, :] = query
        later_ref[first : first + rows, :] = query[:, split * LANES :]
    parts = [caches[k * blocks : (k + 1) * blocks] for k in range(3)]
    attend_groups(query_ref, parts, range(split), heads, keep_ref, send_ref)


def attend_later_kernel(query_ref, *refs, heads, blocks, split):
    *caches, keep_ref, send_ref = refs
    parts = [caches[k * blocks : (k + 1) * blocks] for k in range(3)]
    attend_groups(query_ref, parts, range(split, parts[0][0].shape[1] // LANES), heads, keep_ref, send_ref)


def attention_cost(count, columns, keys, head_dim):
    events = len(keys) * keys[0].shape[0]
    return pl.CostEstimate(
        flops=8 * count * columns * events,
        transcendentals=count * columns // head_dim * events,
        bytes_accessed=4 * columns * events,
    )


def attend_first(rounds, pick, pieces, extra, gain, proj, keys, values, biases, heads, each, split):
    count, width = extra.shape
    columns = split * LANES
    blocks = len(keys)
    return pl.pallas_call(
        functools.partial(attend_first_kernel, heads=heads, blocks=blocks, split=split),
        out_shape=(
            jax.ShapeDtypeStruct((each, width), BF16),
            jax.ShapeDtypeStruct((count // 2, columns), F32),
            jax.ShapeDtypeStruct((count // 2, columns), BF16),
            jax.ShapeDtypeStruct((count, width - columns), BF16),
        ),
        in_specs=[SMEM, VMEM] + [VMEM] * len(pieces) + [HBM] + [VMEM] * (2 + 3 * blocks),
        out_specs=(VMEM,) * 4,
        scratch_shapes=[
            pltpu.VMEM((count, width), BF16),
            pltpu.VMEM((count, width), BF16),
            pltpu.SemaphoreType.DMA,
        ],
        compiler_params=params(20),
        cost_estimate=attention_cost(count, columns, keys, width // heads),
        name="attend_first",
    )(rounds, pick, *pieces, extra, gain, proj, *keys, *values, *biases)


def attend_later(queries, keys, values, biases, heads, split):
    count, columns = queries.shape
    blocks = len(keys)
    return pl.pallas_call(
        functools.partial(attend_later_kernel, heads=heads, blocks=blocks, split=split),
        out_shape=(
            jax.ShapeDtypeStruct((count // 2, columns), F32),
            jax.ShapeDtypeStruct((count // 2, columns), BF16),
        ),
        in_specs=[VMEM] * (1 + 3 * blocks),
        out_specs=(VMEM, VMEM),
        compiler_params=params(20),
        cost_estimate=attention_cost(count, columns, keys, keys[0].shape[1] // heads),
        name="attend_later",
    )(queries, *keys, *values, *biases)


def combine_kernel(*refs, count):
    halves, (own_ref, *go_refs) = refs[:count], refs[count:]
    rows = own_ref.shape[0]
    for k, out_ref in enumerate([own_ref, *go_refs]):
        at = 0
        for keep_ref, came_ref in zip(halves[::2], halves[1::2]):
            to = at + keep_ref.shape[1]
            block = slice(k * rows, (k + 1) * rows)
            total = keep_ref[block, :] + came_ref[block, :].astype(F32)
            out_ref[:, at:to] = total.astype(out_ref.dtype)
            at = to


def combine(halves, blocks):
    rows = halves[0].shape[0] // blocks
    width = sum(h.shape[1] for h in halves[::2])
    return pl.pallas_call(
        functools.partial(combine_kernel, count=len(halves)),
        out_shape=tuple(jax.ShapeDtypeStruct((rows, width), BF16 if k else F32) for k in range(blocks)),
        in_specs=[VMEM] * len(halves),
        out_specs=(VMEM,) * blocks,
        compiler_params=params(12),
        name="combine",
    )(*halves)


def stage_kernel(*refs, width):
    *refs, sems = refs
    count = len(refs) // 2
    copies = [
        pltpu.make_async_copy(
            a if a.shape[1] == width else a.at[:, pl.ds(0, width)], b, sems.at[k]
        )
        for k, (a, b) in enumerate(zip(refs[:count], refs[count:]))
    ]
    for c in copies:
        c.start()
    for c in copies:
        c.wait()


def stage(width, *arrays, held=True):
    return pl.pallas_call(
        functools.partial(stage_kernel, width=width),
        out_shape=tuple(jax.ShapeDtypeStruct((a.shape[0], width), BF16) for a in arrays),
        in_specs=[HBM if held else pl.BlockSpec(memory_space=pl.ANY)] * len(arrays),
        out_specs=(VMEM,) * len(arrays),
        scratch_shapes=[pltpu.SemaphoreType.DMA((len(arrays),))],
        compiler_params=params(4),
        name="stage",
    )(*(pltpu.with_memory_space_constraint(a, pltpu.HBM) if held else a for a in arrays))


def gates_kernel(emb_ref, gain_ref, proj_ref, out_ref):
    normed = normalise(emb_ref[...], gain_ref[...])
    projected = jnp.dot(normed, proj_ref[...], preferred_element_type=F32)
    out_ref[...] = silu(projected).astype(BF16)


def gates_of(embedded, gain, proj_in):
    return pl.pallas_call(
        gates_kernel,
        out_shape=jax.ShapeDtypeStruct(embedded.shape, BF16),
        grid=(1,),
        in_specs=[VMEM, VMEM, pl.BlockSpec(proj_in.shape[:1] * 2, lambda i: (0, 1))],
        out_specs=VMEM,
        compiler_params=params(16),
        cost_estimate=pl.CostEstimate(flops=1 << 26, transcendentals=1 << 14, bytes_accessed=1 << 22),
        name="gates",
    )(embedded, gain, proj_in)


def finish_kernel(own_ref, *refs):
    *parts, emb_ref, gates_ref, gain_ref, proj_ref, out_ref = refs
    attended = own_ref[...]
    for p in parts:
        attended = attended + p[...].astype(F32)
    centred = attended - jnp.mean(attended, axis=-1, keepdims=True)
    variance = jnp.mean(centred * centred, axis=-1, keepdims=True)
    gated = centred * lax.rsqrt(variance + 1e-05) * gain_ref[...] * gates_ref[...].astype(F32)
    product = jnp.dot(gated.astype(BF16), proj_ref[...], preferred_element_type=F32)
    out_ref[...] = (emb_ref[...].astype(F32) + product).astype(BF16)


def finish(own, parts, embedded, gates, gain, proj_out):
    return pl.pallas_call(
        finish_kernel,
        out_shape=jax.ShapeDtypeStruct(embedded.shape, BF16),
        in_specs=[VMEM] * (len(parts) + 5),
        out_specs=VMEM,
        compiler_params=params(16),
        name="finish",
    )(own, *parts, embedded, gates, gain, proj_out)


def on_device(
    item_ids,
    item_table,
    key_cache,
    value_cache,
    time_buckets,
    window_start,
    norm_gain,
    proj_in,
    time_bias,
    pos_bias,
    out_gain,
    proj_out,
):
    axis = "hist"
    size = lax.axis_size(axis)
    each = item_ids.shape[0]
    slots = 2 * each
    heads = time_bias.shape[0]
    events, width = key_cache.shape
    table_rows = item_table.shape[0]
    gain = norm_gain[None, :]

    def partners(x):
        return swap(x, PARTNER, axis, size)

    other_table = partners(item_table)
    other_keys = partners(key_cache)
    other_values = partners(value_cache)
    bias, own_table = prepare(
        window_start, time_buckets[None, :], time_bias, pos_bias, item_table, axis, 2 * events * size
    )
    other_bias = partners(bias)
    ids = gather_relative(item_ids[None, :], 1, axis, size)

    (near_table,) = stage(width, other_table, held=False)
    found = lookup(ids, [own_table, near_table], slots, axis, size)
    pieces = gather_rows(found, axis, size)
    pick, rounds = plan(ids, slots, table_rows, axis, size)

    def more(state):
        turn, so_far = state
        picked, _ = plan(ids, slots, table_rows, axis, size, turn[None])
        found = lookup(ids, [item_table, other_table], slots, axis, size, turn[None])
        return turn + 1, so_far + select(picked, gather_rows(found, axis, size))

    none = jnp.zeros((each * (size // 2), width), BF16)
    _, extra = lax.while_loop(lambda s: s[0] < rounds[0], more, (jnp.int32(1), none))

    proj, keys, values, other_keys, other_values = stage(
        width, proj_in, key_cache, value_cache, other_keys, other_values
    )
    caches = ([keys, other_keys], [values, other_values], [bias, other_bias])
    *far, near = stage_masks(size)
    split = max(1, width // LANES * 7 // 8)
    own, keep, send, later = attend_first(rounds, pick, pieces, extra, gain, proj, *caches, heads, each, split)
    halves = [keep, swap(send, near[0], axis, size)]
    keep, send = attend_later(later, *caches, heads, split)
    halves += [keep, swap(send, near[0], axis, size)]
    gates = gates_of(own, gain, proj_in)

    total, *going = combine(halves, len(combos(far[-1])))
    for bits in far[::-1]:
        parts = [swap(g, m, axis, size) for g, m in zip(going, combos(bits)[1:])]
        if bits is far[0]:
            break
        total, *going = combine([total, sum(p.astype(F32) for p in parts)], len(combos(bits)))
    return finish(total, parts, own, gates, out_gain[None, :], proj_out)


def solution(mesh):
    placed = (
        P(("grp", "hist")),
        P("hist", None),
        P(("grp", "hist"), None),
        P(("grp", "hist"), None),
        P(("grp", "hist")),
        P("grp"),
        P(),
        P(),
        P(),
        P(),
        P(),
        P(),
    )

    return jax.shard_map(on_device, mesh=mesh, in_specs=placed, out_specs=P(("grp", "hist"), None), check_vma=False)
```

```python
import functools

import jax
import jax.numpy as jnp
from jax import lax
from jax.experimental import pallas as pl
from jax.experimental.pallas import tpu as pltpu
from jax.sharding import PartitionSpec as P


BF16 = jnp.bfloat16
F32 = jnp.float32
LANES = 128
ROWS_AT_ONCE = 128
EVENTS_AT_ONCE = 512
STEPS_AHEAD = 2
BLOCK = 16
TN = (((0,), (0,)), ((), ()))
NT = (((1,), (1,)), ((), ()))
VMEM = pl.BlockSpec(memory_space=pltpu.VMEM)
SMEM = pl.BlockSpec(memory_space=pltpu.SMEM)
HBM = pl.BlockSpec(memory_space=pltpu.HBM)


def params(mib):
    return pltpu.CompilerParams(vmem_limit_bytes=mib << 20)


PARTNER = 1


def stage_masks(size):
    bits = [1 << k for k in range(1, size.bit_length() - 1)][::-1]
    far = bits[:-1]
    return [sorted(far[k : k + 2]) for k in range(0, len(far), 2)] + [bits[-1:]]


def combos(bits):
    out = [0]
    for b in bits:
        out = out + [m | b for m in out]
    return out


def swap(x, mask, axis, size):
    return lax.ppermute(x, axis, [(i, i ^ mask) for i in range(size)])


def join_kernel(*refs):
    *parts, out_ref = refs
    rows = parts[0].shape[0]
    for k, p in enumerate(parts):
        out_ref[k * rows : (k + 1) * rows, :] = p[...]


def join(pieces, dim):
    if dim:
        return jnp.concatenate(pieces, axis=dim)
    rows, width = pieces[0].shape
    return pl.pallas_call(
        join_kernel,
        out_shape=jax.ShapeDtypeStruct((len(pieces) * rows, width), BF16),
        in_specs=[VMEM] * len(pieces),
        out_specs=VMEM,
        compiler_params=params(16),
        name="join",
    )(*pieces)


def gather_relative(x, dim, axis, size):
    *far, near = stage_masks(size)
    for bits in far:
        x = join([x] + [swap(x, m, axis, size) for m in combos(bits)[1:]], dim)
    return [x, swap(x, near[0], axis, size)]


def gather_rows(x, axis, size):
    *far, near = stage_masks(size)
    for bits in far[:-1]:
        x = join([x] + [swap(x, m, axis, size) for m in combos(bits)[1:]], 0)
    first, *rest = combos(far[-1])[1:]
    early = swap(x, near[0], axis, size)
    beside = swap(x, first, axis, size)
    others = join([swap(x, m, axis, size) for m in rest], 0)
    late = swap(others, near[0], axis, size)
    across = swap(early, first, axis, size)
    return [x, beside, others, early, across, late]


def position_bits(size):
    return [b for stage in stage_masks(size) for b in stage]


def candidates_info(ids_refs, me, size, table_rows):
    ids = jnp.concatenate([r[...] for r in ids_refs], axis=1)
    count = ids.shape[1]
    each = count // (size // 2)
    owner = ids // table_rows
    place = lax.broadcasted_iota(jnp.int32, (1, count), 1)
    block = place // each
    mask = jnp.zeros_like(place)
    for k, b in enumerate(position_bits(size)):
        mask = mask + ((block >> k) & 1) * b
    pair = owner >> 1
    key = pair * count + ((mask ^ me) >> 1) * each + place % each
    return pair, key, ids - owner * table_rows + ((owner ^ me) & 1) * table_rows


def to_column(row):
    count = row.shape[1]
    r = lax.broadcasted_iota(jnp.int32, (count, count), 0)
    c = lax.broadcasted_iota(jnp.int32, (count, count), 1)
    return jnp.sum(jnp.where(r == c, row, 0), axis=1, keepdims=True)


def lookup_kernel(*refs, axis, size, first_turn):
    if first_turn:
        *ids_refs, own_ref, other_ref, out_ref, blocks_ref = refs
        turn, copies = 0, []
    else:
        turn_ref, *ids_refs, own_hbm, other_hbm, out_ref, blocks_ref, own_ref, other_ref, sems = refs
        turn = turn_ref[0]
        copies = [
            pltpu.make_async_copy(own_hbm, own_ref, sems.at[0]),
            pltpu.make_async_copy(other_hbm, other_ref, sems.at[1]),
        ]
    for c in copies:
        c.start()
    me = lax.axis_index(axis)
    slots = out_ref.shape[0]
    rows = own_ref.shape[0]
    pair, key, offset = candidates_info(ids_refs, me, size, rows)
    count = pair.shape[1]
    key_col = to_column(key)
    before = (key_col < key) & (key_col >= pair * count)
    rank = jnp.sum(before.astype(jnp.int32), axis=0, keepdims=True)
    slot = lax.broadcasted_iota(jnp.int32, (slots, count), 0) + turn * slots
    hit = (pair == (me >> 1)) & (rank == slot)
    want = jnp.sum(jnp.where(hit, offset + 1, 0), axis=1, keepdims=True) - 1
    for c in copies:
        c.wait()
    near = jnp.where(want < 0, 0, want // BLOCK)
    for k in range(slots):
        block = near[k, 0]
        in_own = block < rows // BLOCK
        at = pl.multiple_of((block - jnp.where(in_own, 0, rows // BLOCK)) * BLOCK, BLOCK)
        own, other = own_ref[pl.ds(at, BLOCK), :], other_ref[pl.ds(at, BLOCK), :]
        blocks_ref[k * BLOCK : (k + 1) * BLOCK, :] = jnp.where(in_own, own, other)
    column = lax.broadcasted_iota(jnp.int32, (slots, slots * BLOCK), 1)
    line = lax.broadcasted_iota(jnp.int32, (slots, slots * BLOCK), 0)
    pick = (want >= 0) & (column == line * BLOCK + (want - near * BLOCK))
    found = jnp.dot(pick.astype(F32).astype(BF16), blocks_ref[...], preferred_element_type=F32)
    out_ref[...] = found.astype(BF16)


def lookup(ids, tables, slots, axis, size, turn=None):
    first_turn = turn is None
    if not first_turn:
        tables = [pltpu.with_memory_space_constraint(t, pltpu.HBM) for t in tables]
    rows, width = tables[0].shape
    return pl.pallas_call(
        functools.partial(lookup_kernel, axis=axis, size=size, first_turn=first_turn),
        out_shape=jax.ShapeDtypeStruct((slots, width), BF16),
        in_specs=([] if first_turn else [SMEM]) + [VMEM] * len(ids) + [VMEM if first_turn else HBM] * 2,
        out_specs=VMEM,
        scratch_shapes=[pltpu.VMEM((slots * BLOCK, width), BF16)]
        + ([] if first_turn else [pltpu.VMEM((rows, width), BF16)] * 2 + [pltpu.SemaphoreType.DMA((2,))]),
        compiler_params=params(16),
        name="lookup",
    )(*([] if first_turn else [turn]), *ids, *tables)


def plan_kernel(*refs, axis, size, slots, table_rows, first_turn):
    if first_turn:
        *ids_refs, pick_ref, rounds_ref = refs
        turn = 0
    else:
        turn_ref, *ids_refs, pick_ref, rounds_ref = refs
        turn = turn_ref[0]
    me = lax.axis_index(axis)
    pair, key, _ = candidates_info(ids_refs, me, size, table_rows)
    count = pair.shape[1]
    key_col = to_column(key)
    pair_col = key_col // count
    before = (key < key_col) & (key >= pair_col * count)
    rank = jnp.sum(before.astype(jnp.int32), axis=1, keepdims=True)
    rounds_ref[0] = jnp.max(rank) // slots + 1
    away = pair_col ^ (me >> 1)
    block = jnp.zeros_like(away)
    for k, b in enumerate(position_bits(size)):
        block = block + jnp.where((away & (b >> 1)) != 0, 1 << k, 0)
    mine = rank - turn * slots
    slot = jnp.where((mine >= 0) & (mine < slots), block * slots + mine, -1)
    pick = slot == lax.broadcasted_iota(jnp.int32, pick_ref.shape, 1)
    pick_ref[...] = pick.astype(F32).astype(BF16)


def plan(ids, slots, table_rows, axis, size, turn=None):
    count = sum(i.shape[1] for i in ids)
    first_turn = turn is None
    return pl.pallas_call(
        functools.partial(
            plan_kernel, axis=axis, size=size, slots=slots, table_rows=table_rows, first_turn=first_turn
        ),
        out_shape=(
            jax.ShapeDtypeStruct((count, size // 2 * slots), BF16),
            jax.ShapeDtypeStruct((1,), jnp.int32),
        ),
        in_specs=([] if first_turn else [SMEM]) + [VMEM] * len(ids),
        out_specs=(VMEM, SMEM),
        compiler_params=params(16),
        name="plan",
    )(*([] if first_turn else [turn]), *ids)


def select_kernel(pick_ref, rows_ref, out_ref):
    out_ref[...] = jnp.dot(pick_ref[...], rows_ref[...], preferred_element_type=F32).astype(BF16)


def select(pick, pieces):
    rows = jnp.concatenate(pieces, axis=0)
    return pl.pallas_call(
        select_kernel,
        out_shape=jax.ShapeDtypeStruct((pick.shape[0], rows.shape[1]), BF16),
        in_specs=[VMEM, VMEM],
        out_specs=VMEM,
        compiler_params=params(12),
        name="select",
    )(pick, rows)


def three_parts(x):
    high = x.astype(BF16)
    rest = x - high.astype(F32)
    middle = rest.astype(BF16)
    return [high, middle, (rest - middle.astype(F32)).astype(BF16)]


def prepare_kernel(
    start_ref, times_hbm, time_bias_hbm, pos_bias_hbm, table_hbm, out_ref, table_ref,
    times_ref, time_bias_ref, pos_bias_ref, sems, *, axis, npos, history
):
    pairs = ((times_hbm, times_ref), (time_bias_hbm, time_bias_ref), (pos_bias_hbm, pos_bias_ref), (table_hbm, table_ref))
    copies = [pltpu.make_async_copy(a, b, sems.at[k]) for k, (a, b) in enumerate(pairs)]
    for c in copies:
        c.start()
    events = times_ref.shape[1]
    first = history - start_ref[0] - lax.axis_index(axis) * events
    distance = first - lax.broadcasted_iota(jnp.int32, (1, events), 1)
    bucket = jnp.zeros((1, events), jnp.int32)
    for k in range(1, npos):
        bucket = bucket + (distance >= (1 << k)).astype(jnp.int32)
    for c in copies[:3]:
        c.wait()
    columns = []
    for table_ref_, index in ((time_bias_ref, times_ref[...]), (pos_bias_ref, bucket)):
        table = jnp.concatenate(three_parts(table_ref_[...] * 0.5), axis=0)
        kinds = table.shape[1]
        hot = lax.broadcasted_iota(jnp.int32, (kinds, events), 0) == index
        columns.append(jnp.dot(table, hot.astype(F32).astype(BF16), preferred_element_type=F32))
    used = sum(c.shape[0] for c in columns)
    columns.append(jnp.zeros((LANES - used, events), F32))
    out_ref[...] = jnp.concatenate(columns, axis=0).T.astype(BF16)
    copies[3].wait()


def prepare(start, times, time_bias, pos_bias, table, axis, history):
    arrays = [times, time_bias, pos_bias, table]
    return pl.pallas_call(
        functools.partial(prepare_kernel, axis=axis, npos=pos_bias.shape[1], history=history),
        out_shape=(
            jax.ShapeDtypeStruct((times.shape[1], LANES), BF16),
            jax.ShapeDtypeStruct(table.shape, BF16),
        ),
        in_specs=[SMEM] + [HBM] * 4,
        out_specs=(VMEM, VMEM),
        scratch_shapes=[pltpu.VMEM(a.shape, a.dtype) for a in arrays[:3]] + [pltpu.SemaphoreType.DMA((4,))],
        compiler_params=params(8),
        name="prepare",
    )(start, *(pltpu.with_memory_space_constraint(a, pltpu.HBM) for a in arrays))


def silu(x):
    return x / (1.0 + jnp.exp(-x))


def normalise(embedded, gain):
    x = embedded.astype(F32)
    meansq = jnp.mean(x * x, axis=-1, keepdims=True)
    return (x * lax.rsqrt(meansq + 1e-06) * gain).astype(BF16)


def attend_groups(query_ref, caches, groups, heads, keep_ref, send_ref):
    keys, values, biases = caches
    count = query_ref.shape[0]
    width = keys[0].shape[1]
    head_dim = width // heads
    per = LANES // head_dim
    half = count // 2
    rows = min(ROWS_AT_ONCE, count)
    events = keys[0].shape[0]
    step = min(EVENTS_AT_ONCE, events)
    base = groups[0]
    for first in range(0, count, rows):
        lane = lax.broadcasted_iota(jnp.int32, (rows, LANES), 1)
        stacks = {}

        def stack(group):
            if group not in stacks:
                at = (group - base) * LANES
                part = query_ref[first : first + rows, at : at + LANES]
                zero, one = jnp.zeros_like(part), jnp.ones_like(part)
                blocks = []
                for k in range(per):
                    own = jnp.where(lane // head_dim == k, part, zero)
                    chosen = jnp.where(lane % heads == group * per + k, one, zero)
                    blocks.append(jnp.concatenate([own, chosen], axis=1))
                stacks[group] = jnp.concatenate(blocks, axis=0)
            return stacks[group]

        def halves(group, block, j):
            at = slice(group * LANES, (group + 1) * LANES)
            left = jnp.concatenate([keys[block][j : j + step, at], biases[block][j : j + step, :]], axis=1)
            return lax.dot_general(left, stack(group), NT, preferred_element_type=F32)

        steps = [
            (group, block, j) for group in groups for block in range(len(keys)) for j in range(0, events, step)
        ]
        ahead = [halves(*s) for s in steps[:STEPS_AHEAD]]
        total = None
        for n, (group, block, j) in enumerate(steps):
            if n + STEPS_AHEAD < len(steps):
                ahead.append(halves(*steps[n + STEPS_AHEAD]))
            t = ahead.pop(0)
            weights = (t + t * jnp.tanh(t)).astype(BF16)
            at = slice(group * LANES, (group + 1) * LANES)
            term = lax.dot_general(values[block][j : j + step, at], weights, TN, preferred_element_type=F32)
            total = term if total is None else total + term
            if n + 1 < len(steps) and steps[n + 1][0] == group:
                continue
            out = jnp.concatenate(
                [total[k * head_dim : (k + 1) * head_dim, k * rows : (k + 1) * rows] for k in range(per)], axis=0
            ).T
            total = None
            at = slice((group - base) * LANES, (group - base + 1) * LANES)
            if first + rows <= half:
                keep_ref[first : first + rows, at] = out
            elif first >= half:
                send_ref[first - half : first - half + rows, at] = out.astype(BF16)
            else:
                keep_ref[first:half, at] = out[: half - first]
                send_ref[: first + rows - half, at] = out[half - first :].astype(BF16)


def attend_first_kernel(rounds_ref, pick_ref, *refs, heads, blocks, split):
    *row_refs, extra_hbm, gain_ref, proj_ref = refs[: -7 - 3 * blocks]
    caches = refs[-7 - 3 * blocks : -7]
    own_ref, keep_ref, send_ref, later_ref, emb_ref, query_ref, sem = refs[-7:]
    count, width = emb_ref.shape
    rows = jnp.concatenate([r[...] for r in row_refs], axis=0)
    emb_ref[...] = jnp.dot(pick_ref[...], rows, preferred_element_type=F32).astype(BF16)


    @pl.when(rounds_ref[0] > 1)
    def _():
        extra = pltpu.make_async_copy(extra_hbm, query_ref, sem)
        extra.start()
        extra.wait()
        emb_ref[...] = emb_ref[...] + query_ref[...]

    own_ref[...] = emb_ref[: own_ref.shape[0], :]
    head_dim = width // heads
    rows = min(ROWS_AT_ONCE, count)
    for first in range(0, count, rows):
        normed = normalise(emb_ref[first : first + rows, :], gain_ref[...])
        projected = jnp.dot(normed, proj_ref[:, :width], preferred_element_type=F32)
        query = silu(projected).astype(BF16) * jnp.asarray(0.5 * head_dim**-0.5, BF16)
        query_ref[first : first + rows, :] = query
        later_ref[first : first + rows, :] = query[:, split * LANES :]
    parts = [caches[k * blocks : (k + 1) * blocks] for k in range(3)]
    attend_groups(query_ref, parts, range(split), heads, keep_ref, send_ref)


def attend_later_kernel(query_ref, *refs, heads, blocks, split):
    *caches, keep_ref, send_ref = refs
    parts = [caches[k * blocks : (k + 1) * blocks] for k in range(3)]
    attend_groups(query_ref, parts, range(split, parts[0][0].shape[1] // LANES), heads, keep_ref, send_ref)


def attention_cost(count, columns, keys, head_dim):
    events = len(keys) * keys[0].shape[0]
    return pl.CostEstimate(
        flops=8 * count * columns * events,
        transcendentals=count * columns // head_dim * events,
        bytes_accessed=4 * columns * events,
    )


def attend_first(rounds, pick, pieces, extra, gain, proj, keys, values, biases, heads, each, split):
    count, width = extra.shape
    columns = split * LANES
    blocks = len(keys)
    return pl.pallas_call(
        functools.partial(attend_first_kernel, heads=heads, blocks=blocks, split=split),
        out_shape=(
            jax.ShapeDtypeStruct((each, width), BF16),
            jax.ShapeDtypeStruct((count // 2, columns), F32),
            jax.ShapeDtypeStruct((count // 2, columns), BF16),
            jax.ShapeDtypeStruct((count, width - columns), BF16),
        ),
        in_specs=[SMEM, VMEM] + [VMEM] * len(pieces) + [HBM] + [VMEM] * (2 + 3 * blocks),
        out_specs=(VMEM,) * 4,
        scratch_shapes=[
            pltpu.VMEM((count, width), BF16),
            pltpu.VMEM((count, width), BF16),
            pltpu.SemaphoreType.DMA,
        ],
        compiler_params=params(20),
        cost_estimate=attention_cost(count, columns, keys, width // heads),
        name="attend_first",
    )(rounds, pick, *pieces, extra, gain, proj, *keys, *values, *biases)


def attend_later(queries, keys, values, biases, heads, split):
    count, columns = queries.shape
    blocks = len(keys)
    return pl.pallas_call(
        functools.partial(attend_later_kernel, heads=heads, blocks=blocks, split=split),
        out_shape=(
            jax.ShapeDtypeStruct((count // 2, columns), F32),
            jax.ShapeDtypeStruct((count // 2, columns), BF16),
        ),
        in_specs=[VMEM] * (1 + 3 * blocks),
        out_specs=(VMEM, VMEM),
        compiler_params=params(20),
        cost_estimate=attention_cost(count, columns, keys, keys[0].shape[1] // heads),
        name="attend_later",
    )(queries, *keys, *values, *biases)


def combine_kernel(*refs, count):
    halves, (own_ref, *go_refs) = refs[:count], refs[count:]
    rows = own_ref.shape[0]
    for k, out_ref in enumerate([own_ref, *go_refs]):
        at = 0
        for keep_ref, came_ref in zip(halves[::2], halves[1::2]):
            to = at + keep_ref.shape[1]
            block = slice(k * rows, (k + 1) * rows)
            total = keep_ref[block, :] + came_ref[block, :].astype(F32)
            out_ref[:, at:to] = total.astype(out_ref.dtype)
            at = to


def combine(halves, blocks):
    rows = halves[0].shape[0] // blocks
    width = sum(h.shape[1] for h in halves[::2])
    return pl.pallas_call(
        functools.partial(combine_kernel, count=len(halves)),
        out_shape=tuple(jax.ShapeDtypeStruct((rows, width), BF16 if k else F32) for k in range(blocks)),
        in_specs=[VMEM] * len(halves),
        out_specs=(VMEM,) * blocks,
        compiler_params=params(12),
        name="combine",
    )(*halves)


def stage_kernel(*refs, width):
    *refs, sems = refs
    count = len(refs) // 2
    copies = [
        pltpu.make_async_copy(
            a if a.shape[1] == width else a.at[:, pl.ds(0, width)], b, sems.at[k]
        )
        for k, (a, b) in enumerate(zip(refs[:count], refs[count:]))
    ]
    for c in copies:
        c.start()
    for c in copies:
        c.wait()


def stage(width, *arrays, held=True):
    return pl.pallas_call(
        functools.partial(stage_kernel, width=width),
        out_shape=tuple(jax.ShapeDtypeStruct((a.shape[0], width), BF16) for a in arrays),
        in_specs=[HBM if held else pl.BlockSpec(memory_space=pl.ANY)] * len(arrays),
        out_specs=(VMEM,) * len(arrays),
        scratch_shapes=[pltpu.SemaphoreType.DMA((len(arrays),))],
        compiler_params=params(4),
        name="stage",
    )(*(pltpu.with_memory_space_constraint(a, pltpu.HBM) if held else a for a in arrays))


def gates_kernel(emb_ref, gain_ref, proj_ref, out_ref):
    normed = normalise(emb_ref[...], gain_ref[...])
    projected = jnp.dot(normed, proj_ref[...], preferred_element_type=F32)
    out_ref[...] = silu(projected).astype(BF16)


def gates_of(embedded, gain, proj_in):
    return pl.pallas_call(
        gates_kernel,
        out_shape=jax.ShapeDtypeStruct(embedded.shape, BF16),
        grid=(1,),
        in_specs=[VMEM, VMEM, pl.BlockSpec(proj_in.shape[:1] * 2, lambda i: (0, 1))],
        out_specs=VMEM,
        compiler_params=params(16),
        cost_estimate=pl.CostEstimate(flops=1 << 26, transcendentals=1 << 14, bytes_accessed=1 << 22),
        name="gates",
    )(embedded, gain, proj_in)


def finish_kernel(own_ref, *refs):
    *parts, emb_ref, gates_ref, gain_ref, proj_ref, out_ref = refs
    attended = own_ref[...]
    for p in parts:
        attended = attended + p[...].astype(F32)
    centred = attended - jnp.mean(attended, axis=-1, keepdims=True)
    variance = jnp.mean(centred * centred, axis=-1, keepdims=True)
    gated = centred * lax.rsqrt(variance + 1e-05) * gain_ref[...] * gates_ref[...].astype(F32)
    product = jnp.dot(gated.astype(BF16), proj_ref[...], preferred_element_type=F32)
    out_ref[...] = (emb_ref[...].astype(F32) + product).astype(BF16)


def finish(own, parts, embedded, gates, gain, proj_out):
    return pl.pallas_call(
        finish_kernel,
        out_shape=jax.ShapeDtypeStruct(embedded.shape, BF16),
        in_specs=[VMEM] * (len(parts) + 5),
        out_specs=VMEM,
        compiler_params=params(16),
        name="finish",
    )(own, *parts, embedded, gates, gain, proj_out)


def on_device(
    item_ids,
    item_table,
    key_cache,
    value_cache,
    time_buckets,
    window_start,
    norm_gain,
    proj_in,
    time_bias,
    pos_bias,
    out_gain,
    proj_out,
):
    axis = "hist"
    size = lax.axis_size(axis)
    each = item_ids.shape[0]
    slots = 2 * each
    heads = time_bias.shape[0]
    events, width = key_cache.shape
    table_rows = item_table.shape[0]
    gain = norm_gain[None, :]

    def partners(x):
        return swap(x, PARTNER, axis, size)

    other_table = partners(item_table)
    other_keys = partners(key_cache)
    other_values = partners(value_cache)
    bias, own_table = prepare(
        window_start, time_buckets[None, :], time_bias, pos_bias, item_table, axis, 2 * events * size
    )
    other_bias = partners(bias)
    ids = gather_relative(item_ids[None, :], 1, axis, size)

    (near_table,) = stage(width, other_table, held=False)
    found = lookup(ids, [own_table, near_table], slots, axis, size)
    pieces = gather_rows(found, axis, size)
    pick, rounds = plan(ids, slots, table_rows, axis, size)

    def more(state):
        turn, so_far = state
        picked, _ = plan(ids, slots, table_rows, axis, size, turn[None])
        found = lookup(ids, [item_table, other_table], slots, axis, size, turn[None])
        return turn + 1, so_far + select(picked, gather_rows(found, axis, size))

    none = jnp.zeros((each * (size // 2), width), BF16)
    _, extra = lax.while_loop(lambda s: s[0] < rounds[0], more, (jnp.int32(1), none))

    (proj,) = stage(width, proj_in)
    keys, values, other_keys, other_values = stage(width, key_cache, value_cache, other_keys, other_values)
    caches = ([keys, other_keys], [values, other_values], [bias, other_bias])
    *far, near = stage_masks(size)
    split = max(1, width // LANES * 7 // 8)
    own, keep, send, later = attend_first(rounds, pick, pieces, extra, gain, proj, *caches, heads, each, split)
    halves = [keep, swap(send, near[0], axis, size)]
    keep, send = attend_later(later, *caches, heads, split)
    halves += [keep, swap(send, near[0], axis, size)]
    gates = gates_of(own, gain, proj_in)

    total, *going = combine(halves, len(combos(far[-1])))
    for bits in far[::-1]:
        parts = [swap(g, m, axis, size) for g, m in zip(going, combos(bits)[1:])]
        if bits is far[0]:
            break
        total, *going = combine([total, sum(p.astype(F32) for p in parts)], len(combos(bits)))
    return finish(total, parts, own, gates, out_gain[None, :], proj_out)


def solution(mesh):
    placed = (
        P(("grp", "hist")),
        P("hist", None),
        P(("grp", "hist"), None),
        P(("grp", "hist"), None),
        P(("grp", "hist")),
        P("grp"),
        P(),
        P(),
        P(),
        P(),
        P(),
        P(),
    )

    return jax.shard_map(on_device, mesh=mesh, in_specs=placed, out_specs=P(("grp", "hist"), None), check_vma=False)
```

```python
import functools

import jax
import jax.numpy as jnp
from jax import lax
from jax.experimental import pallas as pl
from jax.experimental.pallas import tpu as pltpu
from jax.sharding import PartitionSpec as P


BF16 = jnp.bfloat16
F32 = jnp.float32
LANES = 128
ROWS_AT_ONCE = 128
EVENTS_AT_ONCE = 512
STEPS_AHEAD = 2
STAGE_COPIES = 4
BLOCK = 16
TN = (((0,), (0,)), ((), ()))
NT = (((1,), (1,)), ((), ()))
VMEM = pl.BlockSpec(memory_space=pltpu.VMEM)
SMEM = pl.BlockSpec(memory_space=pltpu.SMEM)
HBM = pl.BlockSpec(memory_space=pltpu.HBM)


def params(mib):
    return pltpu.CompilerParams(vmem_limit_bytes=mib << 20)


PARTNER = 1


def stage_masks(size):
    bits = [1 << k for k in range(1, size.bit_length() - 1)][::-1]
    far = bits[:-1]
    return [sorted(far[k : k + 2]) for k in range(0, len(far), 2)] + [bits[-1:]]


def combos(bits):
    out = [0]
    for b in bits:
        out = out + [m | b for m in out]
    return out


def swap(x, mask, axis, size):
    return lax.ppermute(x, axis, [(i, i ^ mask) for i in range(size)])


def join_kernel(*refs):
    *parts, out_ref = refs
    rows = parts[0].shape[0]
    for k, p in enumerate(parts):
        out_ref[k * rows : (k + 1) * rows, :] = p[...]


def join(pieces, dim):
    if dim:
        return jnp.concatenate(pieces, axis=dim)
    rows, width = pieces[0].shape
    return pl.pallas_call(
        join_kernel,
        out_shape=jax.ShapeDtypeStruct((len(pieces) * rows, width), BF16),
        in_specs=[VMEM] * len(pieces),
        out_specs=VMEM,
        compiler_params=params(16),
        name="join",
    )(*pieces)


def gather_relative(x, dim, axis, size):
    *far, near = stage_masks(size)
    for bits in far:
        x = join([x] + [swap(x, m, axis, size) for m in combos(bits)[1:]], dim)
    return [x, swap(x, near[0], axis, size)]


def gather_rows(x, axis, size):
    *far, near = stage_masks(size)
    for bits in far[:-1]:
        x = join([x] + [swap(x, m, axis, size) for m in combos(bits)[1:]], 0)
    first, *rest = combos(far[-1])[1:]
    early = swap(x, near[0], axis, size)
    beside = swap(x, first, axis, size)
    others = join([swap(x, m, axis, size) for m in rest], 0)
    late = swap(others, near[0], axis, size)
    across = swap(early, first, axis, size)
    return [x, beside, others, early, across, late]


def position_bits(size):
    return [b for stage in stage_masks(size) for b in stage]


def candidates_info(ids_refs, me, size, table_rows):
    ids = jnp.concatenate([r[...] for r in ids_refs], axis=1)
    count = ids.shape[1]
    each = count // (size // 2)
    owner = ids // table_rows
    place = lax.broadcasted_iota(jnp.int32, (1, count), 1)
    block = place // each
    mask = jnp.zeros_like(place)
    for k, b in enumerate(position_bits(size)):
        mask = mask + ((block >> k) & 1) * b
    pair = owner >> 1
    key = pair * count + ((mask ^ me) >> 1) * each + place % each
    return pair, key, ids - owner * table_rows + ((owner ^ me) & 1) * table_rows


def to_column(row):
    count = row.shape[1]
    r = lax.broadcasted_iota(jnp.int32, (count, count), 0)
    c = lax.broadcasted_iota(jnp.int32, (count, count), 1)
    return jnp.sum(jnp.where(r == c, row, 0), axis=1, keepdims=True)


def lookup_kernel(*refs, axis, size, first_turn):
    if first_turn:
        *ids_refs, own_ref, other_ref, out_ref, blocks_ref = refs
        turn, copies = 0, []
    else:
        turn_ref, *ids_refs, own_hbm, other_hbm, out_ref, blocks_ref, own_ref, other_ref, sems = refs
        turn = turn_ref[0]
        copies = [
            pltpu.make_async_copy(own_hbm, own_ref, sems.at[0]),
            pltpu.make_async_copy(other_hbm, other_ref, sems.at[1]),
        ]
    for c in copies:
        c.start()
    me = lax.axis_index(axis)
    slots = out_ref.shape[0]
    rows = own_ref.shape[0]
    pair, key, offset = candidates_info(ids_refs, me, size, rows)
    count = pair.shape[1]
    key_col = to_column(key)
    before = (key_col < key) & (key_col >= pair * count)
    rank = jnp.sum(before.astype(jnp.int32), axis=0, keepdims=True)
    slot = lax.broadcasted_iota(jnp.int32, (slots, count), 0) + turn * slots
    hit = (pair == (me >> 1)) & (rank == slot)
    want = jnp.sum(jnp.where(hit, offset + 1, 0), axis=1, keepdims=True) - 1
    for c in copies:
        c.wait()
    near = jnp.where(want < 0, 0, want // BLOCK)
    for k in range(slots):
        block = near[k, 0]
        in_own = block < rows // BLOCK
        at = pl.multiple_of((block - jnp.where(in_own, 0, rows // BLOCK)) * BLOCK, BLOCK)
        own, other = own_ref[pl.ds(at, BLOCK), :], other_ref[pl.ds(at, BLOCK), :]
        blocks_ref[k * BLOCK : (k + 1) * BLOCK, :] = jnp.where(in_own, own, other)
    column = lax.broadcasted_iota(jnp.int32, (slots, slots * BLOCK), 1)
    line = lax.broadcasted_iota(jnp.int32, (slots, slots * BLOCK), 0)
    pick = (want >= 0) & (column == line * BLOCK + (want - near * BLOCK))
    found = jnp.dot(pick.astype(F32).astype(BF16), blocks_ref[...], preferred_element_type=F32)
    out_ref[...] = found.astype(BF16)


def lookup(ids, tables, slots, axis, size, turn=None):
    first_turn = turn is None
    if not first_turn:
        tables = [pltpu.with_memory_space_constraint(t, pltpu.HBM) for t in tables]
    rows, width = tables[0].shape
    return pl.pallas_call(
        functools.partial(lookup_kernel, axis=axis, size=size, first_turn=first_turn),
        out_shape=jax.ShapeDtypeStruct((slots, width), BF16),
        in_specs=([] if first_turn else [SMEM]) + [VMEM] * len(ids) + [VMEM if first_turn else HBM] * 2,
        out_specs=VMEM,
        scratch_shapes=[pltpu.VMEM((slots * BLOCK, width), BF16)]
        + ([] if first_turn else [pltpu.VMEM((rows, width), BF16)] * 2 + [pltpu.SemaphoreType.DMA((2,))]),
        compiler_params=params(16),
        name="lookup",
    )(*([] if first_turn else [turn]), *ids, *tables)


def plan_kernel(*refs, axis, size, slots, table_rows, first_turn):
    if first_turn:
        *ids_refs, pick_ref, rounds_ref, beside_ref = refs
        turn = 0
    else:
        turn_ref, *ids_refs, pick_ref, rounds_ref, beside_ref = refs
        turn = turn_ref[0]
    me = lax.axis_index(axis)
    pair, key, _ = candidates_info(ids_refs, me, size, table_rows)
    count = pair.shape[1]
    key_col = to_column(key)
    pair_col = key_col // count
    before = (key < key_col) & (key >= pair_col * count)
    rank = jnp.sum(before.astype(jnp.int32), axis=1, keepdims=True)
    rounds = jnp.max(rank) // slots + 1
    rounds_ref[0] = rounds
    beside_ref[...] = jnp.full(beside_ref.shape, rounds, jnp.int32)
    away = pair_col ^ (me >> 1)
    block = jnp.zeros_like(away)
    for k, b in enumerate(position_bits(size)):
        block = block + jnp.where((away & (b >> 1)) != 0, 1 << k, 0)
    mine = rank - turn * slots
    slot = jnp.where((mine >= 0) & (mine < slots), block * slots + mine, -1)
    pick = slot == lax.broadcasted_iota(jnp.int32, pick_ref.shape, 1)
    pick_ref[...] = pick.astype(F32).astype(BF16)


def plan(ids, slots, table_rows, axis, size, turn=None):
    count = sum(i.shape[1] for i in ids)
    first_turn = turn is None
    return pl.pallas_call(
        functools.partial(
            plan_kernel, axis=axis, size=size, slots=slots, table_rows=table_rows, first_turn=first_turn
        ),
        out_shape=(
            jax.ShapeDtypeStruct((count, size // 2 * slots), BF16),
            jax.ShapeDtypeStruct((1,), jnp.int32),
            jax.ShapeDtypeStruct((8, LANES), jnp.int32),
        ),
        in_specs=([] if first_turn else [SMEM]) + [VMEM] * len(ids),
        out_specs=(VMEM, SMEM, VMEM),
        compiler_params=params(16),
        name="plan",
    )(*([] if first_turn else [turn]), *ids)


def select_kernel(pick_ref, rows_ref, out_ref):
    out_ref[...] = jnp.dot(pick_ref[...], rows_ref[...], preferred_element_type=F32).astype(BF16)


def select(pick, pieces):
    rows = jnp.concatenate(pieces, axis=0)
    return pl.pallas_call(
        select_kernel,
        out_shape=jax.ShapeDtypeStruct((pick.shape[0], rows.shape[1]), BF16),
        in_specs=[VMEM, VMEM],
        out_specs=VMEM,
        compiler_params=params(12),
        name="select",
    )(pick, rows)


def three_parts(x):
    high = x.astype(BF16)
    rest = x - high.astype(F32)
    middle = rest.astype(BF16)
    return [high, middle, (rest - middle.astype(F32)).astype(BF16)]


def prepare_kernel(
    start_ref, times_hbm, time_bias_hbm, pos_bias_hbm, table_hbm, out_ref, table_ref,
    times_ref, time_bias_ref, pos_bias_ref, sems, *, axis, npos, history
):
    pairs = ((times_hbm, times_ref), (time_bias_hbm, time_bias_ref), (pos_bias_hbm, pos_bias_ref), (table_hbm, table_ref))
    copies = [pltpu.make_async_copy(a, b, sems.at[k]) for k, (a, b) in enumerate(pairs)]
    for c in copies:
        c.start()
    events = times_ref.shape[1]
    first = history - start_ref[0] - lax.axis_index(axis) * events
    distance = first - lax.broadcasted_iota(jnp.int32, (1, events), 1)
    bucket = jnp.zeros((1, events), jnp.int32)
    for k in range(1, npos):
        bucket = bucket + (distance >= (1 << k)).astype(jnp.int32)
    for c in copies[:3]:
        c.wait()
    columns = []
    for table_ref_, index in ((time_bias_ref, times_ref[...]), (pos_bias_ref, bucket)):
        table = jnp.concatenate(three_parts(table_ref_[...] * 0.5), axis=0)
        kinds = table.shape[1]
        hot = lax.broadcasted_iota(jnp.int32, (kinds, events), 0) == index
        columns.append(jnp.dot(table, hot.astype(F32).astype(BF16), preferred_element_type=F32))
    used = sum(c.shape[0] for c in columns)
    columns.append(jnp.zeros((LANES - used, events), F32))
    out_ref[...] = jnp.concatenate(columns, axis=0).T.astype(BF16)
    copies[3].wait()


def prepare(start, times, time_bias, pos_bias, table, axis, history):
    arrays = [times, time_bias, pos_bias, table]
    return pl.pallas_call(
        functools.partial(prepare_kernel, axis=axis, npos=pos_bias.shape[1], history=history),
        out_shape=(
            jax.ShapeDtypeStruct((times.shape[1], LANES), BF16),
            jax.ShapeDtypeStruct(table.shape, BF16),
        ),
        in_specs=[SMEM] + [HBM] * 4,
        out_specs=(VMEM, VMEM),
        scratch_shapes=[pltpu.VMEM(a.shape, a.dtype) for a in arrays[:3]] + [pltpu.SemaphoreType.DMA((4,))],
        compiler_params=params(8),
        name="prepare",
    )(start, *(pltpu.with_memory_space_constraint(a, pltpu.HBM) for a in arrays))


def silu(x):
    return x / (1.0 + jnp.exp(-x))


def normalise(embedded, gain):
    x = embedded.astype(F32)
    meansq = jnp.mean(x * x, axis=-1, keepdims=True)
    return (x * lax.rsqrt(meansq + 1e-06) * gain).astype(BF16)


def attend_groups(query_ref, caches, groups, heads, keep_ref, send_ref):
    keys, values, biases = caches
    count = query_ref.shape[0]
    width = keys[0].shape[1]
    head_dim = width // heads
    per = LANES // head_dim
    half = count // 2
    rows = min(ROWS_AT_ONCE, count)
    events = keys[0].shape[0]
    step = min(EVENTS_AT_ONCE, events)
    base = groups[0]
    for first in range(0, count, rows):
        lane = lax.broadcasted_iota(jnp.int32, (rows, LANES), 1)
        stacks = {}

        def stack(group):
            if group not in stacks:
                at = (group - base) * LANES
                part = query_ref[first : first + rows, at : at + LANES]
                zero, one = jnp.zeros_like(part), jnp.ones_like(part)
                blocks = []
                for k in range(per):
                    own = jnp.where(lane // head_dim == k, part, zero)
                    chosen = jnp.where(lane % heads == group * per + k, one, zero)
                    blocks.append(jnp.concatenate([own, chosen], axis=1))
                stacks[group] = jnp.concatenate(blocks, axis=0)
            return stacks[group]

        def halves(group, block, j):
            at = slice(group * LANES, (group + 1) * LANES)
            left = jnp.concatenate([keys[block][j : j + step, at], biases[block][j : j + step, :]], axis=1)
            return lax.dot_general(left, stack(group), NT, preferred_element_type=F32)

        steps = [
            (group, block, j) for group in groups for block in range(len(keys)) for j in range(0, events, step)
        ]
        ahead = [halves(*s) for s in steps[:STEPS_AHEAD]]
        total = None
        for n, (group, block, j) in enumerate(steps):
            if n + STEPS_AHEAD < len(steps):
                ahead.append(halves(*steps[n + STEPS_AHEAD]))
            t = ahead.pop(0)
            weights = (t + t * jnp.tanh(t)).astype(BF16)
            at = slice(group * LANES, (group + 1) * LANES)
            term = lax.dot_general(values[block][j : j + step, at], weights, TN, preferred_element_type=F32)
            total = term if total is None else total + term
            if n + 1 < len(steps) and steps[n + 1][0] == group:
                continue
            out = jnp.concatenate(
                [total[k * head_dim : (k + 1) * head_dim, k * rows : (k + 1) * rows] for k in range(per)], axis=0
            ).T
            total = None
            at = slice((group - base) * LANES, (group - base + 1) * LANES)
            if first + rows <= half:
                keep_ref[first : first + rows, at] = out
            elif first >= half:
                send_ref[first - half : first - half + rows, at] = out.astype(BF16)
            else:
                keep_ref[first:half, at] = out[: half - first]
                send_ref[: first + rows - half, at] = out[half - first :].astype(BF16)


def attend_first_kernel(rounds_ref, pick_ref, *refs, heads, blocks, split):
    *row_refs, extra_hbm, gain_ref, proj_ref = refs[: -7 - 3 * blocks]
    caches = refs[-7 - 3 * blocks : -7]
    own_ref, keep_ref, send_ref, later_ref, emb_ref, query_ref, sem = refs[-7:]
    count, width = emb_ref.shape
    rows = jnp.concatenate([r[...] for r in row_refs], axis=0)
    emb_ref[...] = jnp.dot(pick_ref[...], rows, preferred_element_type=F32).astype(BF16)


    @pl.when(jnp.max(rounds_ref[...]) > 1)
    def _():
        extra = pltpu.make_async_copy(extra_hbm, query_ref, sem)
        extra.start()
        extra.wait()
        emb_ref[...] = emb_ref[...] + query_ref[...]

    own_ref[...] = emb_ref[: own_ref.shape[0], :]
    head_dim = width // heads
    rows = min(ROWS_AT_ONCE, count)
    for first in range(0, count, rows):
        normed = normalise(emb_ref[first : first + rows, :], gain_ref[...])
        projected = jnp.dot(normed, proj_ref[:, :width], preferred_element_type=F32)
        query = silu(projected).astype(BF16) * jnp.asarray(0.5 * head_dim**-0.5, BF16)
        query_ref[first : first + rows, :] = query
        later_ref[first : first + rows, :] = query[:, split * LANES :]
    parts = [caches[k * blocks : (k + 1) * blocks] for k in range(3)]
    attend_groups(query_ref, parts, range(split), heads, keep_ref, send_ref)


def attend_later_kernel(query_ref, *refs, heads, blocks, split):
    *caches, keep_ref, send_ref = refs
    parts = [caches[k * blocks : (k + 1) * blocks] for k in range(3)]
    attend_groups(query_ref, parts, range(split, parts[0][0].shape[1] // LANES), heads, keep_ref, send_ref)


def attention_cost(count, columns, keys, head_dim):
    events = len(keys) * keys[0].shape[0]
    return pl.CostEstimate(
        flops=8 * count * columns * events,
        transcendentals=count * columns // head_dim * events,
        bytes_accessed=4 * columns * events,
    )


def attend_first(rounds, pick, pieces, extra, gain, proj, keys, values, biases, heads, each, split):
    count, width = extra.shape
    columns = split * LANES
    blocks = len(keys)
    return pl.pallas_call(
        functools.partial(attend_first_kernel, heads=heads, blocks=blocks, split=split),
        out_shape=(
            jax.ShapeDtypeStruct((each, width), BF16),
            jax.ShapeDtypeStruct((count // 2, columns), F32),
            jax.ShapeDtypeStruct((count // 2, columns), BF16),
            jax.ShapeDtypeStruct((count, width - columns), BF16),
        ),
        in_specs=[VMEM, VMEM] + [VMEM] * len(pieces) + [HBM] + [VMEM] * (2 + 3 * blocks),
        out_specs=(VMEM,) * 4,
        scratch_shapes=[
            pltpu.VMEM((count, width), BF16),
            pltpu.VMEM((count, width), BF16),
            pltpu.SemaphoreType.DMA,
        ],
        compiler_params=params(20),
        cost_estimate=attention_cost(count, columns, keys, width // heads),
        name="attend_first",
    )(rounds, pick, *pieces, extra, gain, proj, *keys, *values, *biases)


def attend_later(queries, keys, values, biases, heads, split):
    count, columns = queries.shape
    blocks = len(keys)
    return pl.pallas_call(
        functools.partial(attend_later_kernel, heads=heads, blocks=blocks, split=split),
        out_shape=(
            jax.ShapeDtypeStruct((count // 2, columns), F32),
            jax.ShapeDtypeStruct((count // 2, columns), BF16),
        ),
        in_specs=[VMEM] * (1 + 3 * blocks),
        out_specs=(VMEM, VMEM),
        compiler_params=params(20),
        cost_estimate=attention_cost(count, columns, keys, keys[0].shape[1] // heads),
        name="attend_later",
    )(queries, *keys, *values, *biases)


def combine_kernel(*refs, count):
    halves, (own_ref, *go_refs) = refs[:count], refs[count:]
    rows = own_ref.shape[0]
    for k, out_ref in enumerate([own_ref, *go_refs]):
        at = 0
        for keep_ref, came_ref in zip(halves[::2], halves[1::2]):
            to = at + keep_ref.shape[1]
            block = slice(k * rows, (k + 1) * rows)
            total = keep_ref[block, :] + came_ref[block, :].astype(F32)
            out_ref[:, at:to] = total.astype(out_ref.dtype)
            at = to


def combine(halves, blocks):
    rows = halves[0].shape[0] // blocks
    width = sum(h.shape[1] for h in halves[::2])
    return pl.pallas_call(
        functools.partial(combine_kernel, count=len(halves)),
        out_shape=tuple(jax.ShapeDtypeStruct((rows, width), BF16 if k else F32) for k in range(blocks)),
        in_specs=[VMEM] * len(halves),
        out_specs=(VMEM,) * blocks,
        compiler_params=params(12),
        name="combine",
    )(*halves)


def stage_kernel(*refs, width):
    *refs, sems = refs
    count = len(refs) // 2
    copies = []
    for k, (a, b) in enumerate(zip(refs[:count], refs[count:])):
        rows = a.shape[0] // STAGE_COPIES
        for c in range(STAGE_COPIES):
            part = pl.ds(c * rows, rows)
            copies.append(pltpu.make_async_copy(a.at[part, pl.ds(0, width)], b.at[part, :], sems.at[k, c]))
    for c in copies:
        c.start()
    for c in copies:
        c.wait()


def stage(width, *arrays, held=True):
    return pl.pallas_call(
        functools.partial(stage_kernel, width=width),
        out_shape=tuple(jax.ShapeDtypeStruct((a.shape[0], width), BF16) for a in arrays),
        in_specs=[HBM if held else pl.BlockSpec(memory_space=pl.ANY)] * len(arrays),
        out_specs=(VMEM,) * len(arrays),
        scratch_shapes=[pltpu.SemaphoreType.DMA((len(arrays), STAGE_COPIES))],
        compiler_params=params(4),
        name="stage",
    )(*(pltpu.with_memory_space_constraint(a, pltpu.HBM) if held else a for a in arrays))


def gates_kernel(emb_ref, gain_ref, proj_ref, out_ref):
    normed = normalise(emb_ref[...], gain_ref[...])
    projected = jnp.dot(normed, proj_ref[...], preferred_element_type=F32)
    out_ref[...] = silu(projected).astype(BF16)


def gates_of(embedded, gain, proj_in):
    return pl.pallas_call(
        gates_kernel,
        out_shape=jax.ShapeDtypeStruct(embedded.shape, BF16),
        grid=(1,),
        in_specs=[VMEM, VMEM, pl.BlockSpec(proj_in.shape[:1] * 2, lambda i: (0, 1))],
        out_specs=VMEM,
        compiler_params=params(16),
        cost_estimate=pl.CostEstimate(flops=1 << 26, transcendentals=1 << 14, bytes_accessed=1 << 22),
        name="gates",
    )(embedded, gain, proj_in)


def finish_kernel(own_ref, *refs):
    *parts, emb_ref, gates_ref, gain_ref, proj_ref, out_ref = refs
    attended = own_ref[...]
    for p in parts:
        attended = attended + p[...].astype(F32)
    centred = attended - jnp.mean(attended, axis=-1, keepdims=True)
    variance = jnp.mean(centred * centred, axis=-1, keepdims=True)
    gated = centred * lax.rsqrt(variance + 1e-05) * gain_ref[...] * gates_ref[...].astype(F32)
    product = jnp.dot(gated.astype(BF16), proj_ref[...], preferred_element_type=F32)
    out_ref[...] = (emb_ref[...].astype(F32) + product).astype(BF16)


def finish(own, parts, embedded, gates, gain, proj_out):
    return pl.pallas_call(
        finish_kernel,
        out_shape=jax.ShapeDtypeStruct(embedded.shape, BF16),
        in_specs=[VMEM] * (len(parts) + 5),
        out_specs=VMEM,
        compiler_params=params(16),
        name="finish",
    )(own, *parts, embedded, gates, gain, proj_out)


def on_device(
    item_ids,
    item_table,
    key_cache,
    value_cache,
    time_buckets,
    window_start,
    norm_gain,
    proj_in,
    time_bias,
    pos_bias,
    out_gain,
    proj_out,
):
    axis = "hist"
    size = lax.axis_size(axis)
    each = item_ids.shape[0]
    slots = 2 * each
    heads = time_bias.shape[0]
    events, width = key_cache.shape
    table_rows = item_table.shape[0]
    gain = norm_gain[None, :]

    def partners(x):
        return swap(x, PARTNER, axis, size)

    other_table = partners(item_table)
    other_keys = partners(key_cache)
    other_values = partners(value_cache)
    bias, own_table = prepare(
        window_start, time_buckets[None, :], time_bias, pos_bias, item_table, axis, 2 * events * size
    )
    other_bias = partners(bias)
    ids = gather_relative(item_ids[None, :], 1, axis, size)

    (near_table,) = stage(width, other_table, held=False)
    found = lookup(ids, [own_table, near_table], slots, axis, size)
    pieces = gather_rows(found, axis, size)
    pick, rounds, told = plan(ids, slots, table_rows, axis, size)

    def more(state):
        turn, so_far = state
        picked, *_ = plan(ids, slots, table_rows, axis, size, turn[None])
        found = lookup(ids, [item_table, other_table], slots, axis, size, turn[None])
        return turn + 1, so_far + select(picked, gather_rows(found, axis, size))

    none = jnp.zeros((each * (size // 2), width), BF16)
    _, extra = lax.while_loop(lambda s: s[0] < rounds[0], more, (jnp.int32(1), none))

    (keys,) = stage(width, key_cache)
    proj, values, other_keys, other_values = stage(width, proj_in, value_cache, other_keys, other_values)
    caches = ([keys, other_keys], [values, other_values], [bias, other_bias])
    *far, near = stage_masks(size)
    split = max(1, width // LANES * 7 // 8)
    own, keep, send, later = attend_first(told, pick, pieces, extra, gain, proj, *caches, heads, each, split)
    halves = [keep, swap(send, near[0], axis, size)]
    keep, send = attend_later(later, *caches, heads, split)
    halves += [keep, swap(send, near[0], axis, size)]
    gates = gates_of(own, gain, proj_in)

    total, *going = combine(halves, len(combos(far[-1])))
    for bits in far[::-1]:
        parts = [swap(g, m, axis, size) for g, m in zip(going, combos(bits)[1:])]
        if bits is far[0]:
            break
        total, *going = combine([total, sum(p.astype(F32) for p in parts)], len(combos(bits)))
    return finish(total, parts, own, gates, out_gain[None, :], proj_out)


def solution(mesh):
    placed = (
        P(("grp", "hist")),
        P("hist", None),
        P(("grp", "hist"), None),
        P(("grp", "hist"), None),
        P(("grp", "hist")),
        P("grp"),
        P(),
        P(),
        P(),
        P(),
        P(),
        P(),
    )

    return jax.shard_map(on_device, mesh=mesh, in_specs=placed, out_specs=P(("grp", "hist"), None), check_vma=False)
```

```python
import functools

import jax
import jax.numpy as jnp
from jax import lax
from jax.experimental import pallas as pl
from jax.experimental.pallas import tpu as pltpu
from jax.sharding import PartitionSpec as P


BF16 = jnp.bfloat16
F32 = jnp.float32
LANES = 128
ROWS_AT_ONCE = 128
EVENTS_AT_ONCE = 512
STEPS_AHEAD = 2
BLOCK = 16
TN = (((0,), (0,)), ((), ()))
NT = (((1,), (1,)), ((), ()))
VMEM = pl.BlockSpec(memory_space=pltpu.VMEM)
SMEM = pl.BlockSpec(memory_space=pltpu.SMEM)
HBM = pl.BlockSpec(memory_space=pltpu.HBM)


def params(mib):
    return pltpu.CompilerParams(vmem_limit_bytes=mib << 20)


PARTNER = 1


def stage_masks(size):
    bits = [1 << k for k in range(1, size.bit_length() - 1)][::-1]
    far = bits[:-1]
    return [sorted(far[k : k + 2]) for k in range(0, len(far), 2)] + [bits[-1:]]


def combos(bits):
    out = [0]
    for b in bits:
        out = out + [m | b for m in out]
    return out


def swap(x, mask, axis, size):
    return lax.ppermute(x, axis, [(i, i ^ mask) for i in range(size)])


def join_kernel(*refs):
    *parts, out_ref = refs
    rows = parts[0].shape[0]
    for k, p in enumerate(parts):
        out_ref[k * rows : (k + 1) * rows, :] = p[...]


def join(pieces, dim):
    if dim:
        return jnp.concatenate(pieces, axis=dim)
    rows, width = pieces[0].shape
    return pl.pallas_call(
        join_kernel,
        out_shape=jax.ShapeDtypeStruct((len(pieces) * rows, width), BF16),
        in_specs=[VMEM] * len(pieces),
        out_specs=VMEM,
        compiler_params=params(16),
        name="join",
    )(*pieces)


def gather_relative(x, dim, axis, size):
    *far, near = stage_masks(size)
    for bits in far:
        x = join([x] + [swap(x, m, axis, size) for m in combos(bits)[1:]], dim)
    return [x, swap(x, near[0], axis, size)]


def gather_rows(x, axis, size):
    *far, near = stage_masks(size)
    for bits in far[:-1]:
        x = join([x] + [swap(x, m, axis, size) for m in combos(bits)[1:]], 0)
    first, *rest = combos(far[-1])[1:]
    early = swap(x, near[0], axis, size)
    beside = swap(x, first, axis, size)
    others = join([swap(x, m, axis, size) for m in rest], 0)
    late = swap(others, near[0], axis, size)
    across = swap(early, first, axis, size)
    return [x, beside, others, early, across, late]


def position_bits(size):
    return [b for stage in stage_masks(size) for b in stage]


def candidates_info(ids_refs, me, size, table_rows):
    ids = jnp.concatenate([r[...] for r in ids_refs], axis=1)
    count = ids.shape[1]
    each = count // (size // 2)
    owner = ids // table_rows
    place = lax.broadcasted_iota(jnp.int32, (1, count), 1)
    block = place // each
    mask = jnp.zeros_like(place)
    for k, b in enumerate(position_bits(size)):
        mask = mask + ((block >> k) & 1) * b
    pair = owner >> 1
    key = pair * count + ((mask ^ me) >> 1) * each + place % each
    return pair, key, ids - owner * table_rows + ((owner ^ me) & 1) * table_rows


def to_column(row):
    count = row.shape[1]
    r = lax.broadcasted_iota(jnp.int32, (count, count), 0)
    c = lax.broadcasted_iota(jnp.int32, (count, count), 1)
    return jnp.sum(jnp.where(r == c, row, 0), axis=1, keepdims=True)


def lookup_kernel(*refs, axis, size, first_turn):
    if first_turn:
        *ids_refs, own_ref, other_ref, out_ref, blocks_ref = refs
        turn, copies = 0, []
    else:
        turn_ref, *ids_refs, own_hbm, other_hbm, out_ref, blocks_ref, own_ref, other_ref, sems = refs
        turn = turn_ref[0]
        copies = [
            pltpu.make_async_copy(own_hbm, own_ref, sems.at[0]),
            pltpu.make_async_copy(other_hbm, other_ref, sems.at[1]),
        ]
    for c in copies:
        c.start()
    me = lax.axis_index(axis)
    slots = out_ref.shape[0]
    rows = own_ref.shape[0]
    pair, key, offset = candidates_info(ids_refs, me, size, rows)
    count = pair.shape[1]
    key_col = to_column(key)
    before = (key_col < key) & (key_col >= pair * count)
    rank = jnp.sum(before.astype(jnp.int32), axis=0, keepdims=True)
    slot = lax.broadcasted_iota(jnp.int32, (slots, count), 0) + turn * slots
    hit = (pair == (me >> 1)) & (rank == slot)
    want = jnp.sum(jnp.where(hit, offset + 1, 0), axis=1, keepdims=True) - 1
    for c in copies:
        c.wait()
    near = jnp.where(want < 0, 0, want // BLOCK)
    for k in range(slots):
        block = near[k, 0]
        in_own = block < rows // BLOCK
        at = pl.multiple_of((block - jnp.where(in_own, 0, rows // BLOCK)) * BLOCK, BLOCK)
        own, other = own_ref[pl.ds(at, BLOCK), :], other_ref[pl.ds(at, BLOCK), :]
        blocks_ref[k * BLOCK : (k + 1) * BLOCK, :] = jnp.where(in_own, own, other)
    column = lax.broadcasted_iota(jnp.int32, (slots, slots * BLOCK), 1)
    line = lax.broadcasted_iota(jnp.int32, (slots, slots * BLOCK), 0)
    pick = (want >= 0) & (column == line * BLOCK + (want - near * BLOCK))
    found = jnp.dot(pick.astype(F32).astype(BF16), blocks_ref[...], preferred_element_type=F32)
    out_ref[...] = found.astype(BF16)


def lookup(ids, tables, slots, axis, size, turn=None):
    first_turn = turn is None
    if not first_turn:
        tables = [pltpu.with_memory_space_constraint(t, pltpu.HBM) for t in tables]
    rows, width = tables[0].shape
    return pl.pallas_call(
        functools.partial(lookup_kernel, axis=axis, size=size, first_turn=first_turn),
        out_shape=jax.ShapeDtypeStruct((slots, width), BF16),
        in_specs=([] if first_turn else [SMEM]) + [VMEM] * len(ids) + [VMEM if first_turn else HBM] * 2,
        out_specs=VMEM,
        scratch_shapes=[pltpu.VMEM((slots * BLOCK, width), BF16)]
        + ([] if first_turn else [pltpu.VMEM((rows, width), BF16)] * 2 + [pltpu.SemaphoreType.DMA((2,))]),
        compiler_params=params(16),
        name="lookup",
    )(*([] if first_turn else [turn]), *ids, *tables)


def plan_kernel(*refs, axis, size, slots, table_rows, first_turn):
    if first_turn:
        *ids_refs, pick_ref, rounds_ref, beside_ref = refs
        turn = 0
    else:
        turn_ref, *ids_refs, pick_ref, rounds_ref, beside_ref = refs
        turn = turn_ref[0]
    me = lax.axis_index(axis)
    pair, key, _ = candidates_info(ids_refs, me, size, table_rows)
    count = pair.shape[1]
    key_col = to_column(key)
    pair_col = key_col // count
    before = (key < key_col) & (key >= pair_col * count)
    rank = jnp.sum(before.astype(jnp.int32), axis=1, keepdims=True)
    rounds = jnp.max(rank) // slots + 1
    rounds_ref[0] = rounds
    beside_ref[...] = jnp.full(beside_ref.shape, rounds, jnp.int32)
    away = pair_col ^ (me >> 1)
    block = jnp.zeros_like(away)
    for k, b in enumerate(position_bits(size)):
        block = block + jnp.where((away & (b >> 1)) != 0, 1 << k, 0)
    mine = rank - turn * slots
    slot = jnp.where((mine >= 0) & (mine < slots), block * slots + mine, -1)
    pick = slot == lax.broadcasted_iota(jnp.int32, pick_ref.shape, 1)
    pick_ref[...] = pick.astype(F32).astype(BF16)


def plan(ids, slots, table_rows, axis, size, turn=None):
    count = sum(i.shape[1] for i in ids)
    first_turn = turn is None
    return pl.pallas_call(
        functools.partial(
            plan_kernel, axis=axis, size=size, slots=slots, table_rows=table_rows, first_turn=first_turn
        ),
        out_shape=(
            jax.ShapeDtypeStruct((count, size // 2 * slots), BF16),
            jax.ShapeDtypeStruct((1,), jnp.int32),
            jax.ShapeDtypeStruct((8, LANES), jnp.int32),
        ),
        in_specs=([] if first_turn else [SMEM]) + [VMEM] * len(ids),
        out_specs=(VMEM, SMEM, VMEM),
        compiler_params=params(16),
        name="plan",
    )(*([] if first_turn else [turn]), *ids)


def select_kernel(pick_ref, rows_ref, out_ref):
    out_ref[...] = jnp.dot(pick_ref[...], rows_ref[...], preferred_element_type=F32).astype(BF16)


def select(pick, pieces):
    rows = jnp.concatenate(pieces, axis=0)
    return pl.pallas_call(
        select_kernel,
        out_shape=jax.ShapeDtypeStruct((pick.shape[0], rows.shape[1]), BF16),
        in_specs=[VMEM, VMEM],
        out_specs=VMEM,
        compiler_params=params(12),
        name="select",
    )(pick, rows)


def three_parts(x):
    high = x.astype(BF16)
    rest = x - high.astype(F32)
    middle = rest.astype(BF16)
    return [high, middle, (rest - middle.astype(F32)).astype(BF16)]


def prepare_kernel(
    start_ref, times_hbm, time_bias_hbm, pos_bias_hbm, table_hbm, out_ref, table_ref,
    times_ref, time_bias_ref, pos_bias_ref, sems, *, axis, npos, history
):
    pairs = ((times_hbm, times_ref), (time_bias_hbm, time_bias_ref), (pos_bias_hbm, pos_bias_ref), (table_hbm, table_ref))
    copies = [pltpu.make_async_copy(a, b, sems.at[k]) for k, (a, b) in enumerate(pairs)]
    for c in copies:
        c.start()
    events = times_ref.shape[1]
    first = history - start_ref[0] - lax.axis_index(axis) * events
    distance = first - lax.broadcasted_iota(jnp.int32, (1, events), 1)
    bucket = jnp.zeros((1, events), jnp.int32)
    for k in range(1, npos):
        bucket = bucket + (distance >= (1 << k)).astype(jnp.int32)
    for c in copies[:3]:
        c.wait()
    columns = []
    for table_ref_, index in ((time_bias_ref, times_ref[...]), (pos_bias_ref, bucket)):
        table = jnp.concatenate(three_parts(table_ref_[...] * 0.5), axis=0)
        kinds = table.shape[1]
        hot = lax.broadcasted_iota(jnp.int32, (kinds, events), 0) == index
        columns.append(jnp.dot(table, hot.astype(F32).astype(BF16), preferred_element_type=F32))
    used = sum(c.shape[0] for c in columns)
    columns.append(jnp.zeros((LANES - used, events), F32))
    out_ref[...] = jnp.concatenate(columns, axis=0).T.astype(BF16)
    copies[3].wait()


def prepare(start, times, time_bias, pos_bias, table, axis, history):
    arrays = [times, time_bias, pos_bias, table]
    return pl.pallas_call(
        functools.partial(prepare_kernel, axis=axis, npos=pos_bias.shape[1], history=history),
        out_shape=(
            jax.ShapeDtypeStruct((times.shape[1], LANES), BF16),
            jax.ShapeDtypeStruct(table.shape, BF16),
        ),
        in_specs=[SMEM] + [HBM] * 4,
        out_specs=(VMEM, VMEM),
        scratch_shapes=[pltpu.VMEM(a.shape, a.dtype) for a in arrays[:3]] + [pltpu.SemaphoreType.DMA((4,))],
        compiler_params=params(8),
        name="prepare",
    )(start, *(pltpu.with_memory_space_constraint(a, pltpu.HBM) for a in arrays))


def silu(x):
    return x / (1.0 + jnp.exp(-x))


def normalise(embedded, gain):
    x = embedded.astype(F32)
    meansq = jnp.mean(x * x, axis=-1, keepdims=True)
    return (x * lax.rsqrt(meansq + 1e-06) * gain).astype(BF16)


def attend_groups(query_ref, caches, groups, heads, keep_ref, send_ref):
    keys, values, biases = caches
    count = query_ref.shape[0]
    width = keys[0].shape[1]
    head_dim = width // heads
    per = LANES // head_dim
    half = count // 2
    rows = min(ROWS_AT_ONCE, count)
    events = keys[0].shape[0]
    step = min(EVENTS_AT_ONCE, events)
    base = groups[0]
    for first in range(0, count, rows):
        lane = lax.broadcasted_iota(jnp.int32, (rows, LANES), 1)
        stacks = {}

        def stack(group):
            if group not in stacks:
                at = (group - base) * LANES
                part = query_ref[first : first + rows, at : at + LANES]
                zero, one = jnp.zeros_like(part), jnp.ones_like(part)
                blocks = []
                for k in range(per):
                    own = jnp.where(lane // head_dim == k, part, zero)
                    chosen = jnp.where(lane % heads == group * per + k, one, zero)
                    blocks.append(jnp.concatenate([own, chosen], axis=1))
                stacks[group] = jnp.concatenate(blocks, axis=0)
            return stacks[group]

        def halves(group, block, j):
            at = slice(group * LANES, (group + 1) * LANES)
            left = jnp.concatenate([keys[block][j : j + step, at], biases[block][j : j + step, :]], axis=1)
            return lax.dot_general(left, stack(group), NT, preferred_element_type=F32)

        steps = [
            (group, block, j) for group in groups for block in range(len(keys)) for j in range(0, events, step)
        ]
        ahead = [halves(*s) for s in steps[:STEPS_AHEAD]]
        total = None
        for n, (group, block, j) in enumerate(steps):
            if n + STEPS_AHEAD < len(steps):
                ahead.append(halves(*steps[n + STEPS_AHEAD]))
            t = ahead.pop(0)
            weights = (t + t * jnp.tanh(t)).astype(BF16)
            at = slice(group * LANES, (group + 1) * LANES)
            term = lax.dot_general(values[block][j : j + step, at], weights, TN, preferred_element_type=F32)
            total = term if total is None else total + term
            if n + 1 < len(steps) and steps[n + 1][0] == group:
                continue
            out = jnp.concatenate(
                [total[k * head_dim : (k + 1) * head_dim, k * rows : (k + 1) * rows] for k in range(per)], axis=0
            ).T
            total = None
            at = slice((group - base) * LANES, (group - base + 1) * LANES)
            if first + rows <= half:
                keep_ref[first : first + rows, at] = out
            elif first >= half:
                send_ref[first - half : first - half + rows, at] = out.astype(BF16)
            else:
                keep_ref[first:half, at] = out[: half - first]
                send_ref[: first + rows - half, at] = out[half - first :].astype(BF16)


def attend_first_kernel(rounds_ref, pick_ref, *refs, heads, blocks, split):
    *row_refs, extra_hbm, gain_ref, proj_ref = refs[: -6 - 3 * blocks]
    caches = refs[-6 - 3 * blocks : -6]
    own_ref, keep_ref, send_ref, emb_ref, query_ref, sem = refs[-6:]
    count, width = emb_ref.shape
    rows = jnp.concatenate([r[...] for r in row_refs], axis=0)
    emb_ref[...] = jnp.dot(pick_ref[...], rows, preferred_element_type=F32).astype(BF16)


    @pl.when(jnp.max(rounds_ref[...]) > 1)
    def _():
        extra = pltpu.make_async_copy(extra_hbm, query_ref, sem)
        extra.start()
        extra.wait()
        emb_ref[...] = emb_ref[...] + query_ref[...]

    own_ref[...] = emb_ref[: own_ref.shape[0], :]
    head_dim = width // heads
    rows = min(ROWS_AT_ONCE, count)
    for first in range(0, count, rows):
        normed = normalise(emb_ref[first : first + rows, :], gain_ref[...])
        projected = jnp.dot(normed, proj_ref[:, :width], preferred_element_type=F32)
        query = silu(projected).astype(BF16) * jnp.asarray(0.5 * head_dim**-0.5, BF16)
        query_ref[first : first + rows, :] = query
    parts = [caches[k * blocks : (k + 1) * blocks] for k in range(3)]
    attend_groups(query_ref, parts, range(split), heads, keep_ref, send_ref)


def attention_cost(count, columns, keys, head_dim):
    events = len(keys) * keys[0].shape[0]
    return pl.CostEstimate(
        flops=8 * count * columns * events,
        transcendentals=count * columns // head_dim * events,
        bytes_accessed=4 * columns * events,
    )


def attend_first(rounds, pick, pieces, extra, gain, proj, keys, values, biases, heads, each, split):
    count, width = extra.shape
    columns = split * LANES
    blocks = len(keys)
    return pl.pallas_call(
        functools.partial(attend_first_kernel, heads=heads, blocks=blocks, split=split),
        out_shape=(
            jax.ShapeDtypeStruct((each, width), BF16),
            jax.ShapeDtypeStruct((count // 2, columns), F32),
            jax.ShapeDtypeStruct((count // 2, columns), BF16),
        ),
        in_specs=[VMEM, VMEM] + [VMEM] * len(pieces) + [HBM] + [VMEM] * (2 + 3 * blocks),
        out_specs=(VMEM,) * 3,
        scratch_shapes=[
            pltpu.VMEM((count, width), BF16),
            pltpu.VMEM((count, width), BF16),
            pltpu.SemaphoreType.DMA,
        ],
        compiler_params=params(20),
        cost_estimate=attention_cost(count, columns, keys, width // heads),
        name="attend_first",
    )(rounds, pick, *pieces, extra, gain, proj, *keys, *values, *biases)


def combine_kernel(*refs, count):
    halves, (own_ref, *go_refs) = refs[:count], refs[count:]
    rows = own_ref.shape[0]
    for k, out_ref in enumerate([own_ref, *go_refs]):
        at = 0
        for keep_ref, came_ref in zip(halves[::2], halves[1::2]):
            to = at + keep_ref.shape[1]
            block = slice(k * rows, (k + 1) * rows)
            total = keep_ref[block, :] + came_ref[block, :].astype(F32)
            out_ref[:, at:to] = total.astype(out_ref.dtype)
            at = to


def combine(halves, blocks):
    rows = halves[0].shape[0] // blocks
    width = sum(h.shape[1] for h in halves[::2])
    return pl.pallas_call(
        functools.partial(combine_kernel, count=len(halves)),
        out_shape=tuple(jax.ShapeDtypeStruct((rows, width), BF16 if k else F32) for k in range(blocks)),
        in_specs=[VMEM] * len(halves),
        out_specs=(VMEM,) * blocks,
        compiler_params=params(12),
        name="combine",
    )(*halves)


def stage_kernel(*refs, width):
    *refs, sems = refs
    count = len(refs) // 2
    copies = [
        pltpu.make_async_copy(
            a if a.shape[1] == width else a.at[:, pl.ds(0, width)], b, sems.at[k]
        )
        for k, (a, b) in enumerate(zip(refs[:count], refs[count:]))
    ]
    for c in copies:
        c.start()
    for c in copies:
        c.wait()


def stage(width, *arrays, held=True):
    return pl.pallas_call(
        functools.partial(stage_kernel, width=width),
        out_shape=tuple(jax.ShapeDtypeStruct((a.shape[0], width), BF16) for a in arrays),
        in_specs=[HBM if held else pl.BlockSpec(memory_space=pl.ANY)] * len(arrays),
        out_specs=(VMEM,) * len(arrays),
        scratch_shapes=[pltpu.SemaphoreType.DMA((len(arrays),))],
        compiler_params=params(4),
        name="stage",
    )(*(pltpu.with_memory_space_constraint(a, pltpu.HBM) if held else a for a in arrays))


def gates_kernel(emb_ref, gain_ref, proj_ref, out_ref):
    normed = normalise(emb_ref[...], gain_ref[...])
    projected = jnp.dot(normed, proj_ref[...], preferred_element_type=F32)
    out_ref[...] = silu(projected).astype(BF16)


def gates_of(embedded, gain, proj_in):
    return pl.pallas_call(
        gates_kernel,
        out_shape=jax.ShapeDtypeStruct(embedded.shape, BF16),
        grid=(1,),
        in_specs=[VMEM, VMEM, pl.BlockSpec(proj_in.shape[:1] * 2, lambda i: (0, 1))],
        out_specs=VMEM,
        compiler_params=params(16),
        cost_estimate=pl.CostEstimate(flops=1 << 26, transcendentals=1 << 14, bytes_accessed=1 << 22),
        name="gates",
    )(embedded, gain, proj_in)


def finish_kernel(own_ref, *refs):
    *parts, emb_ref, gates_ref, gain_ref, proj_ref, out_ref = refs
    attended = own_ref[...]
    for p in parts:
        attended = attended + p[...].astype(F32)
    centred = attended - jnp.mean(attended, axis=-1, keepdims=True)
    variance = jnp.mean(centred * centred, axis=-1, keepdims=True)
    gated = centred * lax.rsqrt(variance + 1e-05) * gain_ref[...] * gates_ref[...].astype(F32)
    product = jnp.dot(gated.astype(BF16), proj_ref[...], preferred_element_type=F32)
    out_ref[...] = (emb_ref[...].astype(F32) + product).astype(BF16)


def finish(own, parts, embedded, gates, gain, proj_out):
    return pl.pallas_call(
        finish_kernel,
        out_shape=jax.ShapeDtypeStruct(embedded.shape, BF16),
        in_specs=[VMEM] * (len(parts) + 5),
        out_specs=VMEM,
        compiler_params=params(16),
        name="finish",
    )(own, *parts, embedded, gates, gain, proj_out)


def on_device(
    item_ids,
    item_table,
    key_cache,
    value_cache,
    time_buckets,
    window_start,
    norm_gain,
    proj_in,
    time_bias,
    pos_bias,
    out_gain,
    proj_out,
):
    axis = "hist"
    size = lax.axis_size(axis)
    each = item_ids.shape[0]
    slots = 2 * each
    heads = time_bias.shape[0]
    events, width = key_cache.shape
    table_rows = item_table.shape[0]
    gain = norm_gain[None, :]

    def partners(x):
        return swap(x, PARTNER, axis, size)

    other_table = partners(item_table)
    other_keys = partners(key_cache)
    other_values = partners(value_cache)
    bias, own_table = prepare(
        window_start, time_buckets[None, :], time_bias, pos_bias, item_table, axis, 2 * events * size
    )
    other_bias = partners(bias)
    ids = gather_relative(item_ids[None, :], 1, axis, size)

    (near_table,) = stage(width, other_table, held=False)
    found = lookup(ids, [own_table, near_table], slots, axis, size)
    pieces = gather_rows(found, axis, size)
    pick, rounds, told = plan(ids, slots, table_rows, axis, size)

    def more(state):
        turn, so_far = state
        picked, *_ = plan(ids, slots, table_rows, axis, size, turn[None])
        found = lookup(ids, [item_table, other_table], slots, axis, size, turn[None])
        return turn + 1, so_far + select(picked, gather_rows(found, axis, size))

    none = jnp.zeros((each * (size // 2), width), BF16)
    _, extra = lax.while_loop(lambda s: s[0] < rounds[0], more, (jnp.int32(1), none))

    proj, keys, values, other_keys, other_values = stage(
        width, proj_in, key_cache, value_cache, other_keys, other_values
    )
    caches = ([keys, other_keys], [values, other_values], [bias, other_bias])
    *far, near = stage_masks(size)
    own, keep, send = attend_first(told, pick, pieces, extra, gain, proj, *caches, heads, each, width // LANES)
    halves = [keep, swap(send, near[0], axis, size)]
    gates = gates_of(own, gain, proj_in)

    total, *going = combine(halves, len(combos(far[-1])))
    for bits in far[::-1]:
        parts = [swap(g, m, axis, size) for g, m in zip(going, combos(bits)[1:])]
        if bits is far[0]:
            break
        total, *going = combine([total, sum(p.astype(F32) for p in parts)], len(combos(bits)))
    return finish(total, parts, own, gates, out_gain[None, :], proj_out)


def solution(mesh):
    placed = (
        P(("grp", "hist")),
        P("hist", None),
        P(("grp", "hist"), None),
        P(("grp", "hist"), None),
        P(("grp", "hist")),
        P("grp"),
        P(),
        P(),
        P(),
        P(),
        P(),
        P(),
    )

    return jax.shard_map(on_device, mesh=mesh, in_specs=placed, out_specs=P(("grp", "hist"), None), check_vma=False)
```

```python
import functools

import jax
import jax.numpy as jnp
from jax import lax
from jax.experimental import pallas as pl
from jax.experimental.pallas import tpu as pltpu
from jax.sharding import PartitionSpec as P


BF16 = jnp.bfloat16
F32 = jnp.float32
LANES = 128
ROWS_AT_ONCE = 128
EVENTS_AT_ONCE = 512
STEPS_AHEAD = 3
BLOCK = 16
TN = (((0,), (0,)), ((), ()))
NT = (((1,), (1,)), ((), ()))
VMEM = pl.BlockSpec(memory_space=pltpu.VMEM)
SMEM = pl.BlockSpec(memory_space=pltpu.SMEM)
HBM = pl.BlockSpec(memory_space=pltpu.HBM)


def params(mib):
    return pltpu.CompilerParams(vmem_limit_bytes=mib << 20)


PARTNER = 1


def stage_masks(size):
    bits = [1 << k for k in range(1, size.bit_length() - 1)][::-1]
    far = bits[:-1]
    return [sorted(far[k : k + 2]) for k in range(0, len(far), 2)] + [bits[-1:]]


def combos(bits):
    out = [0]
    for b in bits:
        out = out + [m | b for m in out]
    return out


def swap(x, mask, axis, size):
    return lax.ppermute(x, axis, [(i, i ^ mask) for i in range(size)])


def join_kernel(*refs):
    *parts, out_ref = refs
    rows = parts[0].shape[0]
    for k, p in enumerate(parts):
        out_ref[k * rows : (k + 1) * rows, :] = p[...]


def join(pieces, dim):
    if dim:
        return jnp.concatenate(pieces, axis=dim)
    rows, width = pieces[0].shape
    return pl.pallas_call(
        join_kernel,
        out_shape=jax.ShapeDtypeStruct((len(pieces) * rows, width), BF16),
        in_specs=[VMEM] * len(pieces),
        out_specs=VMEM,
        compiler_params=params(16),
        name="join",
    )(*pieces)


def gather_relative(x, dim, axis, size):
    *far, near = stage_masks(size)
    for bits in far:
        x = join([x] + [swap(x, m, axis, size) for m in combos(bits)[1:]], dim)
    return [x, swap(x, near[0], axis, size)]


def gather_rows(x, axis, size):
    *far, near = stage_masks(size)
    for bits in far[:-1]:
        x = join([x] + [swap(x, m, axis, size) for m in combos(bits)[1:]], 0)
    first, *rest = combos(far[-1])[1:]
    early = swap(x, near[0], axis, size)
    beside = swap(x, first, axis, size)
    others = join([swap(x, m, axis, size) for m in rest], 0)
    late = swap(others, near[0], axis, size)
    across = swap(early, first, axis, size)
    return [x, beside, others, early, across, late]


def position_bits(size):
    return [b for stage in stage_masks(size) for b in stage]


def candidates_info(ids_refs, me, size, table_rows):
    ids = jnp.concatenate([r[...] for r in ids_refs], axis=1)
    count = ids.shape[1]
    each = count // (size // 2)
    owner = ids // table_rows
    place = lax.broadcasted_iota(jnp.int32, (1, count), 1)
    block = place // each
    mask = jnp.zeros_like(place)
    for k, b in enumerate(position_bits(size)):
        mask = mask + ((block >> k) & 1) * b
    pair = owner >> 1
    key = pair * count + ((mask ^ me) >> 1) * each + place % each
    return pair, key, ids - owner * table_rows + ((owner ^ me) & 1) * table_rows


def to_column(row):
    count = row.shape[1]
    r = lax.broadcasted_iota(jnp.int32, (count, count), 0)
    c = lax.broadcasted_iota(jnp.int32, (count, count), 1)
    return jnp.sum(jnp.where(r == c, row, 0), axis=1, keepdims=True)


def lookup_kernel(*refs, axis, size, first_turn):
    if first_turn:
        *ids_refs, own_ref, other_ref, out_ref, blocks_ref = refs
        turn, copies = 0, []
    else:
        turn_ref, *ids_refs, own_hbm, other_hbm, out_ref, blocks_ref, own_ref, other_ref, sems = refs
        turn = turn_ref[0]
        copies = [
            pltpu.make_async_copy(own_hbm, own_ref, sems.at[0]),
            pltpu.make_async_copy(other_hbm, other_ref, sems.at[1]),
        ]
    for c in copies:
        c.start()
    me = lax.axis_index(axis)
    slots = out_ref.shape[0]
    rows = own_ref.shape[0]
    pair, key, offset = candidates_info(ids_refs, me, size, rows)
    count = pair.shape[1]
    key_col = to_column(key)
    before = (key_col < key) & (key_col >= pair * count)
    rank = jnp.sum(before.astype(jnp.int32), axis=0, keepdims=True)
    slot = lax.broadcasted_iota(jnp.int32, (slots, count), 0) + turn * slots
    hit = (pair == (me >> 1)) & (rank == slot)
    want = jnp.sum(jnp.where(hit, offset + 1, 0), axis=1, keepdims=True) - 1
    for c in copies:
        c.wait()
    near = jnp.where(want < 0, 0, want // BLOCK)
    for k in range(slots):
        block = near[k, 0]
        in_own = block < rows // BLOCK
        at = pl.multiple_of((block - jnp.where(in_own, 0, rows // BLOCK)) * BLOCK, BLOCK)
        own, other = own_ref[pl.ds(at, BLOCK), :], other_ref[pl.ds(at, BLOCK), :]
        blocks_ref[k * BLOCK : (k + 1) * BLOCK, :] = jnp.where(in_own, own, other)
    column = lax.broadcasted_iota(jnp.int32, (slots, slots * BLOCK), 1)
    line = lax.broadcasted_iota(jnp.int32, (slots, slots * BLOCK), 0)
    pick = (want >= 0) & (column == line * BLOCK + (want - near * BLOCK))
    found = jnp.dot(pick.astype(F32).astype(BF16), blocks_ref[...], preferred_element_type=F32)
    out_ref[...] = found.astype(BF16)


def lookup(ids, tables, slots, axis, size, turn=None):
    first_turn = turn is None
    if not first_turn:
        tables = [pltpu.with_memory_space_constraint(t, pltpu.HBM) for t in tables]
    rows, width = tables[0].shape
    return pl.pallas_call(
        functools.partial(lookup_kernel, axis=axis, size=size, first_turn=first_turn),
        out_shape=jax.ShapeDtypeStruct((slots, width), BF16),
        in_specs=([] if first_turn else [SMEM]) + [VMEM] * len(ids) + [VMEM if first_turn else HBM] * 2,
        out_specs=VMEM,
        scratch_shapes=[pltpu.VMEM((slots * BLOCK, width), BF16)]
        + ([] if first_turn else [pltpu.VMEM((rows, width), BF16)] * 2 + [pltpu.SemaphoreType.DMA((2,))]),
        compiler_params=params(16),
        name="lookup",
    )(*([] if first_turn else [turn]), *ids, *tables)


def plan_kernel(*refs, axis, size, slots, table_rows, first_turn):
    if first_turn:
        *ids_refs, pick_ref, rounds_ref, beside_ref = refs
        turn = 0
    else:
        turn_ref, *ids_refs, pick_ref, rounds_ref, beside_ref = refs
        turn = turn_ref[0]
    me = lax.axis_index(axis)
    pair, key, _ = candidates_info(ids_refs, me, size, table_rows)
    count = pair.shape[1]
    key_col = to_column(key)
    pair_col = key_col // count
    before = (key < key_col) & (key >= pair_col * count)
    rank = jnp.sum(before.astype(jnp.int32), axis=1, keepdims=True)
    rounds = jnp.max(rank) // slots + 1
    rounds_ref[0] = rounds
    beside_ref[...] = jnp.full(beside_ref.shape, rounds, jnp.int32)
    away = pair_col ^ (me >> 1)
    block = jnp.zeros_like(away)
    for k, b in enumerate(position_bits(size)):
        block = block + jnp.where((away & (b >> 1)) != 0, 1 << k, 0)
    mine = rank - turn * slots
    slot = jnp.where((mine >= 0) & (mine < slots), block * slots + mine, -1)
    pick = slot == lax.broadcasted_iota(jnp.int32, pick_ref.shape, 1)
    pick_ref[...] = pick.astype(F32).astype(BF16)


def plan(ids, slots, table_rows, axis, size, turn=None):
    count = sum(i.shape[1] for i in ids)
    first_turn = turn is None
    return pl.pallas_call(
        functools.partial(
            plan_kernel, axis=axis, size=size, slots=slots, table_rows=table_rows, first_turn=first_turn
        ),
        out_shape=(
            jax.ShapeDtypeStruct((count, size // 2 * slots), BF16),
            jax.ShapeDtypeStruct((1,), jnp.int32),
            jax.ShapeDtypeStruct((8, LANES), jnp.int32),
        ),
        in_specs=([] if first_turn else [SMEM]) + [VMEM] * len(ids),
        out_specs=(VMEM, SMEM, VMEM),
        compiler_params=params(16),
        name="plan",
    )(*([] if first_turn else [turn]), *ids)


def select_kernel(pick_ref, rows_ref, out_ref):
    out_ref[...] = jnp.dot(pick_ref[...], rows_ref[...], preferred_element_type=F32).astype(BF16)


def select(pick, pieces):
    rows = jnp.concatenate(pieces, axis=0)
    return pl.pallas_call(
        select_kernel,
        out_shape=jax.ShapeDtypeStruct((pick.shape[0], rows.shape[1]), BF16),
        in_specs=[VMEM, VMEM],
        out_specs=VMEM,
        compiler_params=params(12),
        name="select",
    )(pick, rows)


def three_parts(x):
    high = x.astype(BF16)
    rest = x - high.astype(F32)
    middle = rest.astype(BF16)
    return [high, middle, (rest - middle.astype(F32)).astype(BF16)]


def prepare_kernel(
    start_ref, times_hbm, time_bias_hbm, pos_bias_hbm, table_hbm, out_ref, table_ref,
    times_ref, time_bias_ref, pos_bias_ref, sems, *, axis, npos, history
):
    pairs = ((times_hbm, times_ref), (time_bias_hbm, time_bias_ref), (pos_bias_hbm, pos_bias_ref), (table_hbm, table_ref))
    copies = [pltpu.make_async_copy(a, b, sems.at[k]) for k, (a, b) in enumerate(pairs)]
    for c in copies:
        c.start()
    events = times_ref.shape[1]
    first = history - start_ref[0] - lax.axis_index(axis) * events
    distance = first - lax.broadcasted_iota(jnp.int32, (1, events), 1)
    bucket = jnp.zeros((1, events), jnp.int32)
    for k in range(1, npos):
        bucket = bucket + (distance >= (1 << k)).astype(jnp.int32)
    for c in copies[:3]:
        c.wait()
    columns = []
    for table_ref_, index in ((time_bias_ref, times_ref[...]), (pos_bias_ref, bucket)):
        table = jnp.concatenate(three_parts(table_ref_[...] * 0.5), axis=0)
        kinds = table.shape[1]
        hot = lax.broadcasted_iota(jnp.int32, (kinds, events), 0) == index
        columns.append(jnp.dot(table, hot.astype(F32).astype(BF16), preferred_element_type=F32))
    used = sum(c.shape[0] for c in columns)
    columns.append(jnp.zeros((LANES - used, events), F32))
    out_ref[...] = jnp.concatenate(columns, axis=0).T.astype(BF16)
    copies[3].wait()


def prepare(start, times, time_bias, pos_bias, table, axis, history):
    arrays = [times, time_bias, pos_bias, table]
    return pl.pallas_call(
        functools.partial(prepare_kernel, axis=axis, npos=pos_bias.shape[1], history=history),
        out_shape=(
            jax.ShapeDtypeStruct((times.shape[1], LANES), BF16),
            jax.ShapeDtypeStruct(table.shape, BF16),
        ),
        in_specs=[SMEM] + [HBM] * 4,
        out_specs=(VMEM, VMEM),
        scratch_shapes=[pltpu.VMEM(a.shape, a.dtype) for a in arrays[:3]] + [pltpu.SemaphoreType.DMA((4,))],
        compiler_params=params(8),
        name="prepare",
    )(start, *(pltpu.with_memory_space_constraint(a, pltpu.HBM) for a in arrays))


def silu(x):
    return x / (1.0 + jnp.exp(-x))


def normalise(embedded, gain):
    x = embedded.astype(F32)
    meansq = jnp.mean(x * x, axis=-1, keepdims=True)
    return (x * lax.rsqrt(meansq + 1e-06) * gain).astype(BF16)


def attend_groups(query_ref, caches, groups, heads, keep_ref, send_ref):
    keys, values, biases = caches
    count = query_ref.shape[0]
    width = keys[0].shape[1]
    head_dim = width // heads
    per = LANES // head_dim
    half = count // 2
    rows = min(ROWS_AT_ONCE, count)
    events = keys[0].shape[0]
    step = min(EVENTS_AT_ONCE, events)
    base = groups[0]
    for first in range(0, count, rows):
        lane = lax.broadcasted_iota(jnp.int32, (rows, LANES), 1)
        stacks = {}

        def stack(group):
            if group not in stacks:
                at = (group - base) * LANES
                part = query_ref[first : first + rows, at : at + LANES]
                zero, one = jnp.zeros_like(part), jnp.ones_like(part)
                blocks = []
                for k in range(per):
                    own = jnp.where(lane // head_dim == k, part, zero)
                    chosen = jnp.where(lane % heads == group * per + k, one, zero)
                    blocks.append(jnp.concatenate([own, chosen], axis=1))
                stacks[group] = jnp.concatenate(blocks, axis=0)
            return stacks[group]

        def halves(group, block, j):
            at = slice(group * LANES, (group + 1) * LANES)
            left = jnp.concatenate([keys[block][j : j + step, at], biases[block][j : j + step, :]], axis=1)
            return lax.dot_general(left, stack(group), NT, preferred_element_type=F32)

        steps = [
            (group, block, j) for group in groups for block in range(len(keys)) for j in range(0, events, step)
        ]
        ahead = [halves(*s) for s in steps[:STEPS_AHEAD]]
        total = None
        for n, (group, block, j) in enumerate(steps):
            if n + STEPS_AHEAD < len(steps):
                ahead.append(halves(*steps[n + STEPS_AHEAD]))
            t = ahead.pop(0)
            weights = (t + t * jnp.tanh(t)).astype(BF16)
            at = slice(group * LANES, (group + 1) * LANES)
            term = lax.dot_general(values[block][j : j + step, at], weights, TN, preferred_element_type=F32)
            total = term if total is None else total + term
            if n + 1 < len(steps) and steps[n + 1][0] == group:
                continue
            out = jnp.concatenate(
                [total[k * head_dim : (k + 1) * head_dim, k * rows : (k + 1) * rows] for k in range(per)], axis=0
            ).T
            total = None
            at = slice((group - base) * LANES, (group - base + 1) * LANES)
            if first + rows <= half:
                keep_ref[first : first + rows, at] = out
            elif first >= half:
                send_ref[first - half : first - half + rows, at] = out.astype(BF16)
            else:
                keep_ref[first:half, at] = out[: half - first]
                send_ref[: first + rows - half, at] = out[half - first :].astype(BF16)


def attend_first_kernel(rounds_ref, pick_ref, *refs, heads, blocks, split):
    *row_refs, extra_hbm, gain_ref, proj_ref = refs[: -7 - 3 * blocks]
    caches = refs[-7 - 3 * blocks : -7]
    own_ref, keep_ref, send_ref, later_ref, emb_ref, query_ref, sem = refs[-7:]
    count, width = emb_ref.shape
    rows = jnp.concatenate([r[...] for r in row_refs], axis=0)
    emb_ref[...] = jnp.dot(pick_ref[...], rows, preferred_element_type=F32).astype(BF16)


    @pl.when(jnp.max(rounds_ref[...]) > 1)
    def _():
        extra = pltpu.make_async_copy(extra_hbm, query_ref, sem)
        extra.start()
        extra.wait()
        emb_ref[...] = emb_ref[...] + query_ref[...]

    own_ref[...] = emb_ref[: own_ref.shape[0], :]
    head_dim = width // heads
    rows = min(ROWS_AT_ONCE, count)
    for first in range(0, count, rows):
        normed = normalise(emb_ref[first : first + rows, :], gain_ref[...])
        projected = jnp.dot(normed, proj_ref[:, :width], preferred_element_type=F32)
        query = silu(projected).astype(BF16) * jnp.asarray(0.5 * head_dim**-0.5, BF16)
        query_ref[first : first + rows, :] = query
        later_ref[first : first + rows, :] = query[:, split * LANES :]
    parts = [caches[k * blocks : (k + 1) * blocks] for k in range(3)]
    attend_groups(query_ref, parts, range(split), heads, keep_ref, send_ref)


def attend_later_kernel(query_ref, *refs, heads, blocks, split):
    *caches, keep_ref, send_ref = refs
    parts = [caches[k * blocks : (k + 1) * blocks] for k in range(3)]
    attend_groups(query_ref, parts, range(split, parts[0][0].shape[1] // LANES), heads, keep_ref, send_ref)


def attention_cost(count, columns, keys, head_dim):
    events = len(keys) * keys[0].shape[0]
    return pl.CostEstimate(
        flops=8 * count * columns * events,
        transcendentals=count * columns // head_dim * events,
        bytes_accessed=4 * columns * events,
    )


def attend_first(rounds, pick, pieces, extra, gain, proj, keys, values, biases, heads, each, split):
    count, width = extra.shape
    columns = split * LANES
    blocks = len(keys)
    return pl.pallas_call(
        functools.partial(attend_first_kernel, heads=heads, blocks=blocks, split=split),
        out_shape=(
            jax.ShapeDtypeStruct((each, width), BF16),
            jax.ShapeDtypeStruct((count // 2, columns), F32),
            jax.ShapeDtypeStruct((count // 2, columns), BF16),
            jax.ShapeDtypeStruct((count, width - columns), BF16),
        ),
        in_specs=[VMEM, VMEM] + [VMEM] * len(pieces) + [HBM] + [VMEM] * (2 + 3 * blocks),
        out_specs=(VMEM,) * 4,
        scratch_shapes=[
            pltpu.VMEM((count, width), BF16),
            pltpu.VMEM((count, width), BF16),
            pltpu.SemaphoreType.DMA,
        ],
        compiler_params=params(20),
        cost_estimate=attention_cost(count, columns, keys, width // heads),
        name="attend_first",
    )(rounds, pick, *pieces, extra, gain, proj, *keys, *values, *biases)


def attend_later(queries, keys, values, biases, heads, split):
    count, columns = queries.shape
    blocks = len(keys)
    return pl.pallas_call(
        functools.partial(attend_later_kernel, heads=heads, blocks=blocks, split=split),
        out_shape=(
            jax.ShapeDtypeStruct((count // 2, columns), F32),
            jax.ShapeDtypeStruct((count // 2, columns), BF16),
        ),
        in_specs=[VMEM] * (1 + 3 * blocks),
        out_specs=(VMEM, VMEM),
        compiler_params=params(20),
        cost_estimate=attention_cost(count, columns, keys, keys[0].shape[1] // heads),
        name="attend_later",
    )(queries, *keys, *values, *biases)


def combine_kernel(*refs, count):
    halves, (own_ref, *go_refs) = refs[:count], refs[count:]
    rows = own_ref.shape[0]
    for k, out_ref in enumerate([own_ref, *go_refs]):
        at = 0
        for keep_ref, came_ref in zip(halves[::2], halves[1::2]):
            to = at + keep_ref.shape[1]
            block = slice(k * rows, (k + 1) * rows)
            total = keep_ref[block, :] + came_ref[block, :].astype(F32)
            out_ref[:, at:to] = total.astype(out_ref.dtype)
            at = to


def combine(halves, blocks):
    rows = halves[0].shape[0] // blocks
    width = sum(h.shape[1] for h in halves[::2])
    return pl.pallas_call(
        functools.partial(combine_kernel, count=len(halves)),
        out_shape=tuple(jax.ShapeDtypeStruct((rows, width), BF16 if k else F32) for k in range(blocks)),
        in_specs=[VMEM] * len(halves),
        out_specs=(VMEM,) * blocks,
        compiler_params=params(12),
        name="combine",
    )(*halves)


def stage_kernel(*refs, width):
    *refs, sems = refs
    count = len(refs) // 2
    copies = [
        pltpu.make_async_copy(
            a if a.shape[1] == width else a.at[:, pl.ds(0, width)], b, sems.at[k]
        )
        for k, (a, b) in enumerate(zip(refs[:count], refs[count:]))
    ]
    for c in copies:
        c.start()
    for c in copies:
        c.wait()


def stage(width, *arrays, held=True):
    return pl.pallas_call(
        functools.partial(stage_kernel, width=width),
        out_shape=tuple(jax.ShapeDtypeStruct((a.shape[0], width), BF16) for a in arrays),
        in_specs=[HBM if held else pl.BlockSpec(memory_space=pl.ANY)] * len(arrays),
        out_specs=(VMEM,) * len(arrays),
        scratch_shapes=[pltpu.SemaphoreType.DMA((len(arrays),))],
        compiler_params=params(4),
        name="stage",
    )(*(pltpu.with_memory_space_constraint(a, pltpu.HBM) if held else a for a in arrays))


def gates_kernel(emb_ref, gain_ref, proj_ref, out_ref):
    normed = normalise(emb_ref[...], gain_ref[...])
    projected = jnp.dot(normed, proj_ref[...], preferred_element_type=F32)
    out_ref[...] = silu(projected).astype(BF16)


def gates_of(embedded, gain, proj_in):
    return pl.pallas_call(
        gates_kernel,
        out_shape=jax.ShapeDtypeStruct(embedded.shape, BF16),
        grid=(1,),
        in_specs=[VMEM, VMEM, pl.BlockSpec(proj_in.shape[:1] * 2, lambda i: (0, 1))],
        out_specs=VMEM,
        compiler_params=params(16),
        cost_estimate=pl.CostEstimate(flops=1 << 26, transcendentals=1 << 14, bytes_accessed=1 << 22),
        name="gates",
    )(embedded, gain, proj_in)


def finish_kernel(own_ref, *refs):
    *parts, emb_ref, gates_ref, gain_ref, proj_ref, out_ref = refs
    attended = own_ref[...]
    for p in parts:
        attended = attended + p[...].astype(F32)
    centred = attended - jnp.mean(attended, axis=-1, keepdims=True)
    variance = jnp.mean(centred * centred, axis=-1, keepdims=True)
    gated = centred * lax.rsqrt(variance + 1e-05) * gain_ref[...] * gates_ref[...].astype(F32)
    product = jnp.dot(gated.astype(BF16), proj_ref[...], preferred_element_type=F32)
    out_ref[...] = (emb_ref[...].astype(F32) + product).astype(BF16)


def finish(own, parts, embedded, gates, gain, proj_out):
    return pl.pallas_call(
        finish_kernel,
        out_shape=jax.ShapeDtypeStruct(embedded.shape, BF16),
        in_specs=[VMEM] * (len(parts) + 5),
        out_specs=VMEM,
        compiler_params=params(16),
        name="finish",
    )(own, *parts, embedded, gates, gain, proj_out)


def on_device(
    item_ids,
    item_table,
    key_cache,
    value_cache,
    time_buckets,
    window_start,
    norm_gain,
    proj_in,
    time_bias,
    pos_bias,
    out_gain,
    proj_out,
):
    axis = "hist"
    size = lax.axis_size(axis)
    each = item_ids.shape[0]
    slots = 2 * each
    heads = time_bias.shape[0]
    events, width = key_cache.shape
    table_rows = item_table.shape[0]
    gain = norm_gain[None, :]

    def partners(x):
        return swap(x, PARTNER, axis, size)

    other_table = partners(item_table)
    other_keys = partners(key_cache)
    other_values = partners(value_cache)
    bias, own_table = prepare(
        window_start, time_buckets[None, :], time_bias, pos_bias, item_table, axis, 2 * events * size
    )
    other_bias = partners(bias)
    ids = gather_relative(item_ids[None, :], 1, axis, size)

    (near_table,) = stage(width, other_table, held=False)
    found = lookup(ids, [own_table, near_table], slots, axis, size)
    pieces = gather_rows(found, axis, size)
    pick, rounds, told = plan(ids, slots, table_rows, axis, size)

    def more(state):
        turn, so_far = state
        picked, *_ = plan(ids, slots, table_rows, axis, size, turn[None])
        found = lookup(ids, [item_table, other_table], slots, axis, size, turn[None])
        return turn + 1, so_far + select(picked, gather_rows(found, axis, size))

    none = jnp.zeros((each * (size // 2), width), BF16)
    _, extra = lax.while_loop(lambda s: s[0] < rounds[0], more, (jnp.int32(1), none))

    proj, keys, values, other_keys, other_values = stage(
        width, proj_in, key_cache, value_cache, other_keys, other_values
    )
    caches = ([keys, other_keys], [values, other_values], [bias, other_bias])
    *far, near = stage_masks(size)
    split = max(1, width // LANES * 7 // 8)
    own, keep, send, later = attend_first(told, pick, pieces, extra, gain, proj, *caches, heads, each, split)
    halves = [keep, swap(send, near[0], axis, size)]
    keep, send = attend_later(later, *caches, heads, split)
    halves += [keep, swap(send, near[0], axis, size)]
    gates = gates_of(own, gain, proj_in)

    total, *going = combine(halves, len(combos(far[-1])))
    for bits in far[::-1]:
        parts = [swap(g, m, axis, size) for g, m in zip(going, combos(bits)[1:])]
        if bits is far[0]:
            break
        total, *going = combine([total, sum(p.astype(F32) for p in parts)], len(combos(bits)))
    return finish(total, parts, own, gates, out_gain[None, :], proj_out)


def solution(mesh):
    placed = (
        P(("grp", "hist")),
        P("hist", None),
        P(("grp", "hist"), None),
        P(("grp", "hist"), None),
        P(("grp", "hist")),
        P("grp"),
        P(),
        P(),
        P(),
        P(),
        P(),
        P(),
    )

    return jax.shard_map(on_device, mesh=mesh, in_specs=placed, out_specs=P(("grp", "hist"), None), check_vma=False)
```
